256 devices in a mesh: seq: 32 (over x, z), ch: 8 (over y, core).
Axes of the slice: x: 4, y: 4, z: 8, core: 2. Of those that a mesh axis runs over, the one named last changes fastest.
Arguments:
- out_gate: bfloat16 [12288, 4096], P('seq', 'ch'), may hold values from -6 to 6
- in_gate: bfloat16 [12288, 4096], P('seq', 'ch'), may hold values from -6 to 6
- values: bfloat16 [12288, 4096], P('seq', 'ch'), may hold values from -6 to 6
- short_filter: float32 [3, 3, 4096], P(None, None, 'ch'), may hold values from -3 to 3
- long_filter: float32 [12288, 4096], P('seq', 'ch'), may hold values from -1.5 to 1.5
- skip_gain: float32 [4096], P('ch'), may hold values from -4 to 4
- out_weight: bfloat16 [4096, 4096], P(None, 'ch'), may hold values from -0.09375 to 0.09375
Outputs:
- projected: bfloat16 [12288, 4096], P('seq', 'ch')
The draws below stay inside these ranges and needn't reach their ends.
All inputs are finite; a program needn't handle non-finite values.
Results may differ from the reference program's by a relative error of at most 0.0049.
Values may be sent and summed in bfloat16 or wider, within the bound.
A program may use at most 128 MiB of HBM per device.

```python
import math
import jax
import jax.numpy as jnp

D = 4096
TAPS = 3
SEQ_LEN = 12288


def draw_long_filter(key, part):
    rate_key, noise_key = jax.random.split(jax.random.fold_in(key, 11))
    times = jnp.arange(SEQ_LEN).astype(jnp.float32)[:, None]
    lower = math.log(1.0 / SEQ_LEN)
    upper = math.log(1.0 / 32.0)
    noise = jax.random.truncated_normal(noise_key, -4.0, 4.0, (SEQ_LEN, D), jnp.float32)
    rates = jnp.exp(jax.random.uniform(rate_key, (1, D), jnp.float32, lower, upper))
    scaling = jnp.sqrt(2.0 * rates / (1.0 - jnp.exp(-2.0 * rates * SEQ_LEN)))
    return noise * jnp.exp(-rates * times) * scaling


def block_scale(key, dims, cuts, least, top_value):
    def one(axis_at, blocks):
        draws = jax.random.uniform(jax.random.fold_in(jax.random.fold_in(key, 6), axis_at), (blocks,), jnp.float32, least / len(cuts), top_value / len(cuts))
        return jnp.repeat(jnp.exp(draws), dims[axis_at] // blocks).reshape((-1,) + (1,) * (len(dims) - axis_at - 1))

    factor_of = one(*cuts[0])
    for cut in cuts[1:]:
        factor_of = factor_of * one(*cut)
    return factor_of


def bell_draw(rng, extent, width, reach, cuts=(), kind=jnp.bfloat16):
    array = width * jax.random.normal(rng, extent, jnp.float32)
    if cuts:
        array = array * block_scale(rng, extent, cuts, -0.22, 0.18)
    return jnp.clip(array, -reach, reach).astype(kind)


def setup_inputs(seed: int = 0) -> dict:
    seeds = jax.random.split(jax.random.key(seed), 8)
    out_gate = bell_draw(seeds[0], (SEQ_LEN, D), 1.0, 6.0, ((0, 32), (1, 8)))
    in_gate = bell_draw(seeds[1], (SEQ_LEN, D), 1.0, 6.0, ((0, 32), (1, 8)))
    values = bell_draw(seeds[2], (SEQ_LEN, D), 1.0, 6.0, ((0, 32), (1, 8)))
    short_filter = bell_draw(seeds[3], (3, TAPS, D), 0.6, 3.0, ((2, 8),), jnp.float32)
    long_filter = draw_long_filter(jax.random.fold_in(seeds[7], 71), 0)
    skip_gain = bell_draw(seeds[5], (D,), 1.0, 4.0, ((0, 8),), jnp.float32)
    out_weight = bell_draw(seeds[6], (D, D), D ** -0.5, 0.09375, ((1, 8),))
    return dict(out_gate=out_gate, in_gate=in_gate, values=values, short_filter=short_filter, long_filter=long_filter, skip_gain=skip_gain, out_weight=out_weight)


def short_conv(signal, taps):
    widened = jnp.pad(signal.astype(jnp.float32), ((TAPS - 1, 0), (0, 0)))
    summed = taps[0] * widened[TAPS - 1:]
    for offset in range(1, TAPS):
        summed = summed + taps[offset] * widened[TAPS - 1 - offset:TAPS - 1 - offset + SEQ_LEN]
    return summed


def reference(out_gate, in_gate, values, short_filter, long_filter, skip_gain, out_weight):
    gate_late = short_conv(out_gate, short_filter[0])
    mixed_in = short_conv(in_gate, short_filter[1]) * short_conv(values, short_filter[2])
    padded_size = 2 * SEQ_LEN
    spectrum = jnp.fft.rfft(mixed_in, n=padded_size, axis=0) * jnp.fft.rfft(long_filter, n=padded_size, axis=0)
    long_out = jnp.fft.irfft(spectrum, n=padded_size, axis=0)[:SEQ_LEN].astype(jnp.float32)
    filtered = long_out + skip_gain * mixed_in
    mixed = (gate_late * filtered).astype(jnp.bfloat16)
    return jnp.dot(mixed, out_weight, preferred_element_type=jnp.float32).astype(jnp.bfloat16)
```

```python
import math

import jax
import jax.numpy as jnp
import numpy as np
from jax import lax
from jax.sharding import PartitionSpec as P

high = lax.Precision.HIGH


def contract(pattern, first_op, second_op):
    return jnp.einsum(
        pattern, first_op, second_op, precision=high, preferred_element_type=jnp.float32
    )


def tables(seq_len, inner):
    total = 2 * seq_len
    outer = total // inner
    half = seq_len // inner
    k1 = np.arange(outer)[:, None]
    n1 = np.arange(half)[None, :]
    a1 = 2.0 * np.pi * ((k1 * n1) % outer) / outer
    n2 = np.arange(inner)[None, :]
    at = 2.0 * np.pi * ((k1 * n2) % total) / total
    m2 = np.arange(inner)
    a2 = 2.0 * np.pi * ((m2[:, None] * m2[None, :]) % inner) / inner
    f32 = lambda v: jnp.asarray(v, jnp.float32)
    return dict(
        c1=f32(np.cos(a1)),
        s1=f32(np.sin(a1)),
        tc=f32(np.cos(at)[:, :, None]),
        ts=f32(np.sin(at)[:, :, None]),
        c2=f32(np.cos(a2)),
        s2=f32(np.sin(a2)),
        c1i=f32(np.cos(a1).T / total),
        s1i=f32(np.sin(a1).T / total),
    )


def forward(signal, tb):
    br = contract("kn,nmc->kmc", tb["c1"], signal)
    bi = -contract("kn,nmc->kmc", tb["s1"], signal)
    tr, ti = tb["tc"], -tb["ts"]
    br, bi = br * tr - bi * ti, br * ti + bi * tr
    xr = contract("kmc,mj->kjc", br, tb["c2"]) + contract("kmc,mj->kjc", bi, tb["s2"])
    xi = contract("kmc,mj->kjc", bi, tb["c2"]) - contract("kmc,mj->kjc", br, tb["s2"])
    return xr, xi


def inverse(yr, yi, tb):
    zr = contract("kjc,jm->kmc", yr, tb["c2"]) - contract("kjc,jm->kmc", yi, tb["s2"])
    zi = contract("kjc,jm->kmc", yr, tb["s2"]) + contract("kjc,jm->kmc", yi, tb["c2"])
    tc, ts = tb["tc"], tb["ts"]
    zr, zi = zr * tc - zi * ts, zr * ts + zi * tc
    return contract("nk,kmc->nmc", tb["c1i"], zr) - contract("nk,kmc->nmc", tb["s1i"], zi)


def long_conv(mixed_in, long_filter, inner):
    seq_len, width = mixed_in.shape
    half = seq_len // inner
    tb = tables(seq_len, inner)
    xr, xi = forward(mixed_in.reshape(half, inner, width), tb)
    hr, hi = forward(long_filter.reshape(half, inner, width), tb)
    yr = xr * hr - xi * hi
    yi = xr * hi + xi * hr
    return inverse(yr, yi, tb).reshape(seq_len, width)


def short_conv(signal, taps):
    tap_count = taps.shape[0]
    widened = jnp.pad(signal, ((tap_count - 1, 0), (0, 0)))
    seq_len = signal.shape[0]
    summed = taps[0] * widened[tap_count - 1 :]
    for offset in range(1, tap_count):
        start = tap_count - 1 - offset
        summed = summed + taps[offset] * widened[start : start + seq_len]
    return summed


def on_device(out_gate, in_gate, values, short_filter, long_filter, skip_gain, out_weight):
    seq_count = lax.axis_size("seq")
    seq_index = lax.axis_index("seq")
    width = out_gate.shape[1] // seq_count
    stacked = jnp.stack([out_gate, in_gate, values])
    spread = lax.all_to_all(stacked, "seq", split_axis=2, concat_axis=1, tiled=True)
    filt = lax.all_to_all(long_filter, "seq", split_axis=1, concat_axis=0, tiled=True)
    start = seq_index * width
    taps = lax.dynamic_slice_in_dim(short_filter, start, width, axis=2)
    gain = lax.dynamic_slice_in_dim(skip_gain, start, width, axis=0)
    spread = spread.astype(jnp.float32)
    gate_late = short_conv(spread[0], taps[0])
    mixed_in = short_conv(spread[1], taps[1]) * short_conv(spread[2], taps[2])
    long_out = long_conv(mixed_in, filt, 192)
    filtered = long_out + gain * mixed_in
    mixed = (gate_late * filtered).astype(jnp.bfloat16)
    mixed = lax.all_to_all(mixed, "seq", split_axis=0, concat_axis=1, tiled=True)
    summed = jnp.dot(
        lax.all_gather(mixed, "ch", axis=1, tiled=True),
        out_weight,
        preferred_element_type=jnp.float32,
    )
    return summed.astype(jnp.bfloat16)


def solution(mesh):
    return jax.shard_map(
        on_device,
        mesh=mesh,
        in_specs=(
            P("seq", "ch"),
            P("seq", "ch"),
            P("seq", "ch"),
            P(None, None, "ch"),
            P("seq", "ch"),
            P("ch"),
            P(None, "ch"),
        ),
        out_specs=P("seq", "ch"),
        check_vma=False,
    )
```

```python
import jax
import jax.numpy as jnp
import numpy as np
from jax import lax
from jax.sharding import PartitionSpec as P

high = lax.Precision.HIGH
LANES = 128


def contract(pattern, first_op, second_op):
    return jnp.einsum(
        pattern, first_op, second_op, precision=high, preferred_element_type=jnp.float32
    )


def tables(seq_len):
    total = 2 * seq_len
    outer = total // LANES
    half = seq_len // LANES
    k1 = np.arange(outer)[:, None]
    a1 = 2.0 * np.pi * ((k1 * np.arange(half)[None, :]) % outer) / outer
    at = 2.0 * np.pi * ((k1 * np.arange(LANES)[None, :]) % total) / total
    m2 = np.arange(LANES)
    a2 = 2.0 * np.pi * ((m2[:, None] * m2[None, :]) % LANES) / LANES
    c1, s1 = np.cos(a1), np.sin(a1)
    c2, s2 = np.cos(a2), np.sin(a2)
    f32 = lambda v: jnp.asarray(v, jnp.float32)
    return dict(
        first=f32(np.concatenate([c1, -s1], axis=0)),
        tc=f32(np.cos(at)[:, None, :]),
        ts=f32(np.sin(at)[:, None, :]),
        fwd2=f32(np.block([[c2, -s2], [s2, c2]])),
        inv2=f32(np.block([[c2, s2], [-s2, c2]])),
        last=f32(np.concatenate([c1.T, -s1.T], axis=1) / total),
    )


def forward(signal, tb):
    outer = tb["tc"].shape[0]
    both = contract("kn,ncm->kcm", tb["first"], signal)
    br, bi = both[:outer], both[outer:]
    tr, ti = tb["tc"], -tb["ts"]
    twisted = jnp.concatenate([br * tr - bi * ti, br * ti + bi * tr], axis=2)
    return contract("kcm,mj->kcj", twisted, tb["fwd2"])


def inverse(spectrum, tb):
    z = contract("kcj,jm->kcm", spectrum, tb["inv2"])
    zr, zi = z[:, :, :LANES], z[:, :, LANES:]
    tc, ts = tb["tc"], tb["ts"]
    stacked = jnp.concatenate([zr * tc - zi * ts, zr * ts + zi * tc], axis=0)
    return contract("nk,kcm->ncm", tb["last"], stacked)


def long_conv(mixed_in, long_filter):
    half = mixed_in.shape[0]
    tb = tables(half * LANES)
    xs = forward(mixed_in, tb)
    hs = forward(long_filter, tb)
    xr, xi = xs[:, :, :LANES], xs[:, :, LANES:]
    hr, hi = hs[:, :, :LANES], hs[:, :, LANES:]
    product = jnp.concatenate([xr * hr - xi * hi, xr * hi + xi * hr], axis=2)
    return inverse(product, tb)


def shift_seq(signal, distance):
    rows, width, lanes = signal.shape
    prev = jnp.concatenate([jnp.zeros((1, width, lanes), signal.dtype), signal[:-1]], axis=0)
    return jnp.concatenate(
        [prev[:, :, lanes - distance :], signal[:, :, : lanes - distance]], axis=2
    )


def short_conv(signal, taps):
    summed = taps[0][None, :, None] * signal
    for offset in range(1, taps.shape[0]):
        summed = summed + taps[offset][None, :, None] * shift_seq(signal, offset)
    return summed


def to_ncm(block):
    rows, width = block.shape
    return block.reshape(rows // LANES, LANES, width).transpose(0, 2, 1)


def on_device(out_gate, in_gate, values, short_filter, long_filter, skip_gain, out_weight):
    seq_count = lax.axis_size("seq")
    seq_index = lax.axis_index("seq")
    rows = out_gate.shape[0]
    width = out_gate.shape[1] // seq_count
    stacked = jnp.stack([to_ncm(out_gate), to_ncm(in_gate), to_ncm(values)])
    spread = lax.all_to_all(stacked, "seq", split_axis=2, concat_axis=1, tiled=True)
    filt = lax.all_to_all(to_ncm(long_filter), "seq", split_axis=1, concat_axis=0, tiled=True)
    start = seq_index * width
    taps = lax.dynamic_slice_in_dim(short_filter, start, width, axis=2)
    gain = lax.dynamic_slice_in_dim(skip_gain, start, width, axis=0)
    spread = spread.astype(jnp.float32)
    gate_late = short_conv(spread[0], taps[0])
    mixed_in = short_conv(spread[1], taps[1]) * short_conv(spread[2], taps[2])
    long_out = long_conv(mixed_in, filt)
    filtered = long_out + gain[None, :, None] * mixed_in
    mixed = (gate_late * filtered).astype(jnp.bfloat16)
    mixed = lax.all_to_all(mixed, "seq", split_axis=0, concat_axis=1, tiled=True)
    gathered = lax.all_gather(mixed, "ch", axis=1, tiled=True)
    summed = jnp.einsum(
        "ncm,co->nmo", gathered, out_weight, preferred_element_type=jnp.float32
    )
    return summed.reshape(rows, -1).astype(jnp.bfloat16)


def solution(mesh):
    return jax.shard_map(
        on_device,
        mesh=mesh,
        in_specs=(
            P("seq", "ch"),
            P("seq", "ch"),
            P("seq", "ch"),
            P(None, None, "ch"),
            P("seq", "ch"),
            P("ch"),
            P(None, "ch"),
        ),
        out_specs=P("seq", "ch"),
        check_vma=False,
    )
```

```python
import functools

import jax
import jax.numpy as jnp
import numpy as np
from jax import lax
from jax.experimental import pallas as pl
from jax.experimental.pallas import tpu as pltpu
from jax.sharding import PartitionSpec as P

high = lax.Precision.HIGH
LANES = 128
MESH = pl.DeviceIdType.MESH


def exchange_kernel(group, count, *refs):
    sources, targets = refs[:count], refs[count : 2 * count]
    send_sem, recv_sem, local_sem = refs[2 * count :]
    me = lax.axis_index("seq")
    ch = lax.axis_index("ch")
    barrier = pltpu.get_barrier_semaphore()
    for step in range(1, group):
        peer = lax.rem(me + step, group)
        pl.semaphore_signal(barrier, inc=1, device_id=(peer, ch), device_id_type=MESH)
    pl.semaphore_wait(barrier, group - 1)
    locals_ = []
    for a in range(count):
        cp = pltpu.make_async_copy(sources[a].at[me], targets[a].at[me], local_sem.at[a])
        cp.start()
        locals_.append(cp)
    sent = []
    for step in range(1, group):
        peer = lax.rem(me + step, group)
        for a in range(count):
            cp = pltpu.make_async_remote_copy(
                src_ref=sources[a].at[peer],
                dst_ref=targets[a].at[me],
                send_sem=send_sem.at[a, step],
                recv_sem=recv_sem.at[a, step],
                device_id=(peer, ch),
                device_id_type=MESH,
            )
            cp.start()
            sent.append(cp)
    for cp in locals_:
        cp.wait()
    for cp in sent:
        cp.wait_send()
    for step in range(1, group):
        origin = lax.rem(me + group - step, group)
        for a in range(count):
            pltpu.make_async_remote_copy(
                src_ref=sources[a].at[origin],
                dst_ref=targets[a].at[origin],
                send_sem=send_sem.at[a, step],
                recv_sem=recv_sem.at[a, step],
                device_id=(origin, ch),
                device_id_type=MESH,
            ).wait_recv()


def exchange(arrays, group, tag):
    count = len(arrays)
    return pl.pallas_call(
        functools.partial(exchange_kernel, group, count),
        out_shape=[jax.ShapeDtypeStruct(a.shape, a.dtype) for a in arrays],
        in_specs=[pl.BlockSpec(memory_space=pl.ANY)] * count,
        out_specs=[pl.BlockSpec(memory_space=pl.ANY)] * count,
        scratch_shapes=[
            pltpu.SemaphoreType.DMA((count, group)),
            pltpu.SemaphoreType.DMA((count, group)),
            pltpu.SemaphoreType.DMA((count,)),
        ],
        compiler_params=pltpu.CompilerParams(collective_id=tag, has_side_effects=True),
    )(*arrays)


def contract(pattern, first_op, second_op):
    return jnp.einsum(
        pattern, first_op, second_op, precision=high, preferred_element_type=jnp.float32
    )


def tables(seq_len):
    total = 2 * seq_len
    outer = total // LANES
    half = seq_len // LANES
    k1 = np.arange(outer)[:, None]
    a1 = 2.0 * np.pi * ((k1 * np.arange(half)[None, :]) % outer) / outer
    at = 2.0 * np.pi * ((k1 * np.arange(LANES)[None, :]) % total) / total
    m2 = np.arange(LANES)
    a2 = 2.0 * np.pi * ((m2[:, None] * m2[None, :]) % LANES) / LANES
    c1, s1 = np.cos(a1), np.sin(a1)
    c2, s2 = np.cos(a2), np.sin(a2)
    f32 = lambda v: jnp.asarray(v, jnp.float32)
    return dict(
        first=f32(np.concatenate([c1, -s1], axis=0)),
        tc=f32(np.cos(at)[:, None, :]),
        ts=f32(np.sin(at)[:, None, :]),
        fwd2=f32(np.block([[c2, -s2], [s2, c2]])),
        inv2=f32(np.block([[c2, s2], [-s2, c2]])),
        last=f32(np.concatenate([c1.T, -s1.T], axis=1) / total),
    )


def forward(signal, tb):
    outer = tb["tc"].shape[0]
    both = contract("kn,ncm->kcm", tb["first"], signal)
    br, bi = both[:outer], both[outer:]
    tr, ti = tb["tc"], -tb["ts"]
    twisted = jnp.concatenate([br * tr - bi * ti, br * ti + bi * tr], axis=2)
    return contract("kcm,mj->kcj", twisted, tb["fwd2"])


def inverse(spectrum, tb):
    z = contract("kcj,jm->kcm", spectrum, tb["inv2"])
    zr, zi = z[:, :, :LANES], z[:, :, LANES:]
    tc, ts = tb["tc"], tb["ts"]
    stacked = jnp.concatenate([zr * tc - zi * ts, zr * ts + zi * tc], axis=0)
    return contract("nk,kcm->ncm", tb["last"], stacked)


def long_conv(mixed_in, long_filter):
    half = mixed_in.shape[0]
    tb = tables(half * LANES)
    xs = forward(mixed_in, tb)
    hs = forward(long_filter, tb)
    xr, xi = xs[:, :, :LANES], xs[:, :, LANES:]
    hr, hi = hs[:, :, :LANES], hs[:, :, LANES:]
    product = jnp.concatenate([xr * hr - xi * hi, xr * hi + xi * hr], axis=2)
    return inverse(product, tb)


def shift_seq(signal, distance):
    rows, width, lanes = signal.shape
    prev = jnp.concatenate([jnp.zeros((1, width, lanes), signal.dtype), signal[:-1]], axis=0)
    return jnp.concatenate(
        [prev[:, :, lanes - distance :], signal[:, :, : lanes - distance]], axis=2
    )


def short_conv(signal, taps):
    summed = taps[0][None, :, None] * signal
    for offset in range(1, taps.shape[0]):
        summed = summed + taps[offset][None, :, None] * shift_seq(signal, offset)
    return summed


def to_ncm(block):
    rows, width = block.shape
    return block.reshape(rows // LANES, LANES, width).transpose(0, 2, 1)


def on_device(out_gate, in_gate, values, short_filter, long_filter, skip_gain, out_weight):
    seq_count = lax.axis_size("seq")
    seq_index = lax.axis_index("seq")
    rows = out_gate.shape[0]
    width = out_gate.shape[1] // seq_count
    half = rows // LANES

    def by_target(block):
        return to_ncm(block).reshape(half, seq_count, width, LANES).transpose(1, 0, 2, 3)

    stacked = jnp.stack([by_target(out_gate), by_target(in_gate), by_target(values)], axis=1)
    spread, filt = exchange([stacked, by_target(long_filter)], seq_count, 0)
    spread = spread.transpose(1, 0, 2, 3, 4).reshape(3, seq_count * half, width, LANES)
    filt = filt.reshape(seq_count * half, width, LANES)
    start = seq_index * width
    taps = lax.dynamic_slice_in_dim(short_filter, start, width, axis=2)
    gain = lax.dynamic_slice_in_dim(skip_gain, start, width, axis=0)
    spread = spread.astype(jnp.float32)
    gate_late = short_conv(spread[0], taps[0])
    mixed_in = short_conv(spread[1], taps[1]) * short_conv(spread[2], taps[2])
    long_out = long_conv(mixed_in, filt)
    filtered = long_out + gain[None, :, None] * mixed_in
    mixed = (gate_late * filtered).astype(jnp.bfloat16)
    (mixed,) = exchange([mixed.reshape(seq_count, half, width, LANES)], seq_count, 1)
    mixed = mixed.transpose(1, 0, 2, 3).reshape(half, seq_count * width, LANES)
    gathered = lax.all_gather(mixed, "ch", axis=1, tiled=True)
    summed = jnp.einsum(
        "ncm,co->nmo", gathered, out_weight, preferred_element_type=jnp.float32
    )
    return summed.reshape(rows, -1).astype(jnp.bfloat16)


def solution(mesh):
    return jax.shard_map(
        on_device,
        mesh=mesh,
        in_specs=(
            P("seq", "ch"),
            P("seq", "ch"),
            P("seq", "ch"),
            P(None, None, "ch"),
            P("seq", "ch"),
            P("ch"),
            P(None, "ch"),
        ),
        out_specs=P("seq", "ch"),
        check_vma=False,
    )
```

```python
import functools

import jax
import jax.numpy as jnp
import numpy as np
from jax import lax
from jax.experimental import pallas as pl
from jax.experimental.pallas import tpu as pltpu
from jax.sharding import PartitionSpec as P

high = lax.Precision.HIGH
LANES = 128
MESH = pl.DeviceIdType.MESH


def exchange_kernel(group, count, *refs):
    sources, targets = refs[:count], refs[count : 2 * count]
    send_sem, recv_sem, local_sem = refs[2 * count :]
    me = lax.axis_index("seq")
    ch = lax.axis_index("ch")
    barrier = pltpu.get_barrier_semaphore()
    for step in range(1, group):
        peer = lax.rem(me + step, group)
        pl.semaphore_signal(barrier, inc=1, device_id=(peer, ch), device_id_type=MESH)
    pl.semaphore_wait(barrier, group - 1)
    locals_ = []
    for a in range(count):
        cp = pltpu.make_async_copy(sources[a].at[me], targets[a].at[me], local_sem.at[a])
        cp.start()
        locals_.append(cp)
    sent = []
    for step in range(1, group):
        peer = lax.rem(me + step, group)
        for a in range(count):
            cp = pltpu.make_async_remote_copy(
                src_ref=sources[a].at[peer],
                dst_ref=targets[a].at[me],
                send_sem=send_sem.at[a, step],
                recv_sem=recv_sem.at[a, step],
                device_id=(peer, ch),
                device_id_type=MESH,
            )
            cp.start()
            sent.append(cp)
    for cp in locals_:
        cp.wait()
    for cp in sent:
        cp.wait_send()
    for step in range(1, group):
        origin = lax.rem(me + group - step, group)
        for a in range(count):
            pltpu.make_async_remote_copy(
                src_ref=sources[a].at[origin],
                dst_ref=targets[a].at[origin],
                send_sem=send_sem.at[a, step],
                recv_sem=recv_sem.at[a, step],
                device_id=(origin, ch),
                device_id_type=MESH,
            ).wait_recv()


def exchange(arrays, group, tag):
    count = len(arrays)
    return pl.pallas_call(
        functools.partial(exchange_kernel, group, count),
        out_shape=[jax.ShapeDtypeStruct(a.shape, a.dtype) for a in arrays],
        in_specs=[pl.BlockSpec(memory_space=pl.ANY)] * count,
        out_specs=[pl.BlockSpec(memory_space=pl.ANY)] * count,
        scratch_shapes=[
            pltpu.SemaphoreType.DMA((count, group)),
            pltpu.SemaphoreType.DMA((count, group)),
            pltpu.SemaphoreType.DMA((count,)),
        ],
        compiler_params=pltpu.CompilerParams(collective_id=tag, has_side_effects=True),
    )(*arrays)


def contract(pattern, first_op, second_op):
    return jnp.einsum(
        pattern, first_op, second_op, precision=high, preferred_element_type=jnp.float32
    )


def tables(seq_len):
    total = 2 * seq_len
    outer = total // LANES
    half = seq_len // LANES
    k1 = np.arange(outer)[:, None]
    a1 = 2.0 * np.pi * ((k1 * np.arange(half)[None, :]) % outer) / outer
    at = 2.0 * np.pi * ((k1 * np.arange(LANES)[None, :]) % total) / total
    m2 = np.arange(LANES)
    a2 = 2.0 * np.pi * ((m2[:, None] * m2[None, :]) % LANES) / LANES
    c1, s1 = np.cos(a1), np.sin(a1)
    c2, s2 = np.cos(a2), np.sin(a2)
    f32 = lambda v: jnp.asarray(v, jnp.float32)
    return dict(
        first=f32(np.concatenate([c1, -s1], axis=0)),
        tc=f32(np.cos(at)[:, None, :]),
        ts=f32(np.sin(at)[:, None, :]),
        fwd2=f32(np.block([[c2, -s2], [s2, c2]])),
        inv2=f32(np.block([[c2, s2], [-s2, c2]])),
        last=f32(np.concatenate([c1.T, -s1.T], axis=1) / total),
    )


def forward(signal, tb):
    outer = tb["tc"].shape[0]
    both = contract("kn,ncm->kcm", tb["first"], signal)
    br, bi = both[:outer], both[outer:]
    tr, ti = tb["tc"], -tb["ts"]
    twisted = jnp.concatenate([br * tr - bi * ti, br * ti + bi * tr], axis=2)
    return contract("kcm,mj->kcj", twisted, tb["fwd2"])


def inverse(spectrum, tb):
    z = contract("kcj,jm->kcm", spectrum, tb["inv2"])
    zr, zi = z[:, :, :LANES], z[:, :, LANES:]
    tc, ts = tb["tc"], tb["ts"]
    stacked = jnp.concatenate([zr * tc - zi * ts, zr * ts + zi * tc], axis=0)
    return contract("nk,kcm->ncm", tb["last"], stacked)


def long_conv(mixed_in, long_filter):
    half = mixed_in.shape[0]
    tb = tables(half * LANES)
    xs = forward(mixed_in, tb)
    hs = forward(long_filter, tb)
    xr, xi = xs[:, :, :LANES], xs[:, :, LANES:]
    hr, hi = hs[:, :, :LANES], hs[:, :, LANES:]
    product = jnp.concatenate([xr * hr - xi * hi, xr * hi + xi * hr], axis=2)
    return inverse(product, tb)


def shift_seq(signal, distance):
    rows, width, lanes = signal.shape
    prev = jnp.concatenate([jnp.zeros((1, width, lanes), signal.dtype), signal[:-1]], axis=0)
    return jnp.concatenate(
        [prev[:, :, lanes - distance :], signal[:, :, : lanes - distance]], axis=2
    )


def short_conv(signal, taps):
    summed = taps[0][None, :, None] * signal
    for offset in range(1, taps.shape[0]):
        summed = summed + taps[offset][None, :, None] * shift_seq(signal, offset)
    return summed


def to_ncm(block):
    rows, width = block.shape
    return block.reshape(rows // LANES, LANES, width).transpose(0, 2, 1)


def on_device(out_gate, in_gate, values, short_filter, long_filter, skip_gain, out_weight):
    seq_count = lax.axis_size("seq")
    seq_index = lax.axis_index("seq")
    rows = out_gate.shape[0]
    width = out_gate.shape[1] // seq_count
    half = rows // LANES

    def by_target(block):
        return to_ncm(block).reshape(half, seq_count, width, LANES).transpose(1, 0, 2, 3)

    planes = [out_gate, in_gate, values, long_filter.astype(jnp.bfloat16)]
    stacked = jnp.stack([by_target(plane) for plane in planes], axis=1)
    (spread,) = exchange([stacked], seq_count, 0)
    spread = spread.transpose(1, 0, 2, 3, 4).reshape(len(planes), seq_count * half, width, LANES)
    start = seq_index * width
    taps = lax.dynamic_slice_in_dim(short_filter, start, width, axis=2)
    gain = lax.dynamic_slice_in_dim(skip_gain, start, width, axis=0)
    spread = spread.astype(jnp.float32)
    gate_late = short_conv(spread[0], taps[0])
    mixed_in = short_conv(spread[1], taps[1]) * short_conv(spread[2], taps[2])
    long_out = long_conv(mixed_in, spread[3])
    filtered = long_out + gain[None, :, None] * mixed_in
    mixed = (gate_late * filtered).astype(jnp.bfloat16)
    (mixed,) = exchange([mixed.reshape(seq_count, half, width, LANES)], seq_count, 1)
    mixed = mixed.transpose(1, 0, 2, 3).reshape(half, seq_count * width, LANES)
    gathered = lax.all_gather(mixed, "ch", axis=1, tiled=True)
    summed = jnp.einsum(
        "ncm,co->nmo", gathered, out_weight, preferred_element_type=jnp.float32
    )
    return summed.reshape(rows, -1).astype(jnp.bfloat16)


def solution(mesh):
    return jax.shard_map(
        on_device,
        mesh=mesh,
        in_specs=(
            P("seq", "ch"),
            P("seq", "ch"),
            P("seq", "ch"),
            P(None, None, "ch"),
            P("seq", "ch"),
            P("ch"),
            P(None, "ch"),
        ),
        out_specs=P("seq", "ch"),
        check_vma=False,
    )
```

```python
import functools

import jax
import jax.numpy as jnp
import numpy as np
from jax import lax
from jax.experimental import pallas as pl
from jax.experimental.pallas import tpu as pltpu
from jax.sharding import PartitionSpec as P

high = lax.Precision.HIGH
LANES = 128
MESH = pl.DeviceIdType.MESH


def exchange_kernel(group, count, *refs):
    sources, targets = refs[:count], refs[count : 2 * count]
    send_sem, recv_sem, local_sem = refs[2 * count :]
    me = lax.axis_index("seq")
    ch = lax.axis_index("ch")
    barrier = pltpu.get_barrier_semaphore()
    for step in range(1, group):
        peer = lax.rem(me + step, group)
        pl.semaphore_signal(barrier, inc=1, device_id=(peer, ch), device_id_type=MESH)
    pl.semaphore_wait(barrier, group - 1)
    locals_ = []
    for a in range(count):
        cp = pltpu.make_async_copy(sources[a].at[me], targets[a].at[me], local_sem.at[a])
        cp.start()
        locals_.append(cp)
    sent = []
    for step in range(1, group):
        peer = lax.rem(me + step, group)
        for a in range(count):
            cp = pltpu.make_async_remote_copy(
                src_ref=sources[a].at[peer],
                dst_ref=targets[a].at[me],
                send_sem=send_sem.at[a, step],
                recv_sem=recv_sem.at[a, step],
                device_id=(peer, ch),
                device_id_type=MESH,
            )
            cp.start()
            sent.append(cp)
    for cp in locals_:
        cp.wait()
    for cp in sent:
        cp.wait_send()
    for step in range(1, group):
        origin = lax.rem(me + group - step, group)
        for a in range(count):
            pltpu.make_async_remote_copy(
                src_ref=sources[a].at[origin],
                dst_ref=targets[a].at[origin],
                send_sem=send_sem.at[a, step],
                recv_sem=recv_sem.at[a, step],
                device_id=(origin, ch),
                device_id_type=MESH,
            ).wait_recv()


def exchange(arrays, group, tag):
    count = len(arrays)
    return pl.pallas_call(
        functools.partial(exchange_kernel, group, count),
        out_shape=[jax.ShapeDtypeStruct(a.shape, a.dtype) for a in arrays],
        in_specs=[pl.BlockSpec(memory_space=pl.ANY)] * count,
        out_specs=[pl.BlockSpec(memory_space=pl.ANY)] * count,
        scratch_shapes=[
            pltpu.SemaphoreType.DMA((count, group)),
            pltpu.SemaphoreType.DMA((count, group)),
            pltpu.SemaphoreType.DMA((count,)),
        ],
        compiler_params=pltpu.CompilerParams(collective_id=tag, has_side_effects=True),
    )(*arrays)


def return_kernel(group, chans, source, target, send_sem, recv_sem, pass_sem, got_sem, fwd_sem, local_sem):
    me = lax.axis_index("seq")
    ch = lax.axis_index("ch")
    sibling = ch + 1 - 2 * lax.rem(ch, 2)
    across = [lax.rem(ch + 2 * hop, chans) for hop in range(1, chans // 2)]
    barrier = pltpu.get_barrier_semaphore()
    for step in range(1, group):
        peer = lax.rem(me + step, group)
        pl.semaphore_signal(barrier, inc=1, device_id=(peer, ch), device_id_type=MESH)
    for peer_ch in across + [sibling]:
        pl.semaphore_signal(barrier, inc=1, device_id=(me, peer_ch), device_id_type=MESH)
    pl.semaphore_wait(barrier, group - 1 + len(across) + 1)
    local = pltpu.make_async_copy(source.at[me], target.at[ch, me], local_sem.at[0])
    local.start()
    sent = []
    for step in range(1, group):
        peer = lax.rem(me + step, group)
        cp = pltpu.make_async_remote_copy(
            src_ref=source.at[peer],
            dst_ref=target.at[ch, me],
            send_sem=send_sem.at[step],
            recv_sem=recv_sem.at[step],
            device_id=(peer, ch),
            device_id_type=MESH,
        )
        cp.start()
        sent.append(cp)
    local.wait()
    for step in range(1, group):
        origin = lax.rem(me + group - step, group)
        pltpu.make_async_remote_copy(
            src_ref=source.at[origin],
            dst_ref=target.at[ch, origin],
            send_sem=send_sem.at[step],
            recv_sem=recv_sem.at[step],
            device_id=(origin, ch),
            device_id_type=MESH,
        ).wait_recv()
    passed = []
    for slot, peer_ch in enumerate(across + [sibling]):
        cp = pltpu.make_async_remote_copy(
            src_ref=target.at[ch],
            dst_ref=target.at[ch],
            send_sem=pass_sem.at[slot],
            recv_sem=got_sem.at[ch],
            device_id=(me, peer_ch),
            device_id_type=MESH,
        )
        cp.start()
        passed.append(cp)
    forwarded = []
    for hop in range(1, chans // 2):
        origin = lax.rem(ch + chans - 2 * hop, chans)
        pltpu.make_async_remote_copy(
            src_ref=target.at[origin],
            dst_ref=target.at[origin],
            send_sem=pass_sem.at[0],
            recv_sem=got_sem.at[origin],
            device_id=(me, origin),
            device_id_type=MESH,
        ).wait_recv()
        cp = pltpu.make_async_remote_copy(
            src_ref=target.at[origin],
            dst_ref=target.at[origin],
            send_sem=fwd_sem.at[hop],
            recv_sem=got_sem.at[origin],
            device_id=(me, sibling),
            device_id_type=MESH,
        )
        cp.start()
        forwarded.append(cp)
    for cp in sent + passed + forwarded:
        cp.wait_send()
    for hop in range(1, chans // 2):
        origin = lax.rem(sibling + chans - 2 * hop, chans)
        pltpu.make_async_remote_copy(
            src_ref=target.at[origin],
            dst_ref=target.at[origin],
            send_sem=pass_sem.at[0],
            recv_sem=got_sem.at[origin],
            device_id=(me, origin),
            device_id_type=MESH,
        ).wait_recv()
    pltpu.make_async_remote_copy(
        src_ref=target.at[sibling],
        dst_ref=target.at[sibling],
        send_sem=pass_sem.at[0],
        recv_sem=got_sem.at[sibling],
        device_id=(me, sibling),
        device_id_type=MESH,
    ).wait_recv()


def return_and_gather(block, group, chans, tag):
    return pl.pallas_call(
        functools.partial(return_kernel, group, chans),
        out_shape=jax.ShapeDtypeStruct((chans,) + block.shape, block.dtype),
        in_specs=[pl.BlockSpec(memory_space=pl.ANY)],
        out_specs=pl.BlockSpec(memory_space=pl.ANY),
        scratch_shapes=[
            pltpu.SemaphoreType.DMA((group,)),
            pltpu.SemaphoreType.DMA((group,)),
            pltpu.SemaphoreType.DMA((chans // 2,)),
            pltpu.SemaphoreType.DMA((chans,)),
            pltpu.SemaphoreType.DMA((chans // 2,)),
            pltpu.SemaphoreType.DMA((1,)),
        ],
        compiler_params=pltpu.CompilerParams(collective_id=tag, has_side_effects=True),
    )(block)


def contract(pattern, first_op, second_op):
    return jnp.einsum(
        pattern, first_op, second_op, precision=high, preferred_element_type=jnp.float32
    )


def tables(seq_len):
    total = 2 * seq_len
    outer = total // LANES
    half = seq_len // LANES
    k1 = np.arange(outer)[:, None]
    a1 = 2.0 * np.pi * ((k1 * np.arange(half)[None, :]) % outer) / outer
    at = 2.0 * np.pi * ((k1 * np.arange(LANES)[None, :]) % total) / total
    m2 = np.arange(LANES)
    a2 = 2.0 * np.pi * ((m2[:, None] * m2[None, :]) % LANES) / LANES
    c1, s1 = np.cos(a1), np.sin(a1)
    c2, s2 = np.cos(a2), np.sin(a2)
    f32 = lambda v: jnp.asarray(v, jnp.float32)
    return dict(
        first=f32(np.concatenate([c1, -s1], axis=0)),
        tc=f32(np.cos(at)[:, None, :]),
        ts=f32(np.sin(at)[:, None, :]),
        fwd2=f32(np.block([[c2, -s2], [s2, c2]])),
        inv2=f32(np.block([[c2, s2], [-s2, c2]])),
        last=f32(np.concatenate([c1.T, -s1.T], axis=1) / total),
    )


def forward(signal, tb):
    outer = tb["tc"].shape[0]
    both = contract("kn,ncm->kcm", tb["first"], signal)
    br, bi = both[:outer], both[outer:]
    tr, ti = tb["tc"], -tb["ts"]
    twisted = jnp.concatenate([br * tr - bi * ti, br * ti + bi * tr], axis=2)
    return contract("kcm,mj->kcj", twisted, tb["fwd2"])


def inverse(spectrum, tb):
    z = contract("kcj,jm->kcm", spectrum, tb["inv2"])
    zr, zi = z[:, :, :LANES], z[:, :, LANES:]
    tc, ts = tb["tc"], tb["ts"]
    stacked = jnp.concatenate([zr * tc - zi * ts, zr * ts + zi * tc], axis=0)
    return contract("nk,kcm->ncm", tb["last"], stacked)


def long_conv(mixed_in, long_filter):
    half = mixed_in.shape[0]
    tb = tables(half * LANES)
    xs = forward(mixed_in, tb)
    hs = forward(long_filter, tb)
    xr, xi = xs[:, :, :LANES], xs[:, :, LANES:]
    hr, hi = hs[:, :, :LANES], hs[:, :, LANES:]
    product = jnp.concatenate([xr * hr - xi * hi, xr * hi + xi * hr], axis=2)
    return inverse(product, tb)


def shift_seq(signal, distance):
    rows, width, lanes = signal.shape
    prev = jnp.concatenate([jnp.zeros((1, width, lanes), signal.dtype), signal[:-1]], axis=0)
    return jnp.concatenate(
        [prev[:, :, lanes - distance :], signal[:, :, : lanes - distance]], axis=2
    )


def short_conv(signal, taps):
    summed = taps[0][None, :, None] * signal
    for offset in range(1, taps.shape[0]):
        summed = summed + taps[offset][None, :, None] * shift_seq(signal, offset)
    return summed


def to_ncm(block):
    rows, width = block.shape
    return block.reshape(rows // LANES, LANES, width).transpose(0, 2, 1)


def on_device(out_gate, in_gate, values, short_filter, long_filter, skip_gain, out_weight):
    seq_count = lax.axis_size("seq")
    seq_index = lax.axis_index("seq")
    rows = out_gate.shape[0]
    width = out_gate.shape[1] // seq_count
    half = rows // LANES

    def by_target(block):
        return to_ncm(block).reshape(half, seq_count, width, LANES).transpose(1, 0, 2, 3)

    planes = [out_gate, in_gate, values, long_filter.astype(jnp.bfloat16)]
    stacked = jnp.stack([by_target(plane) for plane in planes], axis=1)
    (spread,) = exchange([stacked], seq_count, 0)
    spread = spread.transpose(1, 0, 2, 3, 4).reshape(len(planes), seq_count * half, width, LANES)
    start = seq_index * width
    taps = lax.dynamic_slice_in_dim(short_filter, start, width, axis=2)
    gain = lax.dynamic_slice_in_dim(skip_gain, start, width, axis=0)
    spread = spread.astype(jnp.float32)
    gate_late = short_conv(spread[0], taps[0])
    mixed_in = short_conv(spread[1], taps[1]) * short_conv(spread[2], taps[2])
    long_out = long_conv(mixed_in, spread[3])
    filtered = long_out + gain[None, :, None] * mixed_in
    mixed = (gate_late * filtered).astype(jnp.bfloat16)
    chans = lax.axis_size("ch")
    gathered = return_and_gather(mixed.reshape(seq_count, half, width, LANES), seq_count, chans, 1)
    gathered = gathered.transpose(2, 0, 1, 3, 4).reshape(half, chans * seq_count * width, LANES)
    summed = jnp.einsum(
        "ncm,co->nmo", gathered, out_weight, preferred_element_type=jnp.float32
    )
    return summed.reshape(rows, -1).astype(jnp.bfloat16)


def solution(mesh):
    return jax.shard_map(
        on_device,
        mesh=mesh,
        in_specs=(
            P("seq", "ch"),
            P("seq", "ch"),
            P("seq", "ch"),
            P(None, None, "ch"),
            P("seq", "ch"),
            P("ch"),
            P(None, "ch"),
        ),
        out_specs=P("seq", "ch"),
        check_vma=False,
    )
```

```python
import functools

import jax
import jax.numpy as jnp
import numpy as np
from jax import lax
from jax.experimental import pallas as pl
from jax.experimental.pallas import tpu as pltpu
from jax.sharding import PartitionSpec as P

high = lax.Precision.HIGH
LANES = 128
MESH = pl.DeviceIdType.MESH


def exchange_kernel(group, count, *refs):
    sources, targets = refs[:count], refs[count : 2 * count]
    send_sem, recv_sem, local_sem = refs[2 * count :]
    me = lax.axis_index("seq")
    ch = lax.axis_index("ch")
    barrier = pltpu.get_barrier_semaphore()
    for step in range(1, group):
        peer = lax.rem(me + step, group)
        pl.semaphore_signal(barrier, inc=1, device_id=(peer, ch), device_id_type=MESH)
    pl.semaphore_wait(barrier, group - 1)
    locals_ = []
    for a in range(count):
        cp = pltpu.make_async_copy(sources[a].at[me], targets[a].at[me], local_sem.at[a])
        cp.start()
        locals_.append(cp)
    sent = []
    for step in range(1, group):
        peer = lax.rem(me + step, group)
        for a in range(count):
            cp = pltpu.make_async_remote_copy(
                src_ref=sources[a].at[peer],
                dst_ref=targets[a].at[me],
                send_sem=send_sem.at[a, step],
                recv_sem=recv_sem.at[a, step],
                device_id=(peer, ch),
                device_id_type=MESH,
            )
            cp.start()
            sent.append(cp)
    for cp in locals_:
        cp.wait()
    for cp in sent:
        cp.wait_send()
    for step in range(1, group):
        origin = lax.rem(me + group - step, group)
        for a in range(count):
            pltpu.make_async_remote_copy(
                src_ref=sources[a].at[origin],
                dst_ref=targets[a].at[origin],
                send_sem=send_sem.at[a, step],
                recv_sem=recv_sem.at[a, step],
                device_id=(origin, ch),
                device_id_type=MESH,
            ).wait_recv()


def exchange(arrays, group, tag):
    count = len(arrays)
    return pl.pallas_call(
        functools.partial(exchange_kernel, group, count),
        out_shape=[jax.ShapeDtypeStruct(a.shape, a.dtype) for a in arrays],
        in_specs=[pl.BlockSpec(memory_space=pl.ANY)] * count,
        out_specs=[pl.BlockSpec(memory_space=pl.ANY)] * count,
        scratch_shapes=[
            pltpu.SemaphoreType.DMA((count, group)),
            pltpu.SemaphoreType.DMA((count, group)),
            pltpu.SemaphoreType.DMA((count,)),
        ],
        compiler_params=pltpu.CompilerParams(collective_id=tag, has_side_effects=True),
    )(*arrays)


def return_kernel(group, chans, source, target, send_sem, recv_sem, pass_sem, got_sem, fwd_sem, local_sem):
    me = lax.axis_index("seq")
    ch = lax.axis_index("ch")
    sibling = ch + 1 - 2 * lax.rem(ch, 2)
    across = [lax.rem(ch + 2 * hop, chans) for hop in range(1, chans // 2)]
    barrier = pltpu.get_barrier_semaphore()
    for step in range(1, group):
        peer = lax.rem(me + step, group)
        pl.semaphore_signal(barrier, inc=1, device_id=(peer, ch), device_id_type=MESH)
    for peer_ch in across + [sibling]:
        pl.semaphore_signal(barrier, inc=1, device_id=(me, peer_ch), device_id_type=MESH)
    pl.semaphore_wait(barrier, group - 1 + len(across) + 1)
    local = pltpu.make_async_copy(source.at[me], target.at[:, ch, me], local_sem.at[0])
    local.start()
    sent = []
    for step in range(1, group):
        peer = lax.rem(me + step, group)
        cp = pltpu.make_async_remote_copy(
            src_ref=source.at[peer],
            dst_ref=target.at[:, ch, me],
            send_sem=send_sem.at[step],
            recv_sem=recv_sem.at[step],
            device_id=(peer, ch),
            device_id_type=MESH,
        )
        cp.start()
        sent.append(cp)
    local.wait()
    for step in range(1, group):
        origin = lax.rem(me + group - step, group)
        pltpu.make_async_remote_copy(
            src_ref=source.at[origin],
            dst_ref=target.at[:, ch, origin],
            send_sem=send_sem.at[step],
            recv_sem=recv_sem.at[step],
            device_id=(origin, ch),
            device_id_type=MESH,
        ).wait_recv()
    passed = []
    for slot, peer_ch in enumerate(across + [sibling]):
        cp = pltpu.make_async_remote_copy(
            src_ref=target.at[:, ch],
            dst_ref=target.at[:, ch],
            send_sem=pass_sem.at[slot],
            recv_sem=got_sem.at[ch],
            device_id=(me, peer_ch),
            device_id_type=MESH,
        )
        cp.start()
        passed.append(cp)
    forwarded = []
    for hop in range(1, chans // 2):
        origin = lax.rem(ch + chans - 2 * hop, chans)
        pltpu.make_async_remote_copy(
            src_ref=target.at[:, origin],
            dst_ref=target.at[:, origin],
            send_sem=pass_sem.at[0],
            recv_sem=got_sem.at[origin],
            device_id=(me, origin),
            device_id_type=MESH,
        ).wait_recv()
        cp = pltpu.make_async_remote_copy(
            src_ref=target.at[:, origin],
            dst_ref=target.at[:, origin],
            send_sem=fwd_sem.at[hop],
            recv_sem=got_sem.at[origin],
            device_id=(me, sibling),
            device_id_type=MESH,
        )
        cp.start()
        forwarded.append(cp)
    for cp in sent + passed + forwarded:
        cp.wait_send()
    for hop in range(1, chans // 2):
        origin = lax.rem(sibling + chans - 2 * hop, chans)
        pltpu.make_async_remote_copy(
            src_ref=target.at[:, origin],
            dst_ref=target.at[:, origin],
            send_sem=pass_sem.at[0],
            recv_sem=got_sem.at[origin],
            device_id=(me, origin),
            device_id_type=MESH,
        ).wait_recv()
    pltpu.make_async_remote_copy(
        src_ref=target.at[:, sibling],
        dst_ref=target.at[:, sibling],
        send_sem=pass_sem.at[0],
        recv_sem=got_sem.at[sibling],
        device_id=(me, sibling),
        device_id_type=MESH,
    ).wait_recv()


def return_and_gather(block, group, chans, tag):
    return pl.pallas_call(
        functools.partial(return_kernel, group, chans),
        out_shape=jax.ShapeDtypeStruct(
            (block.shape[1], chans, block.shape[0]) + block.shape[2:], block.dtype
        ),
        in_specs=[pl.BlockSpec(memory_space=pl.ANY)],
        out_specs=pl.BlockSpec(memory_space=pl.ANY),
        scratch_shapes=[
            pltpu.SemaphoreType.DMA((group,)),
            pltpu.SemaphoreType.DMA((group,)),
            pltpu.SemaphoreType.DMA((chans // 2,)),
            pltpu.SemaphoreType.DMA((chans,)),
            pltpu.SemaphoreType.DMA((chans // 2,)),
            pltpu.SemaphoreType.DMA((1,)),
        ],
        compiler_params=pltpu.CompilerParams(collective_id=tag, has_side_effects=True),
    )(block)


def contract(pattern, first_op, second_op):
    return jnp.einsum(
        pattern, first_op, second_op, precision=high, preferred_element_type=jnp.float32
    )


def tables(seq_len):
    total = 2 * seq_len
    outer = total // LANES
    half = seq_len // LANES
    k1 = np.arange(outer)[:, None]
    a1 = 2.0 * np.pi * ((k1 * np.arange(half)[None, :]) % outer) / outer
    at = 2.0 * np.pi * ((k1 * np.arange(LANES)[None, :]) % total) / total
    m2 = np.arange(LANES)
    a2 = 2.0 * np.pi * ((m2[:, None] * m2[None, :]) % LANES) / LANES
    c1, s1 = np.cos(a1), np.sin(a1)
    c2, s2 = np.cos(a2), np.sin(a2)
    f32 = lambda v: jnp.asarray(v, jnp.float32)
    return dict(
        first=f32(np.concatenate([c1, -s1], axis=0)),
        tc=f32(np.cos(at)[:, None, :]),
        ts=f32(np.sin(at)[:, None, :]),
        fwd2=f32(np.block([[c2, -s2], [s2, c2]])),
        inv2=f32(np.block([[c2, s2], [-s2, c2]])),
        last=f32(np.concatenate([c1.T, -s1.T], axis=1) / total),
    )


def forward(signal, tb):
    outer = tb["tc"].shape[0]
    both = contract("kn,ncm->kcm", tb["first"], signal)
    br, bi = both[:outer], both[outer:]
    tr, ti = tb["tc"], -tb["ts"]
    twisted = jnp.concatenate([br * tr - bi * ti, br * ti + bi * tr], axis=2)
    return contract("kcm,mj->kcj", twisted, tb["fwd2"])


def inverse(spectrum, tb):
    z = contract("kcj,jm->kcm", spectrum, tb["inv2"])
    zr, zi = z[:, :, :LANES], z[:, :, LANES:]
    tc, ts = tb["tc"], tb["ts"]
    stacked = jnp.concatenate([zr * tc - zi * ts, zr * ts + zi * tc], axis=0)
    return contract("nk,kcm->ncm", tb["last"], stacked)


def long_conv(mixed_in, long_filter):
    half = mixed_in.shape[0]
    tb = tables(half * LANES)
    xs = forward(mixed_in, tb)
    hs = forward(long_filter, tb)
    xr, xi = xs[:, :, :LANES], xs[:, :, LANES:]
    hr, hi = hs[:, :, :LANES], hs[:, :, LANES:]
    product = jnp.concatenate([xr * hr - xi * hi, xr * hi + xi * hr], axis=2)
    return inverse(product, tb)


def shift_seq(signal, distance):
    rows, width, lanes = signal.shape
    prev = jnp.concatenate([jnp.zeros((1, width, lanes), signal.dtype), signal[:-1]], axis=0)
    return jnp.concatenate(
        [prev[:, :, lanes - distance :], signal[:, :, : lanes - distance]], axis=2
    )


def short_conv(signal, taps):
    summed = taps[0][None, :, None] * signal
    for offset in range(1, taps.shape[0]):
        summed = summed + taps[offset][None, :, None] * shift_seq(signal, offset)
    return summed


def to_ncm(block):
    rows, width = block.shape
    return block.reshape(rows // LANES, LANES, width).transpose(0, 2, 1)


def on_device(out_gate, in_gate, values, short_filter, long_filter, skip_gain, out_weight):
    seq_count = lax.axis_size("seq")
    seq_index = lax.axis_index("seq")
    rows = out_gate.shape[0]
    width = out_gate.shape[1] // seq_count
    half = rows // LANES

    def by_target(block):
        return to_ncm(block).reshape(half, seq_count, width, LANES).transpose(1, 0, 2, 3)

    planes = [out_gate, in_gate, values, long_filter.astype(jnp.bfloat16)]
    stacked = jnp.stack([by_target(plane) for plane in planes], axis=1)
    (spread,) = exchange([stacked], seq_count, 0)
    spread = spread.transpose(1, 0, 2, 3, 4).reshape(len(planes), seq_count * half, width, LANES)
    start = seq_index * width
    taps = lax.dynamic_slice_in_dim(short_filter, start, width, axis=2)
    gain = lax.dynamic_slice_in_dim(skip_gain, start, width, axis=0)
    spread = spread.astype(jnp.float32)
    gate_late = short_conv(spread[0], taps[0])
    mixed_in = short_conv(spread[1], taps[1]) * short_conv(spread[2], taps[2])
    long_out = long_conv(mixed_in, spread[3])
    filtered = long_out + gain[None, :, None] * mixed_in
    mixed = (gate_late * filtered).astype(jnp.bfloat16)
    chans = lax.axis_size("ch")
    gathered = return_and_gather(mixed.reshape(seq_count, half, width, LANES), seq_count, chans, 1)
    gathered = gathered.reshape(half, chans * seq_count * width, LANES)
    summed = jnp.einsum(
        "ncm,co->nmo", gathered, out_weight, preferred_element_type=jnp.float32
    )
    return summed.reshape(rows, -1).astype(jnp.bfloat16)


def solution(mesh):
    return jax.shard_map(
        on_device,
        mesh=mesh,
        in_specs=(
            P("seq", "ch"),
            P("seq", "ch"),
            P("seq", "ch"),
            P(None, None, "ch"),
            P("seq", "ch"),
            P("ch"),
            P(None, "ch"),
        ),
        out_specs=P("seq", "ch"),
        check_vma=False,
    )
```

```python
import functools

import jax
import jax.numpy as jnp
import numpy as np
from jax import lax
from jax.experimental import pallas as pl
from jax.experimental.pallas import tpu as pltpu
from jax.sharding import PartitionSpec as P

high = lax.Precision.HIGH
LANES = 128
MESH = pl.DeviceIdType.MESH


def exchange_kernel(group, count, *refs):
    sources, targets = refs[:count], refs[count : 2 * count]
    send_sem, recv_sem, local_sem = refs[2 * count :]
    me = lax.axis_index("seq")
    ch = lax.axis_index("ch")
    barrier = pltpu.get_barrier_semaphore()
    for step in range(1, group):
        peer = lax.rem(me + step, group)
        pl.semaphore_signal(barrier, inc=1, device_id=(peer, ch), device_id_type=MESH)
    pl.semaphore_wait(barrier, group - 1)
    locals_ = []
    for a in range(count):
        cp = pltpu.make_async_copy(sources[a].at[me], targets[a].at[me], local_sem.at[a])
        cp.start()
        locals_.append(cp)
    sent = []
    for step in range(1, group):
        peer = lax.rem(me + step, group)
        for a in range(count):
            cp = pltpu.make_async_remote_copy(
                src_ref=sources[a].at[peer],
                dst_ref=targets[a].at[me],
                send_sem=send_sem.at[a, step],
                recv_sem=recv_sem.at[a, step],
                device_id=(peer, ch),
                device_id_type=MESH,
            )
            cp.start()
            sent.append(cp)
    for cp in locals_:
        cp.wait()
    for cp in sent:
        cp.wait_send()
    for step in range(1, group):
        origin = lax.rem(me + group - step, group)
        for a in range(count):
            pltpu.make_async_remote_copy(
                src_ref=sources[a].at[origin],
                dst_ref=targets[a].at[origin],
                send_sem=send_sem.at[a, step],
                recv_sem=recv_sem.at[a, step],
                device_id=(origin, ch),
                device_id_type=MESH,
            ).wait_recv()


def exchange(arrays, group, tag):
    count = len(arrays)
    return pl.pallas_call(
        functools.partial(exchange_kernel, group, count),
        out_shape=[jax.ShapeDtypeStruct(a.shape, a.dtype) for a in arrays],
        in_specs=[pl.BlockSpec(memory_space=pl.ANY)] * count,
        out_specs=[pl.BlockSpec(memory_space=pl.ANY)] * count,
        scratch_shapes=[
            pltpu.SemaphoreType.DMA((count, group)),
            pltpu.SemaphoreType.DMA((count, group)),
            pltpu.SemaphoreType.DMA((count,)),
        ],
        compiler_params=pltpu.CompilerParams(collective_id=tag, has_side_effects=True),
    )(*arrays)


def return_kernel(group, chans, source, target, send_sem, recv_sem, pass_sem, got_sem, fwd_sem, local_sem):
    me = lax.axis_index("seq")
    ch = lax.axis_index("ch")
    half = source.shape[1]
    sibling = ch + 1 - 2 * lax.rem(ch, 2)
    across = [lax.rem(ch + 2 * hop, chans) for hop in range(1, chans // 2)]
    barrier = pltpu.get_barrier_semaphore()
    for step in range(1, group):
        peer = lax.rem(me + step, group)
        pl.semaphore_signal(barrier, inc=1, device_id=(peer, ch), device_id_type=MESH)
    for peer_ch in across + [sibling]:
        pl.semaphore_signal(barrier, inc=1, device_id=(me, peer_ch), device_id_type=MESH)
    pl.semaphore_wait(barrier, group - 1 + len(across) + 1)

    def incoming(part, slot, peer_ch):
        return pltpu.make_async_remote_copy(
            src_ref=target.at[part, slot],
            dst_ref=target.at[part, slot],
            send_sem=pass_sem.at[part, 0],
            recv_sem=got_sem.at[part, slot],
            device_id=(me, peer_ch),
            device_id_type=MESH,
        )

    sent = []
    locals_ = []
    for part in range(half):
        cp = pltpu.make_async_copy(
            source.at[me, part], target.at[part, ch, me], local_sem.at[part]
        )
        cp.start()
        locals_.append(cp)
        for step in range(1, group):
            peer = lax.rem(me + step, group)
            cp = pltpu.make_async_remote_copy(
                src_ref=source.at[peer, part],
                dst_ref=target.at[part, ch, me],
                send_sem=send_sem.at[part, step],
                recv_sem=recv_sem.at[part, step],
                device_id=(peer, ch),
                device_id_type=MESH,
            )
            cp.start()
            sent.append(cp)
    passed = []
    for part in range(half):
        locals_[part].wait()
        for step in range(1, group):
            origin = lax.rem(me + group - step, group)
            pltpu.make_async_remote_copy(
                src_ref=source.at[origin, part],
                dst_ref=target.at[part, ch, origin],
                send_sem=send_sem.at[part, step],
                recv_sem=recv_sem.at[part, step],
                device_id=(origin, ch),
                device_id_type=MESH,
            ).wait_recv()
        for slot, peer_ch in enumerate(across + [sibling]):
            cp = pltpu.make_async_remote_copy(
                src_ref=target.at[part, ch],
                dst_ref=target.at[part, ch],
                send_sem=pass_sem.at[part, slot],
                recv_sem=got_sem.at[part, ch],
                device_id=(me, peer_ch),
                device_id_type=MESH,
            )
            cp.start()
            passed.append(cp)
    forwarded = []
    for part in range(half):
        for hop in range(1, chans // 2):
            origin = lax.rem(ch + chans - 2 * hop, chans)
            incoming(part, origin, origin).wait_recv()
            cp = pltpu.make_async_remote_copy(
                src_ref=target.at[part, origin],
                dst_ref=target.at[part, origin],
                send_sem=fwd_sem.at[part, hop],
                recv_sem=got_sem.at[part, origin],
                device_id=(me, sibling),
                device_id_type=MESH,
            )
            cp.start()
            forwarded.append(cp)
    for cp in sent + passed + forwarded:
        cp.wait_send()
    for part in range(half):
        for hop in range(1, chans // 2):
            origin = lax.rem(sibling + chans - 2 * hop, chans)
            incoming(part, origin, origin).wait_recv()
        incoming(part, sibling, sibling).wait_recv()


def return_and_gather(block, group, chans, tag):
    half = block.shape[1]
    return pl.pallas_call(
        functools.partial(return_kernel, group, chans),
        out_shape=jax.ShapeDtypeStruct(
            (half, chans, block.shape[0]) + block.shape[2:], block.dtype
        ),
        in_specs=[pl.BlockSpec(memory_space=pl.ANY)],
        out_specs=pl.BlockSpec(memory_space=pl.ANY),
        scratch_shapes=[
            pltpu.SemaphoreType.DMA((half, group)),
            pltpu.SemaphoreType.DMA((half, group)),
            pltpu.SemaphoreType.DMA((half, chans // 2)),
            pltpu.SemaphoreType.DMA((half, chans)),
            pltpu.SemaphoreType.DMA((half, chans // 2)),
            pltpu.SemaphoreType.DMA((half,)),
        ],
        compiler_params=pltpu.CompilerParams(collective_id=tag, has_side_effects=True),
    )(block)


def contract(pattern, first_op, second_op):
    return jnp.einsum(
        pattern, first_op, second_op, precision=high, preferred_element_type=jnp.float32
    )


def tables(seq_len):
    total = 2 * seq_len
    outer = total // LANES
    half = seq_len // LANES
    k1 = np.arange(outer)[:, None]
    a1 = 2.0 * np.pi * ((k1 * np.arange(half)[None, :]) % outer) / outer
    at = 2.0 * np.pi * ((k1 * np.arange(LANES)[None, :]) % total) / total
    m2 = np.arange(LANES)
    a2 = 2.0 * np.pi * ((m2[:, None] * m2[None, :]) % LANES) / LANES
    c1, s1 = np.cos(a1), np.sin(a1)
    c2, s2 = np.cos(a2), np.sin(a2)
    f32 = lambda v: jnp.asarray(v, jnp.float32)
    return dict(
        first=f32(np.concatenate([c1, -s1], axis=0)),
        tc=f32(np.cos(at)[:, None, :]),
        ts=f32(np.sin(at)[:, None, :]),
        fwd2=f32(np.block([[c2, -s2], [s2, c2]])),
        inv2=f32(np.block([[c2, s2], [-s2, c2]])),
        last=f32(np.concatenate([c1.T, -s1.T], axis=1) / total),
    )


def forward(signal, tb):
    outer = tb["tc"].shape[0]
    both = contract("kn,ncm->kcm", tb["first"], signal)
    br, bi = both[:outer], both[outer:]
    tr, ti = tb["tc"], -tb["ts"]
    twisted = jnp.concatenate([br * tr - bi * ti, br * ti + bi * tr], axis=2)
    return contract("kcm,mj->kcj", twisted, tb["fwd2"])


def inverse(spectrum, tb):
    z = contract("kcj,jm->kcm", spectrum, tb["inv2"])
    zr, zi = z[:, :, :LANES], z[:, :, LANES:]
    tc, ts = tb["tc"], tb["ts"]
    stacked = jnp.concatenate([zr * tc - zi * ts, zr * ts + zi * tc], axis=0)
    return contract("nk,kcm->ncm", tb["last"], stacked)


def long_conv(mixed_in, long_filter):
    half = mixed_in.shape[0]
    tb = tables(half * LANES)
    xs = forward(mixed_in, tb)
    hs = forward(long_filter, tb)
    xr, xi = xs[:, :, :LANES], xs[:, :, LANES:]
    hr, hi = hs[:, :, :LANES], hs[:, :, LANES:]
    product = jnp.concatenate([xr * hr - xi * hi, xr * hi + xi * hr], axis=2)
    return inverse(product, tb)


def shift_seq(signal, distance):
    rows, width, lanes = signal.shape
    prev = jnp.concatenate([jnp.zeros((1, width, lanes), signal.dtype), signal[:-1]], axis=0)
    return jnp.concatenate(
        [prev[:, :, lanes - distance :], signal[:, :, : lanes - distance]], axis=2
    )


def short_conv(signal, taps):
    summed = taps[0][None, :, None] * signal
    for offset in range(1, taps.shape[0]):
        summed = summed + taps[offset][None, :, None] * shift_seq(signal, offset)
    return summed


def to_ncm(block):
    rows, width = block.shape
    return block.reshape(rows // LANES, LANES, width).transpose(0, 2, 1)


def on_device(out_gate, in_gate, values, short_filter, long_filter, skip_gain, out_weight):
    seq_count = lax.axis_size("seq")
    seq_index = lax.axis_index("seq")
    rows = out_gate.shape[0]
    width = out_gate.shape[1] // seq_count
    half = rows // LANES

    def by_target(block):
        return to_ncm(block).reshape(half, seq_count, width, LANES).transpose(1, 0, 2, 3)

    planes = [out_gate, in_gate, values, long_filter.astype(jnp.bfloat16)]
    stacked = jnp.stack([by_target(plane) for plane in planes], axis=1)
    (spread,) = exchange([stacked], seq_count, 0)
    spread = spread.transpose(1, 0, 2, 3, 4).reshape(len(planes), seq_count * half, width, LANES)
    start = seq_index * width
    taps = lax.dynamic_slice_in_dim(short_filter, start, width, axis=2)
    gain = lax.dynamic_slice_in_dim(skip_gain, start, width, axis=0)
    spread = spread.astype(jnp.float32)
    gate_late = short_conv(spread[0], taps[0])
    mixed_in = short_conv(spread[1], taps[1]) * short_conv(spread[2], taps[2])
    long_out = long_conv(mixed_in, spread[3])
    filtered = long_out + gain[None, :, None] * mixed_in
    mixed = (gate_late * filtered).astype(jnp.bfloat16)
    chans = lax.axis_size("ch")
    gathered = return_and_gather(mixed.reshape(seq_count, half, width, LANES), seq_count, chans, 1)
    gathered = gathered.reshape(half, chans * seq_count * width, LANES)
    summed = jnp.einsum(
        "ncm,co->nmo", gathered, out_weight, preferred_element_type=jnp.float32
    )
    return summed.reshape(rows, -1).astype(jnp.bfloat16)


def solution(mesh):
    return jax.shard_map(
        on_device,
        mesh=mesh,
        in_specs=(
            P("seq", "ch"),
            P("seq", "ch"),
            P("seq", "ch"),
            P(None, None, "ch"),
            P("seq", "ch"),
            P("ch"),
            P(None, "ch"),
        ),
        out_specs=P("seq", "ch"),
        check_vma=False,
    )
```

```python
import functools

import jax
import jax.numpy as jnp
import numpy as np
from jax import lax
from jax.experimental import pallas as pl
from jax.experimental.pallas import tpu as pltpu
from jax.sharding import PartitionSpec as P

high = lax.Precision.HIGH
LANES = 128
MESH = pl.DeviceIdType.MESH


def exchange_kernel(group, count, *refs):
    sources, targets = refs[:count], refs[count : 2 * count]
    send_sem, recv_sem, local_sem = refs[2 * count :]
    me = lax.axis_index("seq")
    ch = lax.axis_index("ch")
    barrier = pltpu.get_barrier_semaphore()
    for step in range(1, group):
        peer = lax.rem(me + step, group)
        pl.semaphore_signal(barrier, inc=1, device_id=(peer, ch), device_id_type=MESH)
    pl.semaphore_wait(barrier, group - 1)
    locals_ = []
    for a in range(count):
        cp = pltpu.make_async_copy(sources[a].at[me], targets[a].at[me], local_sem.at[a])
        cp.start()
        locals_.append(cp)
    sent = []
    for step in range(1, group):
        peer = lax.rem(me + step, group)
        for a in range(count):
            cp = pltpu.make_async_remote_copy(
                src_ref=sources[a].at[peer],
                dst_ref=targets[a].at[me],
                send_sem=send_sem.at[a, step],
                recv_sem=recv_sem.at[a, step],
                device_id=(peer, ch),
                device_id_type=MESH,
            )
            cp.start()
            sent.append(cp)
    for cp in locals_:
        cp.wait()
    for cp in sent:
        cp.wait_send()
    for step in range(1, group):
        origin = lax.rem(me + group - step, group)
        for a in range(count):
            pltpu.make_async_remote_copy(
                src_ref=sources[a].at[origin],
                dst_ref=targets[a].at[origin],
                send_sem=send_sem.at[a, step],
                recv_sem=recv_sem.at[a, step],
                device_id=(origin, ch),
                device_id_type=MESH,
            ).wait_recv()


def exchange(arrays, group, tag):
    count = len(arrays)
    return pl.pallas_call(
        functools.partial(exchange_kernel, group, count),
        out_shape=[jax.ShapeDtypeStruct(a.shape, a.dtype) for a in arrays],
        in_specs=[pl.BlockSpec(memory_space=pl.ANY)] * count,
        out_specs=[pl.BlockSpec(memory_space=pl.ANY)] * count,
        scratch_shapes=[
            pltpu.SemaphoreType.DMA((count, group)),
            pltpu.SemaphoreType.DMA((count, group)),
            pltpu.SemaphoreType.DMA((count,)),
        ],
        compiler_params=pltpu.CompilerParams(collective_id=tag, has_side_effects=True),
    )(*arrays)


def return_kernel(group, chans, source, target, send_sem, recv_sem, pass_sem, got_sem, fwd_sem, local_sem):
    me = lax.axis_index("seq")
    ch = lax.axis_index("ch")
    half = source.shape[1]
    sibling = ch + 1 - 2 * lax.rem(ch, 2)
    across = [lax.rem(ch + 2 * hop, chans) for hop in range(1, chans // 2)]
    barrier = pltpu.get_barrier_semaphore()
    for step in range(1, group):
        peer = lax.rem(me + step, group)
        pl.semaphore_signal(barrier, inc=1, device_id=(peer, ch), device_id_type=MESH)
    for peer_ch in across + [sibling]:
        pl.semaphore_signal(barrier, inc=1, device_id=(me, peer_ch), device_id_type=MESH)
    pl.semaphore_wait(barrier, group - 1 + len(across) + 1)

    def incoming(part, slot, peer_ch):
        return pltpu.make_async_remote_copy(
            src_ref=target.at[part, slot],
            dst_ref=target.at[part, slot],
            send_sem=pass_sem.at[part, 0],
            recv_sem=got_sem.at[part, slot],
            device_id=(me, peer_ch),
            device_id_type=MESH,
        )

    sent = []
    locals_ = []
    for part in range(half):
        cp = pltpu.make_async_copy(
            source.at[me, part], target.at[part, ch, me], local_sem.at[part]
        )
        cp.start()
        locals_.append(cp)
        for step in range(1, group):
            peer = lax.rem(me + step, group)
            cp = pltpu.make_async_remote_copy(
                src_ref=source.at[peer, part],
                dst_ref=target.at[part, ch, me],
                send_sem=send_sem.at[part, step],
                recv_sem=recv_sem.at[part, step],
                device_id=(peer, ch),
                device_id_type=MESH,
            )
            cp.start()
            sent.append(cp)
    passed = []
    for part in range(half):
        locals_[part].wait()
        for step in range(1, group):
            origin = lax.rem(me + group - step, group)
            pltpu.make_async_remote_copy(
                src_ref=source.at[origin, part],
                dst_ref=target.at[part, ch, origin],
                send_sem=send_sem.at[part, step],
                recv_sem=recv_sem.at[part, step],
                device_id=(origin, ch),
                device_id_type=MESH,
            ).wait_recv()
        for slot, peer_ch in enumerate(across + [sibling]):
            cp = pltpu.make_async_remote_copy(
                src_ref=target.at[part, ch],
                dst_ref=target.at[part, ch],
                send_sem=pass_sem.at[part, slot],
                recv_sem=got_sem.at[part, ch],
                device_id=(me, peer_ch),
                device_id_type=MESH,
            )
            cp.start()
            passed.append(cp)
    forwarded = []
    for part in range(half):
        for hop in range(1, chans // 2):
            origin = lax.rem(ch + chans - 2 * hop, chans)
            incoming(part, origin, origin).wait_recv()
            cp = pltpu.make_async_remote_copy(
                src_ref=target.at[part, origin],
                dst_ref=target.at[part, origin],
                send_sem=fwd_sem.at[part, hop],
                recv_sem=got_sem.at[part, origin],
                device_id=(me, sibling),
                device_id_type=MESH,
            )
            cp.start()
            forwarded.append(cp)
    for cp in sent + passed + forwarded:
        cp.wait_send()
    for part in range(half):
        for hop in range(1, chans // 2):
            origin = lax.rem(sibling + chans - 2 * hop, chans)
            incoming(part, origin, origin).wait_recv()
        incoming(part, sibling, sibling).wait_recv()


def return_and_gather(block, group, chans, tag):
    half = block.shape[1]
    return pl.pallas_call(
        functools.partial(return_kernel, group, chans),
        out_shape=jax.ShapeDtypeStruct(
            (half, chans, block.shape[0]) + block.shape[2:], block.dtype
        ),
        in_specs=[pl.BlockSpec(memory_space=pl.ANY)],
        out_specs=pl.BlockSpec(memory_space=pl.ANY),
        scratch_shapes=[
            pltpu.SemaphoreType.DMA((half, group)),
            pltpu.SemaphoreType.DMA((half, group)),
            pltpu.SemaphoreType.DMA((half, chans // 2)),
            pltpu.SemaphoreType.DMA((half, chans)),
            pltpu.SemaphoreType.DMA((half, chans // 2)),
            pltpu.SemaphoreType.DMA((half,)),
        ],
        compiler_params=pltpu.CompilerParams(collective_id=tag, has_side_effects=True),
    )(block)


def contract(pattern, first_op, second_op):
    return jnp.einsum(
        pattern, first_op, second_op, precision=high, preferred_element_type=jnp.float32
    )


def tables(seq_len):
    total = 2 * seq_len
    outer = total // LANES
    half = seq_len // LANES
    k1 = np.arange(outer)[:, None]
    a1 = 2.0 * np.pi * ((k1 * np.arange(half)[None, :]) % outer) / outer
    at = 2.0 * np.pi * ((k1 * np.arange(LANES)[None, :]) % total) / total
    m2 = np.arange(LANES)
    a2 = 2.0 * np.pi * ((m2[:, None] * m2[None, :]) % LANES) / LANES
    c1, s1 = np.cos(a1), np.sin(a1)
    c2, s2 = np.cos(a2), np.sin(a2)
    f32 = lambda v: jnp.asarray(v, jnp.float32)
    return dict(
        first=f32(np.concatenate([c1, -s1], axis=0)),
        tc=f32(np.cos(at)[:, None, :]),
        ts=f32(np.sin(at)[:, None, :]),
        fwd2=f32(np.block([[c2, -s2], [s2, c2]])),
        inv2=f32(np.block([[c2, s2], [-s2, c2]])),
        last=f32(np.concatenate([c1.T, -s1.T], axis=1) / total),
    )


def forward(signal, tb):
    outer = tb["tc"].shape[0]
    both = contract("kn,ncm->kcm", tb["first"], signal)
    br, bi = both[:outer], both[outer:]
    tr, ti = tb["tc"], -tb["ts"]
    twisted = jnp.concatenate([br * tr - bi * ti, br * ti + bi * tr], axis=2)
    return contract("kcm,mj->kcj", twisted, tb["fwd2"])


def inverse(spectrum, tb):
    z = contract("kcj,jm->kcm", spectrum, tb["inv2"])
    zr, zi = z[:, :, :LANES], z[:, :, LANES:]
    tc, ts = tb["tc"], tb["ts"]
    stacked = jnp.concatenate([zr * tc - zi * ts, zr * ts + zi * tc], axis=0)
    return contract("nk,kcm->ncm", tb["last"], stacked)


def long_conv(mixed_in, long_filter):
    half = mixed_in.shape[0]
    tb = tables(half * LANES)
    xs = forward(mixed_in, tb)
    hs = forward(long_filter, tb)
    xr, xi = xs[:, :, :LANES], xs[:, :, LANES:]
    hr, hi = hs[:, :, :LANES], hs[:, :, LANES:]
    product = jnp.concatenate([xr * hr - xi * hi, xr * hi + xi * hr], axis=2)
    return inverse(product, tb)


def shift_seq(signal, distance):
    rows, width, lanes = signal.shape
    prev = jnp.concatenate([jnp.zeros((1, width, lanes), signal.dtype), signal[:-1]], axis=0)
    return jnp.concatenate(
        [prev[:, :, lanes - distance :], signal[:, :, : lanes - distance]], axis=2
    )


def short_conv(signal, taps):
    summed = taps[0][None, :, None] * signal
    for offset in range(1, taps.shape[0]):
        summed = summed + taps[offset][None, :, None] * shift_seq(signal, offset)
    return summed


def to_ncm(block):
    rows, width = block.shape
    return block.reshape(rows // LANES, LANES, width).transpose(0, 2, 1)


def on_device(out_gate, in_gate, values, short_filter, long_filter, skip_gain, out_weight):
    seq_count = lax.axis_size("seq")
    seq_index = lax.axis_index("seq")
    rows = out_gate.shape[0]
    width = out_gate.shape[1] // seq_count
    half = rows // LANES

    def by_target(block):
        return to_ncm(block).reshape(half, seq_count, width, LANES).transpose(1, 0, 2, 3)

    gate_in = lax.all_to_all(to_ncm(out_gate), "seq", split_axis=1, concat_axis=0, tiled=True)
    planes = [in_gate, values, long_filter.astype(jnp.bfloat16)]
    stacked = jnp.stack([by_target(plane) for plane in planes], axis=1)
    (spread,) = exchange([stacked], seq_count, 0)
    spread = spread.transpose(1, 0, 2, 3, 4).reshape(len(planes), seq_count * half, width, LANES)
    start = seq_index * width
    taps = lax.dynamic_slice_in_dim(short_filter, start, width, axis=2)
    gain = lax.dynamic_slice_in_dim(skip_gain, start, width, axis=0)
    spread = spread.astype(jnp.float32)
    mixed_in = short_conv(spread[0], taps[1]) * short_conv(spread[1], taps[2])
    long_out = long_conv(mixed_in, spread[2])
    gate_late = short_conv(gate_in.astype(jnp.float32), taps[0])
    filtered = long_out + gain[None, :, None] * mixed_in
    mixed = (gate_late * filtered).astype(jnp.bfloat16)
    chans = lax.axis_size("ch")
    gathered = return_and_gather(mixed.reshape(seq_count, half, width, LANES), seq_count, chans, 1)
    gathered = gathered.reshape(half, chans * seq_count * width, LANES)
    summed = jnp.einsum(
        "ncm,co->nmo", gathered, out_weight, preferred_element_type=jnp.float32
    )
    return summed.reshape(rows, -1).astype(jnp.bfloat16)


def solution(mesh):
    return jax.shard_map(
        on_device,
        mesh=mesh,
        in_specs=(
            P("seq", "ch"),
            P("seq", "ch"),
            P("seq", "ch"),
            P(None, None, "ch"),
            P("seq", "ch"),
            P("ch"),
            P(None, "ch"),
        ),
        out_specs=P("seq", "ch"),
        check_vma=False,
    )
```

```python
import functools

import jax
import jax.numpy as jnp
import numpy as np
from jax import lax
from jax.experimental import pallas as pl
from jax.experimental.pallas import tpu as pltpu
from jax.sharding import PartitionSpec as P

high = lax.Precision.HIGH
LANES = 128
MESH = pl.DeviceIdType.MESH


def exchange_kernel(group, count, *refs):
    sources, targets = refs[:count], refs[count : 2 * count]
    send_sem, recv_sem, local_sem = refs[2 * count :]
    me = lax.axis_index("seq")
    ch = lax.axis_index("ch")
    locals_ = []
    for a in range(count):
        cp = pltpu.make_async_copy(sources[a].at[me], targets[a].at[me], local_sem.at[a])
        cp.start()
        locals_.append(cp)
    sent = []
    for step in range(1, group):
        peer = lax.rem(me + step, group)
        for a in range(count):
            cp = pltpu.make_async_remote_copy(
                src_ref=sources[a].at[peer],
                dst_ref=targets[a].at[me],
                send_sem=send_sem.at[a, step],
                recv_sem=recv_sem.at[a, step],
                device_id=(peer, ch),
                device_id_type=MESH,
            )
            cp.start()
            sent.append(cp)
    for cp in locals_:
        cp.wait()
    for cp in sent:
        cp.wait_send()
    for step in range(1, group):
        origin = lax.rem(me + group - step, group)
        for a in range(count):
            pltpu.make_async_remote_copy(
                src_ref=sources[a].at[origin],
                dst_ref=targets[a].at[origin],
                send_sem=send_sem.at[a, step],
                recv_sem=recv_sem.at[a, step],
                device_id=(origin, ch),
                device_id_type=MESH,
            ).wait_recv()


def exchange(arrays, group, tag):
    count = len(arrays)
    return pl.pallas_call(
        functools.partial(exchange_kernel, group, count),
        out_shape=[jax.ShapeDtypeStruct(a.shape, a.dtype) for a in arrays],
        in_specs=[pl.BlockSpec(memory_space=pl.ANY)] * count,
        out_specs=[pl.BlockSpec(memory_space=pl.ANY)] * count,
        scratch_shapes=[
            pltpu.SemaphoreType.DMA((count, group)),
            pltpu.SemaphoreType.DMA((count, group)),
            pltpu.SemaphoreType.DMA((count,)),
        ],
        compiler_params=pltpu.CompilerParams(has_side_effects=True),
    )(*arrays)


def return_kernel(group, chans, source, target, send_sem, recv_sem, pass_sem, got_sem, fwd_sem, local_sem):
    me = lax.axis_index("seq")
    ch = lax.axis_index("ch")
    half = source.shape[1]
    sibling = ch + 1 - 2 * lax.rem(ch, 2)
    across = [lax.rem(ch + 2 * hop, chans) for hop in range(1, chans // 2)]

    def incoming(part, slot, peer_ch):
        return pltpu.make_async_remote_copy(
            src_ref=target.at[part, slot],
            dst_ref=target.at[part, slot],
            send_sem=pass_sem.at[part, 0],
            recv_sem=got_sem.at[part, slot],
            device_id=(me, peer_ch),
            device_id_type=MESH,
        )

    sent = []
    locals_ = []
    for part in range(half):
        cp = pltpu.make_async_copy(
            source.at[me, part], target.at[part, ch, me], local_sem.at[part]
        )
        cp.start()
        locals_.append(cp)
        for step in range(1, group):
            peer = lax.rem(me + step, group)
            cp = pltpu.make_async_remote_copy(
                src_ref=source.at[peer, part],
                dst_ref=target.at[part, ch, me],
                send_sem=send_sem.at[part, step],
                recv_sem=recv_sem.at[part, step],
                device_id=(peer, ch),
                device_id_type=MESH,
            )
            cp.start()
            sent.append(cp)
    passed = []
    for part in range(half):
        locals_[part].wait()
        for step in range(1, group):
            origin = lax.rem(me + group - step, group)
            pltpu.make_async_remote_copy(
                src_ref=source.at[origin, part],
                dst_ref=target.at[part, ch, origin],
                send_sem=send_sem.at[part, step],
                recv_sem=recv_sem.at[part, step],
                device_id=(origin, ch),
                device_id_type=MESH,
            ).wait_recv()
        for slot, peer_ch in enumerate(across + [sibling]):
            cp = pltpu.make_async_remote_copy(
                src_ref=target.at[part, ch],
                dst_ref=target.at[part, ch],
                send_sem=pass_sem.at[part, slot],
                recv_sem=got_sem.at[part, ch],
                device_id=(me, peer_ch),
                device_id_type=MESH,
            )
            cp.start()
            passed.append(cp)
    forwarded = []
    for part in range(half):
        for hop in range(1, chans // 2):
            origin = lax.rem(ch + chans - 2 * hop, chans)
            incoming(part, origin, origin).wait_recv()
            cp = pltpu.make_async_remote_copy(
                src_ref=target.at[part, origin],
                dst_ref=target.at[part, origin],
                send_sem=fwd_sem.at[part, hop],
                recv_sem=got_sem.at[part, origin],
                device_id=(me, sibling),
                device_id_type=MESH,
            )
            cp.start()
            forwarded.append(cp)
    for cp in sent + passed + forwarded:
        cp.wait_send()
    for part in range(half):
        for hop in range(1, chans // 2):
            origin = lax.rem(sibling + chans - 2 * hop, chans)
            incoming(part, origin, origin).wait_recv()
        incoming(part, sibling, sibling).wait_recv()


def return_and_gather(block, group, chans, tag):
    half = block.shape[1]
    return pl.pallas_call(
        functools.partial(return_kernel, group, chans),
        out_shape=jax.ShapeDtypeStruct(
            (half, chans, block.shape[0]) + block.shape[2:], block.dtype
        ),
        in_specs=[pl.BlockSpec(memory_space=pl.ANY)],
        out_specs=pl.BlockSpec(memory_space=pl.ANY),
        scratch_shapes=[
            pltpu.SemaphoreType.DMA((half, group)),
            pltpu.SemaphoreType.DMA((half, group)),
            pltpu.SemaphoreType.DMA((half, chans // 2)),
            pltpu.SemaphoreType.DMA((half, chans)),
            pltpu.SemaphoreType.DMA((half, chans // 2)),
            pltpu.SemaphoreType.DMA((half,)),
        ],
        compiler_params=pltpu.CompilerParams(has_side_effects=True),
    )(block)


def contract(pattern, first_op, second_op):
    return jnp.einsum(
        pattern, first_op, second_op, precision=high, preferred_element_type=jnp.float32
    )


def tables(seq_len):
    total = 2 * seq_len
    outer = total // LANES
    half = seq_len // LANES
    k1 = np.arange(outer)[:, None]
    a1 = 2.0 * np.pi * ((k1 * np.arange(half)[None, :]) % outer) / outer
    at = 2.0 * np.pi * ((k1 * np.arange(LANES)[None, :]) % total) / total
    m2 = np.arange(LANES)
    a2 = 2.0 * np.pi * ((m2[:, None] * m2[None, :]) % LANES) / LANES
    c1, s1 = np.cos(a1), np.sin(a1)
    c2, s2 = np.cos(a2), np.sin(a2)
    f32 = lambda v: jnp.asarray(v, jnp.float32)
    return dict(
        first=f32(np.concatenate([c1, -s1], axis=0)),
        tc=f32(np.cos(at)[:, None, :]),
        ts=f32(np.sin(at)[:, None, :]),
        fwd2=f32(np.block([[c2, -s2], [s2, c2]])),
        inv2=f32(np.block([[c2, s2], [-s2, c2]])),
        last=f32(np.concatenate([c1.T, -s1.T], axis=1) / total),
    )


def forward(signal, tb):
    outer = tb["tc"].shape[0]
    both = contract("kn,ncm->kcm", tb["first"], signal)
    br, bi = both[:outer], both[outer:]
    tr, ti = tb["tc"], -tb["ts"]
    twisted = jnp.concatenate([br * tr - bi * ti, br * ti + bi * tr], axis=2)
    return contract("kcm,mj->kcj", twisted, tb["fwd2"])


def inverse(spectrum, tb):
    z = contract("kcj,jm->kcm", spectrum, tb["inv2"])
    zr, zi = z[:, :, :LANES], z[:, :, LANES:]
    tc, ts = tb["tc"], tb["ts"]
    stacked = jnp.concatenate([zr * tc - zi * ts, zr * ts + zi * tc], axis=0)
    return contract("nk,kcm->ncm", tb["last"], stacked)


def long_conv(mixed_in, long_filter):
    half = mixed_in.shape[0]
    tb = tables(half * LANES)
    xs = forward(mixed_in, tb)
    hs = forward(long_filter, tb)
    xr, xi = xs[:, :, :LANES], xs[:, :, LANES:]
    hr, hi = hs[:, :, :LANES], hs[:, :, LANES:]
    product = jnp.concatenate([xr * hr - xi * hi, xr * hi + xi * hr], axis=2)
    return inverse(product, tb)


def shift_seq(signal, distance):
    rows, width, lanes = signal.shape
    prev = jnp.concatenate([jnp.zeros((1, width, lanes), signal.dtype), signal[:-1]], axis=0)
    return jnp.concatenate(
        [prev[:, :, lanes - distance :], signal[:, :, : lanes - distance]], axis=2
    )


def short_conv(signal, taps):
    summed = taps[0][None, :, None] * signal
    for offset in range(1, taps.shape[0]):
        summed = summed + taps[offset][None, :, None] * shift_seq(signal, offset)
    return summed


def to_ncm(block):
    rows, width = block.shape
    return block.reshape(rows // LANES, LANES, width).transpose(0, 2, 1)


def on_device(out_gate, in_gate, values, short_filter, long_filter, skip_gain, out_weight):
    seq_count = lax.axis_size("seq")
    seq_index = lax.axis_index("seq")
    rows = out_gate.shape[0]
    width = out_gate.shape[1] // seq_count
    half = rows // LANES

    def by_target(block):
        return to_ncm(block).reshape(half, seq_count, width, LANES).transpose(1, 0, 2, 3)

    planes = [out_gate, in_gate, values, long_filter.astype(jnp.bfloat16)]
    stacked = jnp.stack([by_target(plane) for plane in planes], axis=1)
    (spread,) = exchange([stacked], seq_count, 0)
    spread = spread.transpose(1, 0, 2, 3, 4).reshape(len(planes), seq_count * half, width, LANES)
    start = seq_index * width
    taps = lax.dynamic_slice_in_dim(short_filter, start, width, axis=2)
    gain = lax.dynamic_slice_in_dim(skip_gain, start, width, axis=0)
    spread = spread.astype(jnp.float32)
    gate_late = short_conv(spread[0], taps[0])
    mixed_in = short_conv(spread[1], taps[1]) * short_conv(spread[2], taps[2])
    long_out = long_conv(mixed_in, spread[3])
    filtered = long_out + gain[None, :, None] * mixed_in
    mixed = (gate_late * filtered).astype(jnp.bfloat16)
    chans = lax.axis_size("ch")
    gathered = return_and_gather(mixed.reshape(seq_count, half, width, LANES), seq_count, chans, 1)
    gathered = gathered.reshape(half, chans * seq_count * width, LANES)
    summed = jnp.einsum(
        "ncm,co->nmo", gathered, out_weight, preferred_element_type=jnp.float32
    )
    return summed.reshape(rows, -1).astype(jnp.bfloat16)


def solution(mesh):
    return jax.shard_map(
        on_device,
        mesh=mesh,
        in_specs=(
            P("seq", "ch"),
            P("seq", "ch"),
            P("seq", "ch"),
            P(None, None, "ch"),
            P("seq", "ch"),
            P("ch"),
            P(None, "ch"),
        ),
        out_specs=P("seq", "ch"),
        check_vma=False,
    )
```

```python
import functools

import jax
import jax.numpy as jnp
import numpy as np
from jax import lax
from jax.experimental import pallas as pl
from jax.experimental.pallas import tpu as pltpu
from jax.sharding import PartitionSpec as P

high = lax.Precision.HIGH
LANES = 128
MESH = pl.DeviceIdType.MESH


def exchange_kernel(group, source, target, send_sem, recv_sem, local_sem):
    me = lax.axis_index("seq")
    ch = lax.axis_index("ch")
    half = source.shape[1]
    width = target.shape[2]
    barrier = pltpu.get_barrier_semaphore()
    for step in range(1, group):
        peer = lax.rem(me + step, group)
        pl.semaphore_signal(barrier, inc=1, device_id=(peer, ch), device_id_type=MESH)
    pl.semaphore_wait(barrier, group - 1)

    def piece(ref_src, peer, origin):
        return (
            ref_src.at[:, :, pl.ds(peer * width, width)],
            target.at[:, pl.ds(origin * half, half)],
        )

    src, dst = piece(source, me, me)
    local = pltpu.make_async_copy(src, dst, local_sem.at[0])
    local.start()
    sent = []
    for step in range(1, group):
        peer = lax.rem(me + step, group)
        src, dst = piece(source, peer, me)
        cp = pltpu.make_async_remote_copy(
            src_ref=src,
            dst_ref=dst,
            send_sem=send_sem.at[step],
            recv_sem=recv_sem.at[step],
            device_id=(peer, ch),
            device_id_type=MESH,
        )
        cp.start()
        sent.append(cp)
    local.wait()
    for cp in sent:
        cp.wait_send()
    for step in range(1, group):
        origin = lax.rem(me + group - step, group)
        src, dst = piece(source, me, origin)
        pltpu.make_async_remote_copy(
            src_ref=src,
            dst_ref=dst,
            send_sem=send_sem.at[step],
            recv_sem=recv_sem.at[step],
            device_id=(origin, ch),
            device_id_type=MESH,
        ).wait_recv()


def exchange(stacked, group, tag):
    planes, half, full, lanes = stacked.shape
    return pl.pallas_call(
        functools.partial(exchange_kernel, group),
        out_shape=jax.ShapeDtypeStruct((planes, group * half, full // group, lanes), stacked.dtype),
        in_specs=[pl.BlockSpec(memory_space=pl.ANY)],
        out_specs=pl.BlockSpec(memory_space=pl.ANY),
        scratch_shapes=[
            pltpu.SemaphoreType.DMA((group,)),
            pltpu.SemaphoreType.DMA((group,)),
            pltpu.SemaphoreType.DMA((1,)),
        ],
        compiler_params=pltpu.CompilerParams(collective_id=tag, has_side_effects=True),
    )(stacked)


def return_kernel(group, chans, source, target, send_sem, recv_sem, pass_sem, got_sem, fwd_sem, local_sem):
    me = lax.axis_index("seq")
    ch = lax.axis_index("ch")
    half = source.shape[1]
    sibling = ch + 1 - 2 * lax.rem(ch, 2)
    across = [lax.rem(ch + 2 * hop, chans) for hop in range(1, chans // 2)]
    barrier = pltpu.get_barrier_semaphore()
    for step in range(1, group):
        peer = lax.rem(me + step, group)
        pl.semaphore_signal(barrier, inc=1, device_id=(peer, ch), device_id_type=MESH)
    for peer_ch in across + [sibling]:
        pl.semaphore_signal(barrier, inc=1, device_id=(me, peer_ch), device_id_type=MESH)
    pl.semaphore_wait(barrier, group - 1 + len(across) + 1)

    def incoming(part, slot, peer_ch):
        return pltpu.make_async_remote_copy(
            src_ref=target.at[part, slot],
            dst_ref=target.at[part, slot],
            send_sem=pass_sem.at[part, 0],
            recv_sem=got_sem.at[part, slot],
            device_id=(me, peer_ch),
            device_id_type=MESH,
        )

    sent = []
    locals_ = []
    for part in range(half):
        cp = pltpu.make_async_copy(
            source.at[me, part], target.at[part, ch, me], local_sem.at[part]
        )
        cp.start()
        locals_.append(cp)
        for step in range(1, group):
            peer = lax.rem(me + step, group)
            cp = pltpu.make_async_remote_copy(
                src_ref=source.at[peer, part],
                dst_ref=target.at[part, ch, me],
                send_sem=send_sem.at[part, step],
                recv_sem=recv_sem.at[part, step],
                device_id=(peer, ch),
                device_id_type=MESH,
            )
            cp.start()
            sent.append(cp)
    passed = []
    for part in range(half):
        locals_[part].wait()
        for step in range(1, group):
            origin = lax.rem(me + group - step, group)
            pltpu.make_async_remote_copy(
                src_ref=source.at[origin, part],
                dst_ref=target.at[part, ch, origin],
                send_sem=send_sem.at[part, step],
                recv_sem=recv_sem.at[part, step],
                device_id=(origin, ch),
                device_id_type=MESH,
            ).wait_recv()
        for slot, peer_ch in enumerate(across + [sibling]):
            cp = pltpu.make_async_remote_copy(
                src_ref=target.at[part, ch],
                dst_ref=target.at[part, ch],
                send_sem=pass_sem.at[part, slot],
                recv_sem=got_sem.at[part, ch],
                device_id=(me, peer_ch),
                device_id_type=MESH,
            )
            cp.start()
            passed.append(cp)
    forwarded = []
    for part in range(half):
        for hop in range(1, chans // 2):
            origin = lax.rem(ch + chans - 2 * hop, chans)
            incoming(part, origin, origin).wait_recv()
            cp = pltpu.make_async_remote_copy(
                src_ref=target.at[part, origin],
                dst_ref=target.at[part, origin],
                send_sem=fwd_sem.at[part, hop],
                recv_sem=got_sem.at[part, origin],
                device_id=(me, sibling),
                device_id_type=MESH,
            )
            cp.start()
            forwarded.append(cp)
    for cp in sent + passed + forwarded:
        cp.wait_send()
    for part in range(half):
        for hop in range(1, chans // 2):
            origin = lax.rem(sibling + chans - 2 * hop, chans)
            incoming(part, origin, origin).wait_recv()
        incoming(part, sibling, sibling).wait_recv()


def return_and_gather(block, group, chans, tag):
    half = block.shape[1]
    return pl.pallas_call(
        functools.partial(return_kernel, group, chans),
        out_shape=jax.ShapeDtypeStruct(
            (half, chans, block.shape[0]) + block.shape[2:], block.dtype
        ),
        in_specs=[pl.BlockSpec(memory_space=pl.ANY)],
        out_specs=pl.BlockSpec(memory_space=pl.ANY),
        scratch_shapes=[
            pltpu.SemaphoreType.DMA((half, group)),
            pltpu.SemaphoreType.DMA((half, group)),
            pltpu.SemaphoreType.DMA((half, chans // 2)),
            pltpu.SemaphoreType.DMA((half, chans)),
            pltpu.SemaphoreType.DMA((half, chans // 2)),
            pltpu.SemaphoreType.DMA((half,)),
        ],
        compiler_params=pltpu.CompilerParams(collective_id=tag, has_side_effects=True),
    )(block)


def contract(pattern, first_op, second_op):
    return jnp.einsum(
        pattern, first_op, second_op, precision=high, preferred_element_type=jnp.float32
    )


def tables(seq_len):
    total = 2 * seq_len
    outer = total // LANES
    half = seq_len // LANES
    k1 = np.arange(outer)[:, None]
    a1 = 2.0 * np.pi * ((k1 * np.arange(half)[None, :]) % outer) / outer
    at = 2.0 * np.pi * ((k1 * np.arange(LANES)[None, :]) % total) / total
    m2 = np.arange(LANES)
    a2 = 2.0 * np.pi * ((m2[:, None] * m2[None, :]) % LANES) / LANES
    c1, s1 = np.cos(a1), np.sin(a1)
    c2, s2 = np.cos(a2), np.sin(a2)
    f32 = lambda v: jnp.asarray(v, jnp.float32)
    return dict(
        first=f32(np.concatenate([c1, -s1], axis=0)),
        tc=f32(np.cos(at)[:, None, :]),
        ts=f32(np.sin(at)[:, None, :]),
        fwd2=f32(np.block([[c2, -s2], [s2, c2]])),
        inv2=f32(np.block([[c2, s2], [-s2, c2]])),
        last=f32(np.concatenate([c1.T, -s1.T], axis=1) / total),
    )


def forward(signal, tb):
    outer = tb["tc"].shape[0]
    both = contract("kn,ncm->kcm", tb["first"], signal)
    br, bi = both[:outer], both[outer:]
    tr, ti = tb["tc"], -tb["ts"]
    twisted = jnp.concatenate([br * tr - bi * ti, br * ti + bi * tr], axis=2)
    return contract("kcm,mj->kcj", twisted, tb["fwd2"])


def inverse(spectrum, tb):
    z = contract("kcj,jm->kcm", spectrum, tb["inv2"])
    zr, zi = z[:, :, :LANES], z[:, :, LANES:]
    tc, ts = tb["tc"], tb["ts"]
    stacked = jnp.concatenate([zr * tc - zi * ts, zr * ts + zi * tc], axis=0)
    return contract("nk,kcm->ncm", tb["last"], stacked)


def long_conv(mixed_in, long_filter):
    half = mixed_in.shape[0]
    tb = tables(half * LANES)
    width = mixed_in.shape[1]
    both = forward(jnp.concatenate([mixed_in, long_filter], axis=1), tb)
    xs, hs = both[:, :width], both[:, width:]
    xr, xi = xs[:, :, :LANES], xs[:, :, LANES:]
    hr, hi = hs[:, :, :LANES], hs[:, :, LANES:]
    product = jnp.concatenate([xr * hr - xi * hi, xr * hi + xi * hr], axis=2)
    return inverse(product, tb)


def shift_seq(signal, distance):
    rows, width, lanes = signal.shape
    prev = jnp.concatenate([jnp.zeros((1, width, lanes), signal.dtype), signal[:-1]], axis=0)
    return jnp.concatenate(
        [prev[:, :, lanes - distance :], signal[:, :, : lanes - distance]], axis=2
    )


def short_conv(signal, taps):
    summed = taps[0][None, :, None] * signal
    for offset in range(1, taps.shape[0]):
        summed = summed + taps[offset][None, :, None] * shift_seq(signal, offset)
    return summed


def to_ncm(block):
    rows, width = block.shape
    return block.reshape(rows // LANES, LANES, width).transpose(0, 2, 1)


def on_device(out_gate, in_gate, values, short_filter, long_filter, skip_gain, out_weight):
    seq_count = lax.axis_size("seq")
    seq_index = lax.axis_index("seq")
    rows = out_gate.shape[0]
    width = out_gate.shape[1] // seq_count
    half = rows // LANES

    planes = [out_gate, in_gate, values, long_filter.astype(jnp.bfloat16)]
    stacked = jnp.stack([to_ncm(plane) for plane in planes])
    spread = exchange(stacked, seq_count, 0)
    start = seq_index * width
    taps = lax.dynamic_slice_in_dim(short_filter, start, width, axis=2)
    gain = lax.dynamic_slice_in_dim(skip_gain, start, width, axis=0)
    spread = spread.astype(jnp.float32)
    gate_late = short_conv(spread[0], taps[0])
    mixed_in = short_conv(spread[1], taps[1]) * short_conv(spread[2], taps[2])
    long_out = long_conv(mixed_in, spread[3])
    filtered = long_out + gain[None, :, None] * mixed_in
    mixed = (gate_late * filtered).astype(jnp.bfloat16)
    chans = lax.axis_size("ch")
    gathered = return_and_gather(mixed.reshape(seq_count, half, width, LANES), seq_count, chans, 1)
    gathered = gathered.reshape(half, chans * seq_count * width, LANES)
    summed = jnp.einsum(
        "ncm,co->nmo", gathered, out_weight, preferred_element_type=jnp.float32
    )
    return summed.reshape(rows, -1).astype(jnp.bfloat16)


def solution(mesh):
    return jax.shard_map(
        on_device,
        mesh=mesh,
        in_specs=(
            P("seq", "ch"),
            P("seq", "ch"),
            P("seq", "ch"),
            P(None, None, "ch"),
            P("seq", "ch"),
            P("ch"),
            P(None, "ch"),
        ),
        out_specs=P("seq", "ch"),
        check_vma=False,
    )
```

```python
import functools

import jax
import jax.numpy as jnp
import numpy as np
from jax import lax
from jax.experimental import pallas as pl
from jax.experimental.pallas import tpu as pltpu
from jax.sharding import PartitionSpec as P

high = lax.Precision.HIGH
LANES = 128
MESH = pl.DeviceIdType.MESH


def peer_offsets(group, inner=8):
    if group % inner:
        inner = group
    outer = group // inner
    dist = lambda d, n: min(d, n - d)
    seen, order = set(), []
    cands = [(dx, dz) for dx in range(outer) for dz in range(inner) if dx or dz]
    cands.sort(key=lambda o: (-(dist(o[0], outer) + dist(o[1], inner)), o))
    for dx, dz in cands:
        for off in ((dx, dz), ((outer - dx) % outer, (inner - dz) % inner)):
            if off not in seen:
                seen.add(off)
                order.append(off)
    return inner, order


def shifted_peer(me, off, inner, group, sign):
    outer = group // inner
    x, z = me // inner, lax.rem(me, inner)
    dx, dz = off
    return lax.rem(x + sign * dx + outer, outer) * inner + lax.rem(z + sign * dz + inner, inner)


def exchange_kernel(group, source, target, send_sem, recv_sem, local_sem):
    me = lax.axis_index("seq")
    ch = lax.axis_index("ch")
    half = source.shape[1]
    width = target.shape[2]
    barrier = pltpu.get_barrier_semaphore()
    for step in range(1, group):
        peer = lax.rem(me + step, group)
        pl.semaphore_signal(barrier, inc=1, device_id=(peer, ch), device_id_type=MESH)
    pl.semaphore_wait(barrier, group - 1)

    def piece(ref_src, peer, origin):
        return (
            ref_src.at[:, :, pl.ds(peer * width, width)],
            target.at[:, pl.ds(origin * half, half)],
        )

    src, dst = piece(source, me, me)
    local = pltpu.make_async_copy(src, dst, local_sem.at[0])
    local.start()
    inner, offsets = peer_offsets(group)
    sent = []
    for step, off in enumerate(offsets, start=1):
        peer = shifted_peer(me, off, inner, group, 1)
        src, dst = piece(source, peer, me)
        cp = pltpu.make_async_remote_copy(
            src_ref=src,
            dst_ref=dst,
            send_sem=send_sem.at[step],
            recv_sem=recv_sem.at[step],
            device_id=(peer, ch),
            device_id_type=MESH,
        )
        cp.start()
        sent.append(cp)
    local.wait()
    for cp in sent:
        cp.wait_send()
    for step, off in enumerate(offsets, start=1):
        origin = shifted_peer(me, off, inner, group, -1)
        src, dst = piece(source, me, origin)
        pltpu.make_async_remote_copy(
            src_ref=src,
            dst_ref=dst,
            send_sem=send_sem.at[step],
            recv_sem=recv_sem.at[step],
            device_id=(origin, ch),
            device_id_type=MESH,
        ).wait_recv()


def exchange(stacked, group, tag):
    planes, half, full, lanes = stacked.shape
    return pl.pallas_call(
        functools.partial(exchange_kernel, group),
        out_shape=jax.ShapeDtypeStruct((planes, group * half, full // group, lanes), stacked.dtype),
        in_specs=[pl.BlockSpec(memory_space=pl.ANY)],
        out_specs=pl.BlockSpec(memory_space=pl.ANY),
        scratch_shapes=[
            pltpu.SemaphoreType.DMA((group,)),
            pltpu.SemaphoreType.DMA((group,)),
            pltpu.SemaphoreType.DMA((1,)),
        ],
        compiler_params=pltpu.CompilerParams(collective_id=tag, has_side_effects=True),
    )(stacked)


def return_kernel(group, chans, source, target, send_sem, recv_sem, pass_sem, got_sem, fwd_sem, local_sem):
    me = lax.axis_index("seq")
    ch = lax.axis_index("ch")
    half = source.shape[1]
    sibling = ch + 1 - 2 * lax.rem(ch, 2)
    across = [lax.rem(ch + 2 * hop, chans) for hop in range(1, chans // 2)]
    barrier = pltpu.get_barrier_semaphore()
    for step in range(1, group):
        peer = lax.rem(me + step, group)
        pl.semaphore_signal(barrier, inc=1, device_id=(peer, ch), device_id_type=MESH)
    for peer_ch in across + [sibling]:
        pl.semaphore_signal(barrier, inc=1, device_id=(me, peer_ch), device_id_type=MESH)
    pl.semaphore_wait(barrier, group - 1 + len(across) + 1)

    def incoming(part, slot, peer_ch):
        return pltpu.make_async_remote_copy(
            src_ref=target.at[part, slot],
            dst_ref=target.at[part, slot],
            send_sem=pass_sem.at[part, 0],
            recv_sem=got_sem.at[part, slot],
            device_id=(me, peer_ch),
            device_id_type=MESH,
        )

    inner, offsets = peer_offsets(group)
    sent = []
    locals_ = []
    for part in range(half):
        cp = pltpu.make_async_copy(
            source.at[me, part], target.at[part, ch, me], local_sem.at[part]
        )
        cp.start()
        locals_.append(cp)
        for step, off in enumerate(offsets, start=1):
            peer = shifted_peer(me, off, inner, group, 1)
            cp = pltpu.make_async_remote_copy(
                src_ref=source.at[peer, part],
                dst_ref=target.at[part, ch, me],
                send_sem=send_sem.at[part, step],
                recv_sem=recv_sem.at[part, step],
                device_id=(peer, ch),
                device_id_type=MESH,
            )
            cp.start()
            sent.append(cp)
    passed = []
    for part in range(half):
        locals_[part].wait()
        for step, off in enumerate(offsets, start=1):
            origin = shifted_peer(me, off, inner, group, -1)
            pltpu.make_async_remote_copy(
                src_ref=source.at[origin, part],
                dst_ref=target.at[part, ch, origin],
                send_sem=send_sem.at[part, step],
                recv_sem=recv_sem.at[part, step],
                device_id=(origin, ch),
                device_id_type=MESH,
            ).wait_recv()
        for slot, peer_ch in enumerate(across + [sibling]):
            cp = pltpu.make_async_remote_copy(
                src_ref=target.at[part, ch],
                dst_ref=target.at[part, ch],
                send_sem=pass_sem.at[part, slot],
                recv_sem=got_sem.at[part, ch],
                device_id=(me, peer_ch),
                device_id_type=MESH,
            )
            cp.start()
            passed.append(cp)
    forwarded = []
    for part in range(half):
        for hop in range(1, chans // 2):
            origin = lax.rem(ch + chans - 2 * hop, chans)
            incoming(part, origin, origin).wait_recv()
            cp = pltpu.make_async_remote_copy(
                src_ref=target.at[part, origin],
                dst_ref=target.at[part, origin],
                send_sem=fwd_sem.at[part, hop],
                recv_sem=got_sem.at[part, origin],
                device_id=(me, sibling),
                device_id_type=MESH,
            )
            cp.start()
            forwarded.append(cp)
    for cp in sent + passed + forwarded:
        cp.wait_send()
    for part in range(half):
        for hop in range(1, chans // 2):
            origin = lax.rem(sibling + chans - 2 * hop, chans)
            incoming(part, origin, origin).wait_recv()
        incoming(part, sibling, sibling).wait_recv()


def return_and_gather(block, group, chans, tag):
    half = block.shape[1]
    return pl.pallas_call(
        functools.partial(return_kernel, group, chans),
        out_shape=jax.ShapeDtypeStruct(
            (half, chans, block.shape[0]) + block.shape[2:], block.dtype
        ),
        in_specs=[pl.BlockSpec(memory_space=pl.ANY)],
        out_specs=pl.BlockSpec(memory_space=pl.ANY),
        scratch_shapes=[
            pltpu.SemaphoreType.DMA((half, group)),
            pltpu.SemaphoreType.DMA((half, group)),
            pltpu.SemaphoreType.DMA((half, chans // 2)),
            pltpu.SemaphoreType.DMA((half, chans)),
            pltpu.SemaphoreType.DMA((half, chans // 2)),
            pltpu.SemaphoreType.DMA((half,)),
        ],
        compiler_params=pltpu.CompilerParams(collective_id=tag, has_side_effects=True),
    )(block)


def contract(pattern, first_op, second_op):
    return jnp.einsum(
        pattern, first_op, second_op, precision=high, preferred_element_type=jnp.float32
    )


def tables(seq_len):
    total = 2 * seq_len
    outer = total // LANES
    half = seq_len // LANES
    k1 = np.arange(outer)[:, None]
    a1 = 2.0 * np.pi * ((k1 * np.arange(half)[None, :]) % outer) / outer
    at = 2.0 * np.pi * ((k1 * np.arange(LANES)[None, :]) % total) / total
    m2 = np.arange(LANES)
    a2 = 2.0 * np.pi * ((m2[:, None] * m2[None, :]) % LANES) / LANES
    c1, s1 = np.cos(a1), np.sin(a1)
    c2, s2 = np.cos(a2), np.sin(a2)
    f32 = lambda v: jnp.asarray(v, jnp.float32)
    return dict(
        first=f32(np.concatenate([c1, -s1], axis=0)),
        tc=f32(np.cos(at)[:, None, :]),
        ts=f32(np.sin(at)[:, None, :]),
        fwd2=f32(np.block([[c2, -s2], [s2, c2]])),
        inv2=f32(np.block([[c2, s2], [-s2, c2]])),
        last=f32(np.concatenate([c1.T, -s1.T], axis=1) / total),
    )


def forward(signal, tb):
    outer = tb["tc"].shape[0]
    both = contract("kn,ncm->kcm", tb["first"], signal)
    br, bi = both[:outer], both[outer:]
    tr, ti = tb["tc"], -tb["ts"]
    twisted = jnp.concatenate([br * tr - bi * ti, br * ti + bi * tr], axis=2)
    return contract("kcm,mj->kcj", twisted, tb["fwd2"])


def inverse(spectrum, tb):
    z = contract("kcj,jm->kcm", spectrum, tb["inv2"])
    zr, zi = z[:, :, :LANES], z[:, :, LANES:]
    tc, ts = tb["tc"], tb["ts"]
    stacked = jnp.concatenate([zr * tc - zi * ts, zr * ts + zi * tc], axis=0)
    return contract("nk,kcm->ncm", tb["last"], stacked)


def long_conv(mixed_in, long_filter):
    half = mixed_in.shape[0]
    tb = tables(half * LANES)
    width = mixed_in.shape[1]
    both = forward(jnp.concatenate([mixed_in, long_filter], axis=1), tb)
    xs, hs = both[:, :width], both[:, width:]
    xr, xi = xs[:, :, :LANES], xs[:, :, LANES:]
    hr, hi = hs[:, :, :LANES], hs[:, :, LANES:]
    product = jnp.concatenate([xr * hr - xi * hi, xr * hi + xi * hr], axis=2)
    return inverse(product, tb)


def shift_seq(signal, distance):
    rows, width, lanes = signal.shape
    prev = jnp.concatenate([jnp.zeros((1, width, lanes), signal.dtype), signal[:-1]], axis=0)
    return jnp.concatenate(
        [prev[:, :, lanes - distance :], signal[:, :, : lanes - distance]], axis=2
    )


def short_conv(signal, taps):
    summed = taps[0][None, :, None] * signal
    for offset in range(1, taps.shape[0]):
        summed = summed + taps[offset][None, :, None] * shift_seq(signal, offset)
    return summed


def to_ncm(block):
    rows, width = block.shape
    return block.reshape(rows // LANES, LANES, width).transpose(0, 2, 1)


def on_device(out_gate, in_gate, values, short_filter, long_filter, skip_gain, out_weight):
    seq_count = lax.axis_size("seq")
    seq_index = lax.axis_index("seq")
    rows = out_gate.shape[0]
    width = out_gate.shape[1] // seq_count
    half = rows // LANES

    planes = [out_gate, in_gate, values, long_filter.astype(jnp.bfloat16)]
    stacked = jnp.stack([to_ncm(plane) for plane in planes])
    spread = exchange(stacked, seq_count, 0)
    start = seq_index * width
    taps = lax.dynamic_slice_in_dim(short_filter, start, width, axis=2)
    gain = lax.dynamic_slice_in_dim(skip_gain, start, width, axis=0)
    spread = spread.astype(jnp.float32)
    gate_late = short_conv(spread[0], taps[0])
    mixed_in = short_conv(spread[1], taps[1]) * short_conv(spread[2], taps[2])
    long_out = long_conv(mixed_in, spread[3])
    filtered = long_out + gain[None, :, None] * mixed_in
    mixed = (gate_late * filtered).astype(jnp.bfloat16)
    chans = lax.axis_size("ch")
    gathered = return_and_gather(mixed.reshape(seq_count, half, width, LANES), seq_count, chans, 1)
    gathered = gathered.reshape(half, chans * seq_count * width, LANES)
    summed = jnp.einsum(
        "ncm,co->nmo", gathered, out_weight, preferred_element_type=jnp.float32
    )
    return summed.reshape(rows, -1).astype(jnp.bfloat16)


def solution(mesh):
    return jax.shard_map(
        on_device,
        mesh=mesh,
        in_specs=(
            P("seq", "ch"),
            P("seq", "ch"),
            P("seq", "ch"),
            P(None, None, "ch"),
            P("seq", "ch"),
            P("ch"),
            P(None, "ch"),
        ),
        out_specs=P("seq", "ch"),
        check_vma=False,
    )
```

```python
import functools

import jax
import jax.numpy as jnp
import numpy as np
from jax import lax
from jax.experimental import pallas as pl
from jax.experimental.pallas import tpu as pltpu
from jax.sharding import PartitionSpec as P

high = lax.Precision.HIGH
LANES = 128
MESH = pl.DeviceIdType.MESH


def peer_offsets(group, inner=8):
    if group % inner:
        inner = group
    outer = group // inner
    dist = lambda d, n: min(d, n - d)
    seen, order = set(), []
    cands = [(dx, dz) for dx in range(outer) for dz in range(inner) if dx or dz]
    cands.sort(key=lambda o: (-(dist(o[0], outer) + dist(o[1], inner)), o))
    for dx, dz in cands:
        for off in ((dx, dz), ((outer - dx) % outer, (inner - dz) % inner)):
            if off not in seen:
                seen.add(off)
                order.append(off)
    return inner, order


def shifted_peer(me, off, inner, group, sign):
    outer = group // inner
    x, z = me // inner, lax.rem(me, inner)
    dx, dz = off
    return lax.rem(x + sign * dx + outer, outer) * inner + lax.rem(z + sign * dz + inner, inner)


def exchange_kernel(group, source, target, send_sem, recv_sem, local_sem):
    me = lax.axis_index("seq")
    ch = lax.axis_index("ch")
    half = source.shape[1]
    width = target.shape[2]
    barrier = pltpu.get_barrier_semaphore()
    for step in range(1, group):
        peer = lax.rem(me + step, group)
        pl.semaphore_signal(barrier, inc=1, device_id=(peer, ch), device_id_type=MESH)
    pl.semaphore_wait(barrier, group - 1)

    def piece(ref_src, peer, origin):
        return (
            ref_src.at[:, :, pl.ds(peer * width, width)],
            target.at[:, pl.ds(origin * half, half)],
        )

    src, dst = piece(source, me, me)
    local = pltpu.make_async_copy(src, dst, local_sem.at[0])
    local.start()
    inner, offsets = peer_offsets(group)
    sent = []
    for step, off in enumerate(offsets, start=1):
        peer = shifted_peer(me, off, inner, group, 1)
        src, dst = piece(source, peer, me)
        cp = pltpu.make_async_remote_copy(
            src_ref=src,
            dst_ref=dst,
            send_sem=send_sem.at[step],
            recv_sem=recv_sem.at[step],
            device_id=(peer, ch),
            device_id_type=MESH,
        )
        cp.start()
        sent.append(cp)
    local.wait()
    for cp in sent:
        cp.wait_send()
    for step, off in enumerate(offsets, start=1):
        origin = shifted_peer(me, off, inner, group, -1)
        src, dst = piece(source, me, origin)
        pltpu.make_async_remote_copy(
            src_ref=src,
            dst_ref=dst,
            send_sem=send_sem.at[step],
            recv_sem=recv_sem.at[step],
            device_id=(origin, ch),
            device_id_type=MESH,
        ).wait_recv()


def exchange(stacked, group, tag):
    planes, half, full, lanes = stacked.shape
    return pl.pallas_call(
        functools.partial(exchange_kernel, group),
        out_shape=jax.ShapeDtypeStruct((planes, group * half, full // group, lanes), stacked.dtype),
        in_specs=[pl.BlockSpec(memory_space=pl.ANY)],
        out_specs=pl.BlockSpec(memory_space=pl.ANY),
        scratch_shapes=[
            pltpu.SemaphoreType.DMA((group,)),
            pltpu.SemaphoreType.DMA((group,)),
            pltpu.SemaphoreType.DMA((1,)),
        ],
        compiler_params=pltpu.CompilerParams(collective_id=tag, has_side_effects=True),
    )(stacked)


def return_kernel(group, chans, source, target, send_sem, recv_sem, pass_sem, got_sem, fwd_sem, local_sem):
    me = lax.axis_index("seq")
    ch = lax.axis_index("ch")
    half = source.shape[1]
    sibling = ch + 1 - 2 * lax.rem(ch, 2)
    across = [lax.rem(ch + 2 * hop, chans) for hop in range(1, chans // 2)]
    barrier = pltpu.get_barrier_semaphore()
    for step in range(1, group):
        peer = lax.rem(me + step, group)
        pl.semaphore_signal(barrier, inc=1, device_id=(peer, ch), device_id_type=MESH)
    for peer_ch in across + [sibling]:
        pl.semaphore_signal(barrier, inc=1, device_id=(me, peer_ch), device_id_type=MESH)
    pl.semaphore_wait(barrier, group - 1 + len(across) + 1)

    def incoming(part, slot, peer_ch):
        return pltpu.make_async_remote_copy(
            src_ref=target.at[part, slot],
            dst_ref=target.at[part, slot],
            send_sem=pass_sem.at[part, 0],
            recv_sem=got_sem.at[part, slot],
            device_id=(me, peer_ch),
            device_id_type=MESH,
        )

    inner, offsets = peer_offsets(group)
    sent = []
    locals_ = []
    for part in range(half):
        cp = pltpu.make_async_copy(
            source.at[me, part], target.at[part, ch, me], local_sem.at[part]
        )
        cp.start()
        locals_.append(cp)
        for step, off in enumerate(offsets, start=1):
            peer = shifted_peer(me, off, inner, group, 1)
            cp = pltpu.make_async_remote_copy(
                src_ref=source.at[peer, part],
                dst_ref=target.at[part, ch, me],
                send_sem=send_sem.at[part, step],
                recv_sem=recv_sem.at[part, step],
                device_id=(peer, ch),
                device_id_type=MESH,
            )
            cp.start()
            sent.append(cp)
    passed = []
    for part in range(half):
        locals_[part].wait()
        for step, off in enumerate(offsets, start=1):
            origin = shifted_peer(me, off, inner, group, -1)
            pltpu.make_async_remote_copy(
                src_ref=source.at[origin, part],
                dst_ref=target.at[part, ch, origin],
                send_sem=send_sem.at[part, step],
                recv_sem=recv_sem.at[part, step],
                device_id=(origin, ch),
                device_id_type=MESH,
            ).wait_recv()
        for slot, peer_ch in enumerate(across + [sibling]):
            cp = pltpu.make_async_remote_copy(
                src_ref=target.at[part, ch],
                dst_ref=target.at[part, ch],
                send_sem=pass_sem.at[part, slot],
                recv_sem=got_sem.at[part, ch],
                device_id=(me, peer_ch),
                device_id_type=MESH,
            )
            cp.start()
            passed.append(cp)
    forwarded = []
    for part in range(half):
        for hop in range(1, chans // 2):
            origin = lax.rem(ch + chans - 2 * hop, chans)
            incoming(part, origin, origin).wait_recv()
            cp = pltpu.make_async_remote_copy(
                src_ref=target.at[part, origin],
                dst_ref=target.at[part, origin],
                send_sem=fwd_sem.at[part, hop],
                recv_sem=got_sem.at[part, origin],
                device_id=(me, sibling),
                device_id_type=MESH,
            )
            cp.start()
            forwarded.append(cp)
    for cp in sent + passed + forwarded:
        cp.wait_send()
    for part in range(half):
        for hop in range(1, chans // 2):
            origin = lax.rem(sibling + chans - 2 * hop, chans)
            incoming(part, origin, origin).wait_recv()
        incoming(part, sibling, sibling).wait_recv()


def return_and_gather(block, group, chans, tag):
    half = block.shape[1]
    return pl.pallas_call(
        functools.partial(return_kernel, group, chans),
        out_shape=jax.ShapeDtypeStruct(
            (half, chans, block.shape[0]) + block.shape[2:], block.dtype
        ),
        in_specs=[pl.BlockSpec(memory_space=pl.ANY)],
        out_specs=pl.BlockSpec(memory_space=pl.ANY),
        scratch_shapes=[
            pltpu.SemaphoreType.DMA((half, group)),
            pltpu.SemaphoreType.DMA((half, group)),
            pltpu.SemaphoreType.DMA((half, chans // 2)),
            pltpu.SemaphoreType.DMA((half, chans)),
            pltpu.SemaphoreType.DMA((half, chans // 2)),
            pltpu.SemaphoreType.DMA((half,)),
        ],
        compiler_params=pltpu.CompilerParams(collective_id=tag, has_side_effects=True),
    )(block)


def contract(pattern, first_op, second_op):
    return jnp.einsum(
        pattern, first_op, second_op, precision=high, preferred_element_type=jnp.float32
    )


def tables(seq_len):
    total = 2 * seq_len
    outer = total // LANES
    half = seq_len // LANES
    k1 = np.arange(outer)[:, None]
    a1 = 2.0 * np.pi * ((k1 * np.arange(half)[None, :]) % outer) / outer
    at = 2.0 * np.pi * ((k1 * np.arange(LANES)[None, :]) % total) / total
    m2 = np.arange(LANES)
    a2 = 2.0 * np.pi * ((m2[:, None] * m2[None, :]) % LANES) / LANES
    c1, s1 = np.cos(a1), np.sin(a1)
    c2, s2 = np.cos(a2), np.sin(a2)
    f32 = lambda v: jnp.asarray(v, jnp.float32)
    return dict(
        first=f32(np.concatenate([c1, -s1], axis=0)),
        tc=f32(np.cos(at)[:, None, :]),
        ts=f32(np.sin(at)[:, None, :]),
        fwd2=f32(np.block([[c2, -s2], [s2, c2]])),
        inv2=f32(np.block([[c2, s2], [-s2, c2]])),
        last=f32(np.concatenate([c1.T, -s1.T], axis=1) / total),
    )


def forward(signal, tb):
    outer = tb["tc"].shape[0]
    both = contract("kn,ncm->kcm", tb["first"], signal)
    br, bi = both[:outer], both[outer:]
    tr, ti = tb["tc"], -tb["ts"]
    twisted = jnp.concatenate([br * tr - bi * ti, br * ti + bi * tr], axis=2)
    return contract("kcm,mj->kcj", twisted, tb["fwd2"])


def inverse(spectrum, tb):
    z = contract("kcj,jm->kcm", spectrum, tb["inv2"])
    zr, zi = z[:, :, :LANES], z[:, :, LANES:]
    tc, ts = tb["tc"], tb["ts"]
    stacked = jnp.concatenate([zr * tc - zi * ts, zr * ts + zi * tc], axis=0)
    return contract("nk,kcm->ncm", tb["last"], stacked)


def long_conv(mixed_in, long_filter):
    half = mixed_in.shape[0]
    tb = tables(half * LANES)
    width = mixed_in.shape[1]
    both = forward(jnp.concatenate([mixed_in, long_filter], axis=1), tb)
    xs, hs = both[:, :width], both[:, width:]
    xr, xi = xs[:, :, :LANES], xs[:, :, LANES:]
    hr, hi = hs[:, :, :LANES], hs[:, :, LANES:]
    product = jnp.concatenate([xr * hr - xi * hi, xr * hi + xi * hr], axis=2)
    return inverse(product, tb)


def shift_seq(signal, distance):
    rows, width, lanes = signal.shape
    prev = jnp.concatenate([jnp.zeros((1, width, lanes), signal.dtype), signal[:-1]], axis=0)
    return jnp.concatenate(
        [prev[:, :, lanes - distance :], signal[:, :, : lanes - distance]], axis=2
    )


def short_conv(signal, taps):
    summed = taps[0][None, :, None] * signal
    for offset in range(1, taps.shape[0]):
        summed = summed + taps[offset][None, :, None] * shift_seq(signal, offset)
    return summed


def to_ncm(block):
    rows, width = block.shape
    return block.reshape(rows // LANES, LANES, width).transpose(0, 2, 1)


def on_device(out_gate, in_gate, values, short_filter, long_filter, skip_gain, out_weight):
    seq_count = lax.axis_size("seq")
    seq_index = lax.axis_index("seq")
    rows = out_gate.shape[0]
    width = out_gate.shape[1] // seq_count
    half = rows // LANES

    planes = [out_gate, in_gate, values, long_filter.astype(jnp.bfloat16)]
    stacked = jnp.stack([to_ncm(plane) for plane in planes])
    spread = exchange(stacked, seq_count, 0)
    start = seq_index * width
    taps = lax.dynamic_slice_in_dim(short_filter, start, width, axis=2)
    gain = lax.dynamic_slice_in_dim(skip_gain, start, width, axis=0)
    spread = spread.astype(jnp.float32)
    gate_late = short_conv(spread[0], taps[0])
    mixed_in = short_conv(spread[1], taps[1]) * short_conv(spread[2], taps[2])
    long_out = long_conv(mixed_in, spread[3])
    filtered = long_out + gain[None, :, None] * mixed_in
    mixed = (gate_late * filtered).astype(jnp.bfloat16)
    chans = lax.axis_size("ch")
    gathered = return_and_gather(mixed.reshape(seq_count, half, width, LANES), seq_count, chans, 1)
    gathered = gathered.reshape(half, chans * seq_count * width, LANES)
    summed = jnp.einsum(
        "co,ncm->nom", out_weight, gathered, preferred_element_type=jnp.float32
    )
    return summed.astype(jnp.bfloat16).transpose(0, 2, 1).reshape(rows, -1)


def solution(mesh):
    return jax.shard_map(
        on_device,
        mesh=mesh,
        in_specs=(
            P("seq", "ch"),
            P("seq", "ch"),
            P("seq", "ch"),
            P(None, None, "ch"),
            P("seq", "ch"),
            P("ch"),
            P(None, "ch"),
        ),
        out_specs=P("seq", "ch"),
        check_vma=False,
    )
```

```python
import functools

import jax
import jax.numpy as jnp
import numpy as np
from jax import lax
from jax.experimental import pallas as pl
from jax.experimental.pallas import tpu as pltpu
from jax.sharding import PartitionSpec as P

high = lax.Precision.HIGH
LANES = 128
MESH = pl.DeviceIdType.MESH


def peer_offsets(group, inner=8):
    if group % inner:
        inner = group
    outer = group // inner
    dist = lambda d, n: min(d, n - d)
    seen, order = set(), []
    cands = [(dx, dz) for dx in range(outer) for dz in range(inner) if dx or dz]
    cands.sort(key=lambda o: (-(dist(o[0], outer) + dist(o[1], inner)), o))
    for dx, dz in cands:
        for off in ((dx, dz), ((outer - dx) % outer, (inner - dz) % inner)):
            if off not in seen:
                seen.add(off)
                order.append(off)
    return inner, order


def shifted_peer(me, off, inner, group, sign):
    outer = group // inner
    x, z = me // inner, lax.rem(me, inner)
    dx, dz = off
    return lax.rem(x + sign * dx + outer, outer) * inner + lax.rem(z + sign * dz + inner, inner)


def exchange_kernel(group, count, *refs):
    sources, target = refs[:count], refs[count]
    send_sem, recv_sem, local_sem = refs[count + 1 :]
    me = lax.axis_index("seq")
    ch = lax.axis_index("ch")
    half = sources[0].shape[0]
    width = target.shape[2]
    barrier = pltpu.get_barrier_semaphore()
    for step in range(1, group):
        peer = lax.rem(me + step, group)
        pl.semaphore_signal(barrier, inc=1, device_id=(peer, ch), device_id_type=MESH)
    pl.semaphore_wait(barrier, group - 1)

    def piece(plane, peer, origin):
        return (
            sources[plane].at[:, pl.ds(peer * width, width)],
            target.at[plane, pl.ds(origin * half, half)],
        )

    locals_ = []
    for plane in range(count):
        src, dst = piece(plane, me, me)
        cp = pltpu.make_async_copy(src, dst, local_sem.at[plane])
        cp.start()
        locals_.append(cp)
    inner, offsets = peer_offsets(group)
    sent = []
    for step, off in enumerate(offsets, start=1):
        peer = shifted_peer(me, off, inner, group, 1)
        for plane in range(count):
            src, dst = piece(plane, peer, me)
            cp = pltpu.make_async_remote_copy(
                src_ref=src,
                dst_ref=dst,
                send_sem=send_sem.at[plane, step],
                recv_sem=recv_sem.at[plane, step],
                device_id=(peer, ch),
                device_id_type=MESH,
            )
            cp.start()
            sent.append(cp)
    for cp in locals_:
        cp.wait()
    for cp in sent:
        cp.wait_send()
    for step, off in enumerate(offsets, start=1):
        origin = shifted_peer(me, off, inner, group, -1)
        for plane in range(count):
            src, dst = piece(plane, me, origin)
            pltpu.make_async_remote_copy(
                src_ref=src,
                dst_ref=dst,
                send_sem=send_sem.at[plane, step],
                recv_sem=recv_sem.at[plane, step],
                device_id=(origin, ch),
                device_id_type=MESH,
            ).wait_recv()


def exchange(planes, group, tag):
    count = len(planes)
    half, full, lanes = planes[0].shape
    return pl.pallas_call(
        functools.partial(exchange_kernel, group, count),
        out_shape=jax.ShapeDtypeStruct(
            (count, group * half, full // group, lanes), planes[0].dtype
        ),
        in_specs=[pl.BlockSpec(memory_space=pl.ANY)] * count,
        out_specs=pl.BlockSpec(memory_space=pl.ANY),
        scratch_shapes=[
            pltpu.SemaphoreType.DMA((count, group)),
            pltpu.SemaphoreType.DMA((count, group)),
            pltpu.SemaphoreType.DMA((count,)),
        ],
        compiler_params=pltpu.CompilerParams(collective_id=tag, has_side_effects=True),
    )(*planes)


def return_kernel(group, chans, source, target, send_sem, recv_sem, pass_sem, got_sem, fwd_sem, local_sem):
    me = lax.axis_index("seq")
    ch = lax.axis_index("ch")
    half = source.shape[1]
    sibling = ch + 1 - 2 * lax.rem(ch, 2)
    across = [lax.rem(ch + 2 * hop, chans) for hop in range(1, chans // 2)]
    barrier = pltpu.get_barrier_semaphore()
    for step in range(1, group):
        peer = lax.rem(me + step, group)
        pl.semaphore_signal(barrier, inc=1, device_id=(peer, ch), device_id_type=MESH)
    for peer_ch in across + [sibling]:
        pl.semaphore_signal(barrier, inc=1, device_id=(me, peer_ch), device_id_type=MESH)
    pl.semaphore_wait(barrier, group - 1 + len(across) + 1)

    def incoming(part, slot, peer_ch):
        return pltpu.make_async_remote_copy(
            src_ref=target.at[part, slot],
            dst_ref=target.at[part, slot],
            send_sem=pass_sem.at[part, 0],
            recv_sem=got_sem.at[part, slot],
            device_id=(me, peer_ch),
            device_id_type=MESH,
        )

    inner, offsets = peer_offsets(group)
    sent = []
    locals_ = []
    for part in range(half):
        cp = pltpu.make_async_copy(
            source.at[me, part], target.at[part, ch, me], local_sem.at[part]
        )
        cp.start()
        locals_.append(cp)
        for step, off in enumerate(offsets, start=1):
            peer = shifted_peer(me, off, inner, group, 1)
            cp = pltpu.make_async_remote_copy(
                src_ref=source.at[peer, part],
                dst_ref=target.at[part, ch, me],
                send_sem=send_sem.at[part, step],
                recv_sem=recv_sem.at[part, step],
                device_id=(peer, ch),
                device_id_type=MESH,
            )
            cp.start()
            sent.append(cp)
    passed = []
    for part in range(half):
        locals_[part].wait()
        for step, off in enumerate(offsets, start=1):
            origin = shifted_peer(me, off, inner, group, -1)
            pltpu.make_async_remote_copy(
                src_ref=source.at[origin, part],
                dst_ref=target.at[part, ch, origin],
                send_sem=send_sem.at[part, step],
                recv_sem=recv_sem.at[part, step],
                device_id=(origin, ch),
                device_id_type=MESH,
            ).wait_recv()
        for slot, peer_ch in enumerate(across + [sibling]):
            cp = pltpu.make_async_remote_copy(
                src_ref=target.at[part, ch],
                dst_ref=target.at[part, ch],
                send_sem=pass_sem.at[part, slot],
                recv_sem=got_sem.at[part, ch],
                device_id=(me, peer_ch),
                device_id_type=MESH,
            )
            cp.start()
            passed.append(cp)
    forwarded = []
    for part in range(half):
        for hop in range(1, chans // 2):
            origin = lax.rem(ch + chans - 2 * hop, chans)
            incoming(part, origin, origin).wait_recv()
            cp = pltpu.make_async_remote_copy(
                src_ref=target.at[part, origin],
                dst_ref=target.at[part, origin],
                send_sem=fwd_sem.at[part, hop],
                recv_sem=got_sem.at[part, origin],
                device_id=(me, sibling),
                device_id_type=MESH,
            )
            cp.start()
            forwarded.append(cp)
    for cp in sent + passed + forwarded:
        cp.wait_send()
    for part in range(half):
        for hop in range(1, chans // 2):
            origin = lax.rem(sibling + chans - 2 * hop, chans)
            incoming(part, origin, origin).wait_recv()
        incoming(part, sibling, sibling).wait_recv()


def return_and_gather(block, group, chans, tag):
    half = block.shape[1]
    return pl.pallas_call(
        functools.partial(return_kernel, group, chans),
        out_shape=jax.ShapeDtypeStruct(
            (half, chans, block.shape[0]) + block.shape[2:], block.dtype
        ),
        in_specs=[pl.BlockSpec(memory_space=pl.ANY)],
        out_specs=pl.BlockSpec(memory_space=pl.ANY),
        scratch_shapes=[
            pltpu.SemaphoreType.DMA((half, group)),
            pltpu.SemaphoreType.DMA((half, group)),
            pltpu.SemaphoreType.DMA((half, chans // 2)),
            pltpu.SemaphoreType.DMA((half, chans)),
            pltpu.SemaphoreType.DMA((half, chans // 2)),
            pltpu.SemaphoreType.DMA((half,)),
        ],
        compiler_params=pltpu.CompilerParams(collective_id=tag, has_side_effects=True),
    )(block)


def contract(pattern, first_op, second_op):
    return jnp.einsum(
        pattern, first_op, second_op, precision=high, preferred_element_type=jnp.float32
    )


def tables(seq_len):
    total = 2 * seq_len
    outer = total // LANES
    half = seq_len // LANES
    k1 = np.arange(outer)[:, None]
    a1 = 2.0 * np.pi * ((k1 * np.arange(half)[None, :]) % outer) / outer
    at = 2.0 * np.pi * ((k1 * np.arange(LANES)[None, :]) % total) / total
    m2 = np.arange(LANES)
    a2 = 2.0 * np.pi * ((m2[:, None] * m2[None, :]) % LANES) / LANES
    c1, s1 = np.cos(a1), np.sin(a1)
    c2, s2 = np.cos(a2), np.sin(a2)
    f32 = lambda v: jnp.asarray(v, jnp.float32)
    return dict(
        first=f32(np.concatenate([c1, -s1], axis=0)),
        tc=f32(np.cos(at)[:, None, :]),
        ts=f32(np.sin(at)[:, None, :]),
        fwd2=f32(np.block([[c2, -s2], [s2, c2]])),
        inv2=f32(np.block([[c2, s2], [-s2, c2]])),
        last=f32(np.concatenate([c1.T, -s1.T], axis=1) / total),
    )


def forward(signal, tb):
    outer = tb["tc"].shape[0]
    both = contract("kn,ncm->kcm", tb["first"], signal)
    br, bi = both[:outer], both[outer:]
    tr, ti = tb["tc"], -tb["ts"]
    twisted = jnp.concatenate([br * tr - bi * ti, br * ti + bi * tr], axis=2)
    return contract("kcm,mj->kcj", twisted, tb["fwd2"])


def inverse(spectrum, tb):
    z = contract("kcj,jm->kcm", spectrum, tb["inv2"])
    zr, zi = z[:, :, :LANES], z[:, :, LANES:]
    tc, ts = tb["tc"], tb["ts"]
    stacked = jnp.concatenate([zr * tc - zi * ts, zr * ts + zi * tc], axis=0)
    return contract("nk,kcm->ncm", tb["last"], stacked)


def long_conv(mixed_in, long_filter):
    half = mixed_in.shape[0]
    tb = tables(half * LANES)
    width = mixed_in.shape[1]
    both = forward(jnp.concatenate([mixed_in, long_filter], axis=1), tb)
    xs, hs = both[:, :width], both[:, width:]
    xr, xi = xs[:, :, :LANES], xs[:, :, LANES:]
    hr, hi = hs[:, :, :LANES], hs[:, :, LANES:]
    product = jnp.concatenate([xr * hr - xi * hi, xr * hi + xi * hr], axis=2)
    return inverse(product, tb)


def shift_seq(signal, distance):
    rows, width, lanes = signal.shape
    prev = jnp.concatenate([jnp.zeros((1, width, lanes), signal.dtype), signal[:-1]], axis=0)
    return jnp.concatenate(
        [prev[:, :, lanes - distance :], signal[:, :, : lanes - distance]], axis=2
    )


def short_conv(signal, taps):
    summed = taps[0][None, :, None] * signal
    for offset in range(1, taps.shape[0]):
        summed = summed + taps[offset][None, :, None] * shift_seq(signal, offset)
    return summed


def to_ncm(block):
    rows, width = block.shape
    return block.reshape(rows // LANES, LANES, width).transpose(0, 2, 1)


def on_device(out_gate, in_gate, values, short_filter, long_filter, skip_gain, out_weight):
    seq_count = lax.axis_size("seq")
    seq_index = lax.axis_index("seq")
    rows = out_gate.shape[0]
    width = out_gate.shape[1] // seq_count
    half = rows // LANES

    planes = [to_ncm(out_gate), to_ncm(in_gate), to_ncm(values)]
    planes.append(to_ncm(long_filter).astype(jnp.bfloat16))
    spread = exchange(planes, seq_count, 0)
    start = seq_index * width
    taps = lax.dynamic_slice_in_dim(short_filter, start, width, axis=2)
    gain = lax.dynamic_slice_in_dim(skip_gain, start, width, axis=0)
    spread = spread.astype(jnp.float32)
    gate_late = short_conv(spread[0], taps[0])
    mixed_in = short_conv(spread[1], taps[1]) * short_conv(spread[2], taps[2])
    long_out = long_conv(mixed_in, spread[3])
    filtered = long_out + gain[None, :, None] * mixed_in
    mixed = (gate_late * filtered).astype(jnp.bfloat16)
    chans = lax.axis_size("ch")
    gathered = return_and_gather(mixed.reshape(seq_count, half, width, LANES), seq_count, chans, 1)
    gathered = gathered.reshape(half, chans * seq_count * width, LANES)
    summed = jnp.einsum(
        "co,ncm->nom", out_weight, gathered, preferred_element_type=jnp.float32
    )
    return summed.astype(jnp.bfloat16).transpose(0, 2, 1).reshape(rows, -1)


def solution(mesh):
    return jax.shard_map(
        on_device,
        mesh=mesh,
        in_specs=(
            P("seq", "ch"),
            P("seq", "ch"),
            P("seq", "ch"),
            P(None, None, "ch"),
            P("seq", "ch"),
            P("ch"),
            P(None, "ch"),
        ),
        out_specs=P("seq", "ch"),
        check_vma=False,
    )
```

```python
import functools

import jax
import jax.numpy as jnp
import numpy as np
from jax import lax
from jax.experimental import pallas as pl
from jax.experimental.pallas import tpu as pltpu
from jax.sharding import PartitionSpec as P

high = lax.Precision.HIGH
LANES = 128
MESH = pl.DeviceIdType.MESH


def peer_offsets(group, inner=8):
    if group % inner:
        inner = group
    outer = group // inner
    dist = lambda d, n: min(d, n - d)
    seen, order = set(), []
    cands = [(dx, dz) for dx in range(outer) for dz in range(inner) if dx or dz]
    cands.sort(key=lambda o: (-(dist(o[0], outer) + dist(o[1], inner)), o))
    for dx, dz in cands:
        for off in ((dx, dz), ((outer - dx) % outer, (inner - dz) % inner)):
            if off not in seen:
                seen.add(off)
                order.append(off)
    return inner, order


def shifted_peer(me, off, inner, group, sign):
    outer = group // inner
    x, z = me // inner, lax.rem(me, inner)
    dx, dz = off
    return lax.rem(x + sign * dx + outer, outer) * inner + lax.rem(z + sign * dz + inner, inner)


def exchange_kernel(group, source, target, send_sem, recv_sem, local_sem):
    me = lax.axis_index("seq")
    ch = lax.axis_index("ch")
    half = source.shape[1]
    width = target.shape[2]
    barrier = pltpu.get_barrier_semaphore()
    for step in range(1, group):
        peer = lax.rem(me + step, group)
        pl.semaphore_signal(barrier, inc=1, device_id=(peer, ch), device_id_type=MESH)
    pl.semaphore_wait(barrier, group - 1)

    def piece(ref_src, peer, origin):
        return (
            ref_src.at[:, :, pl.ds(peer * width, width)],
            target.at[:, pl.ds(origin * half, half)],
        )

    src, dst = piece(source, me, me)
    local = pltpu.make_async_copy(src, dst, local_sem.at[0])
    local.start()
    inner, offsets = peer_offsets(group)
    sent = []
    for step, off in enumerate(offsets, start=1):
        peer = shifted_peer(me, off, inner, group, 1)
        src, dst = piece(source, peer, me)
        cp = pltpu.make_async_remote_copy(
            src_ref=src,
            dst_ref=dst,
            send_sem=send_sem.at[step],
            recv_sem=recv_sem.at[step],
            device_id=(peer, ch),
            device_id_type=MESH,
        )
        cp.start()
        sent.append(cp)
    local.wait()
    for cp in sent:
        cp.wait_send()
    for step, off in enumerate(offsets, start=1):
        origin = shifted_peer(me, off, inner, group, -1)
        src, dst = piece(source, me, origin)
        pltpu.make_async_remote_copy(
            src_ref=src,
            dst_ref=dst,
            send_sem=send_sem.at[step],
            recv_sem=recv_sem.at[step],
            device_id=(origin, ch),
            device_id_type=MESH,
        ).wait_recv()


def exchange(stacked, group, tag):
    planes, half, full, lanes = stacked.shape
    return pl.pallas_call(
        functools.partial(exchange_kernel, group),
        out_shape=jax.ShapeDtypeStruct((planes, group * half, full // group, lanes), stacked.dtype),
        in_specs=[pl.BlockSpec(memory_space=pl.ANY)],
        out_specs=pl.BlockSpec(memory_space=pl.ANY),
        scratch_shapes=[
            pltpu.SemaphoreType.DMA((group,)),
            pltpu.SemaphoreType.DMA((group,)),
            pltpu.SemaphoreType.DMA((1,)),
        ],
        compiler_params=pltpu.CompilerParams(collective_id=tag, has_side_effects=True),
    )(stacked)


def return_kernel(group, chans, source, target, send_sem, recv_sem, pass_sem, got_sem, fwd_sem, local_sem):
    me = lax.axis_index("seq")
    ch = lax.axis_index("ch")
    half = source.shape[1]
    sibling = ch + 1 - 2 * lax.rem(ch, 2)
    across = [lax.rem(ch + 2 * hop, chans) for hop in range(1, chans // 2)]
    barrier = pltpu.get_barrier_semaphore()
    for step in range(1, group):
        peer = lax.rem(me + step, group)
        pl.semaphore_signal(barrier, inc=1, device_id=(peer, ch), device_id_type=MESH)
    for peer_ch in across + [sibling]:
        pl.semaphore_signal(barrier, inc=1, device_id=(me, peer_ch), device_id_type=MESH)
    pl.semaphore_wait(barrier, group - 1 + len(across) + 1)

    def incoming(part, slot, peer_ch):
        return pltpu.make_async_remote_copy(
            src_ref=target.at[part, slot],
            dst_ref=target.at[part, slot],
            send_sem=pass_sem.at[part, 0],
            recv_sem=got_sem.at[part, slot],
            device_id=(me, peer_ch),
            device_id_type=MESH,
        )

    inner, offsets = peer_offsets(group)
    sent = []
    locals_ = []
    for part in range(half):
        cp = pltpu.make_async_copy(
            source.at[me, part], target.at[part, ch, me], local_sem.at[part]
        )
        cp.start()
        locals_.append(cp)
        for step, off in enumerate(offsets, start=1):
            peer = shifted_peer(me, off, inner, group, 1)
            cp = pltpu.make_async_remote_copy(
                src_ref=source.at[peer, part],
                dst_ref=target.at[part, ch, me],
                send_sem=send_sem.at[part, step],
                recv_sem=recv_sem.at[part, step],
                device_id=(peer, ch),
                device_id_type=MESH,
            )
            cp.start()
            sent.append(cp)
    passed = []
    for part in range(half):
        locals_[part].wait()
        for step, off in enumerate(offsets, start=1):
            origin = shifted_peer(me, off, inner, group, -1)
            pltpu.make_async_remote_copy(
                src_ref=source.at[origin, part],
                dst_ref=target.at[part, ch, origin],
                send_sem=send_sem.at[part, step],
                recv_sem=recv_sem.at[part, step],
                device_id=(origin, ch),
                device_id_type=MESH,
            ).wait_recv()
        for slot, peer_ch in enumerate(across + [sibling]):
            cp = pltpu.make_async_remote_copy(
                src_ref=target.at[part, ch],
                dst_ref=target.at[part, ch],
                send_sem=pass_sem.at[part, slot],
                recv_sem=got_sem.at[part, ch],
                device_id=(me, peer_ch),
                device_id_type=MESH,
            )
            cp.start()
            passed.append(cp)
    forwarded = []
    for part in range(half):
        for hop in range(1, chans // 2):
            origin = lax.rem(ch + chans - 2 * hop, chans)
            incoming(part, origin, origin).wait_recv()
            cp = pltpu.make_async_remote_copy(
                src_ref=target.at[part, origin],
                dst_ref=target.at[part, origin],
                send_sem=fwd_sem.at[part, hop],
                recv_sem=got_sem.at[part, origin],
                device_id=(me, sibling),
                device_id_type=MESH,
            )
            cp.start()
            forwarded.append(cp)
    for cp in sent + passed + forwarded:
        cp.wait_send()
    for part in range(half):
        for hop in range(1, chans // 2):
            origin = lax.rem(sibling + chans - 2 * hop, chans)
            incoming(part, origin, origin).wait_recv()
        incoming(part, sibling, sibling).wait_recv()


def return_and_gather(block, group, chans, tag):
    half = block.shape[1]
    return pl.pallas_call(
        functools.partial(return_kernel, group, chans),
        out_shape=jax.ShapeDtypeStruct(
            (half, chans, block.shape[0]) + block.shape[2:], block.dtype
        ),
        in_specs=[pl.BlockSpec(memory_space=pl.ANY)],
        out_specs=pl.BlockSpec(memory_space=pl.ANY),
        scratch_shapes=[
            pltpu.SemaphoreType.DMA((half, group)),
            pltpu.SemaphoreType.DMA((half, group)),
            pltpu.SemaphoreType.DMA((half, chans // 2)),
            pltpu.SemaphoreType.DMA((half, chans)),
            pltpu.SemaphoreType.DMA((half, chans // 2)),
            pltpu.SemaphoreType.DMA((half,)),
        ],
        compiler_params=pltpu.CompilerParams(collective_id=tag, has_side_effects=True),
    )(block)


def contract(pattern, first_op, second_op):
    return jnp.einsum(
        pattern, first_op, second_op, precision=high, preferred_element_type=jnp.float32
    )


def tables(seq_len):
    total = 2 * seq_len
    outer = total // LANES
    half = seq_len // LANES
    k1 = np.arange(outer)[:, None]
    a1 = 2.0 * np.pi * ((k1 * np.arange(half)[None, :]) % outer) / outer
    at = 2.0 * np.pi * ((k1 * np.arange(LANES)[None, :]) % total) / total
    m2 = np.arange(LANES)
    a2 = 2.0 * np.pi * ((m2[:, None] * m2[None, :]) % LANES) / LANES
    c1, s1 = np.cos(a1), np.sin(a1)
    c2, s2 = np.cos(a2), np.sin(a2)
    f32 = lambda v: jnp.asarray(v, jnp.float32)
    return dict(
        first=f32(np.concatenate([c1, -s1], axis=0)),
        tc=f32(np.cos(at)[:, None, :]),
        ts=f32(np.sin(at)[:, None, :]),
        fwd2=f32(np.block([[c2, -s2], [s2, c2]])),
        inv2=f32(np.block([[c2, s2], [-s2, c2]])),
        last=f32(np.concatenate([c1.T, -s1.T], axis=1) / total),
    )


def forward(signal, tb):
    outer = tb["tc"].shape[0]
    both = contract("kn,ncm->kcm", tb["first"], signal)
    br, bi = both[:outer], both[outer:]
    tr, ti = tb["tc"], -tb["ts"]
    twisted = jnp.concatenate([br * tr - bi * ti, br * ti + bi * tr], axis=2)
    return contract("kcm,mj->kcj", twisted, tb["fwd2"])


def inverse(spectrum, tb):
    z = contract("kcj,jm->kcm", spectrum, tb["inv2"])
    zr, zi = z[:, :, :LANES], z[:, :, LANES:]
    tc, ts = tb["tc"], tb["ts"]
    stacked = jnp.concatenate([zr * tc - zi * ts, zr * ts + zi * tc], axis=0)
    return contract("nk,kcm->ncm", tb["last"], stacked)


def long_conv(mixed_in, long_filter):
    half = mixed_in.shape[0]
    tb = tables(half * LANES)
    width = mixed_in.shape[1]
    both = forward(jnp.concatenate([mixed_in, long_filter], axis=1), tb)
    xs, hs = both[:, :width], both[:, width:]
    xr, xi = xs[:, :, :LANES], xs[:, :, LANES:]
    hr, hi = hs[:, :, :LANES], hs[:, :, LANES:]
    product = jnp.concatenate([xr * hr - xi * hi, xr * hi + xi * hr], axis=2)
    return inverse(product, tb)


def shift_seq(signal, distance):
    rows, width, lanes = signal.shape
    prev = jnp.concatenate([jnp.zeros((1, width, lanes), signal.dtype), signal[:-1]], axis=0)
    return jnp.concatenate(
        [prev[:, :, lanes - distance :], signal[:, :, : lanes - distance]], axis=2
    )


def short_conv(signal, taps):
    summed = taps[0][None, :, None] * signal
    for offset in range(1, taps.shape[0]):
        summed = summed + taps[offset][None, :, None] * shift_seq(signal, offset)
    return summed


def to_ncm(block):
    rows, width = block.shape
    return block.reshape(rows // LANES, LANES, width).transpose(0, 2, 1)


def on_device(out_gate, in_gate, values, short_filter, long_filter, skip_gain, out_weight):
    seq_count = lax.axis_size("seq")
    seq_index = lax.axis_index("seq")
    rows = out_gate.shape[0]
    width = out_gate.shape[1] // seq_count
    half = rows // LANES

    planes = [out_gate, in_gate, values, long_filter.astype(jnp.bfloat16)]
    stacked = jnp.stack([to_ncm(plane) for plane in planes])
    spread = exchange(stacked, seq_count, 0)
    start = seq_index * width
    taps = lax.dynamic_slice_in_dim(short_filter, start, width, axis=2)
    gain = lax.dynamic_slice_in_dim(skip_gain, start, width, axis=0)
    plane = lambda index: spread[index].astype(jnp.float32)
    gate_late = short_conv(plane(0), taps[0])
    mixed_in = short_conv(plane(1), taps[1]) * short_conv(plane(2), taps[2])
    long_out = long_conv(mixed_in, plane(3))
    filtered = long_out + gain[None, :, None] * mixed_in
    mixed = (gate_late * filtered).astype(jnp.bfloat16)
    chans = lax.axis_size("ch")
    gathered = return_and_gather(mixed.reshape(seq_count, half, width, LANES), seq_count, chans, 1)
    gathered = gathered.reshape(half, chans * seq_count * width, LANES)
    summed = jnp.einsum(
        "co,ncm->nom", out_weight, gathered, preferred_element_type=jnp.float32
    )
    return summed.astype(jnp.bfloat16).transpose(0, 2, 1).reshape(rows, -1)


def solution(mesh):
    return jax.shard_map(
        on_device,
        mesh=mesh,
        in_specs=(
            P("seq", "ch"),
            P("seq", "ch"),
            P("seq", "ch"),
            P(None, None, "ch"),
            P("seq", "ch"),
            P("ch"),
            P(None, "ch"),
        ),
        out_specs=P("seq", "ch"),
        check_vma=False,
    )
```

```python
import functools

import jax
import jax.numpy as jnp
import numpy as np
from jax import lax
from jax.experimental import pallas as pl
from jax.experimental.pallas import tpu as pltpu
from jax.sharding import PartitionSpec as P

high = lax.Precision.HIGH
LANES = 128
MESH = pl.DeviceIdType.MESH


def peer_offsets(group, inner=8):
    if group % inner:
        inner = group
    outer = group // inner
    dist = lambda d, n: min(d, n - d)
    seen, order = set(), []
    cands = [(dx, dz) for dx in range(outer) for dz in range(inner) if dx or dz]
    cands.sort(key=lambda o: (-(dist(o[0], outer) + dist(o[1], inner)), o))
    for dx, dz in cands:
        for off in ((dx, dz), ((outer - dx) % outer, (inner - dz) % inner)):
            if off not in seen:
                seen.add(off)
                order.append(off)
    return inner, order


def shifted_peer(me, off, inner, group, sign):
    outer = group // inner
    x, z = me // inner, lax.rem(me, inner)
    dx, dz = off
    return lax.rem(x + sign * dx + outer, outer) * inner + lax.rem(z + sign * dz + inner, inner)


def exchange_kernel(group, source, target, send_sem, recv_sem, local_sem):
    me = lax.axis_index("seq")
    ch = lax.axis_index("ch")
    half = source.shape[1]
    width = target.shape[2]
    barrier = pltpu.get_barrier_semaphore()
    for step in range(1, group):
        peer = lax.rem(me + step, group)
        pl.semaphore_signal(barrier, inc=1, device_id=(peer, ch), device_id_type=MESH)
    pl.semaphore_wait(barrier, group - 1)

    def piece(ref_src, peer, origin):
        return (
            ref_src.at[:, :, pl.ds(peer * width, width)],
            target.at[:, pl.ds(origin * half, half)],
        )

    src, dst = piece(source, me, me)
    local = pltpu.make_async_copy(src, dst, local_sem.at[0])
    local.start()
    inner, offsets = peer_offsets(group)
    sent = []
    for step, off in enumerate(offsets, start=1):
        peer = shifted_peer(me, off, inner, group, 1)
        src, dst = piece(source, peer, me)
        cp = pltpu.make_async_remote_copy(
            src_ref=src,
            dst_ref=dst,
            send_sem=send_sem.at[step],
            recv_sem=recv_sem.at[step],
            device_id=(peer, ch),
            device_id_type=MESH,
        )
        cp.start()
        sent.append(cp)
    local.wait()
    for cp in sent:
        cp.wait_send()
    for step, off in enumerate(offsets, start=1):
        origin = shifted_peer(me, off, inner, group, -1)
        src, dst = piece(source, me, origin)
        pltpu.make_async_remote_copy(
            src_ref=src,
            dst_ref=dst,
            send_sem=send_sem.at[step],
            recv_sem=recv_sem.at[step],
            device_id=(origin, ch),
            device_id_type=MESH,
        ).wait_recv()


def exchange(stacked, group, tag):
    planes, half, full, lanes = stacked.shape
    return pl.pallas_call(
        functools.partial(exchange_kernel, group),
        out_shape=jax.ShapeDtypeStruct((planes, group * half, full // group, lanes), stacked.dtype),
        in_specs=[pl.BlockSpec(memory_space=pl.ANY)],
        out_specs=pl.BlockSpec(memory_space=pl.ANY),
        scratch_shapes=[
            pltpu.SemaphoreType.DMA((group,)),
            pltpu.SemaphoreType.DMA((group,)),
            pltpu.SemaphoreType.DMA((1,)),
        ],
        compiler_params=pltpu.CompilerParams(collective_id=tag, has_side_effects=True),
    )(stacked)


def return_kernel(group, chans, source, target, send_sem, recv_sem, pass_sem, got_sem, fwd_sem, local_sem):
    me = lax.axis_index("seq")
    ch = lax.axis_index("ch")
    half = source.shape[1]
    sibling = ch + 1 - 2 * lax.rem(ch, 2)
    across = [lax.rem(ch + 2 * hop, chans) for hop in range(1, chans // 2)]
    barrier = pltpu.get_barrier_semaphore()
    for step in range(1, group):
        peer = lax.rem(me + step, group)
        pl.semaphore_signal(barrier, inc=1, device_id=(peer, ch), device_id_type=MESH)
    for peer_ch in across + [sibling]:
        pl.semaphore_signal(barrier, inc=1, device_id=(me, peer_ch), device_id_type=MESH)
    pl.semaphore_wait(barrier, group - 1 + len(across) + 1)

    def incoming(part, slot, peer_ch):
        return pltpu.make_async_remote_copy(
            src_ref=target.at[part, slot],
            dst_ref=target.at[part, slot],
            send_sem=pass_sem.at[part, 0],
            recv_sem=got_sem.at[part, slot],
            device_id=(me, peer_ch),
            device_id_type=MESH,
        )

    inner, offsets = peer_offsets(group)
    sent = []
    locals_ = []
    for part in range(half):
        cp = pltpu.make_async_copy(
            source.at[me, part], target.at[part, ch, me], local_sem.at[part]
        )
        cp.start()
        locals_.append(cp)
        for step, off in enumerate(offsets, start=1):
            peer = shifted_peer(me, off, inner, group, 1)
            cp = pltpu.make_async_remote_copy(
                src_ref=source.at[peer, part],
                dst_ref=target.at[part, ch, me],
                send_sem=send_sem.at[part, step],
                recv_sem=recv_sem.at[part, step],
                device_id=(peer, ch),
                device_id_type=MESH,
            )
            cp.start()
            sent.append(cp)
    passed = []
    for part in range(half):
        locals_[part].wait()
        for step, off in enumerate(offsets, start=1):
            origin = shifted_peer(me, off, inner, group, -1)
            pltpu.make_async_remote_copy(
                src_ref=source.at[origin, part],
                dst_ref=target.at[part, ch, origin],
                send_sem=send_sem.at[part, step],
                recv_sem=recv_sem.at[part, step],
                device_id=(origin, ch),
                device_id_type=MESH,
            ).wait_recv()
        for slot, peer_ch in enumerate(across + [sibling]):
            cp = pltpu.make_async_remote_copy(
                src_ref=target.at[part, ch],
                dst_ref=target.at[part, ch],
                send_sem=pass_sem.at[part, slot],
                recv_sem=got_sem.at[part, ch],
                device_id=(me, peer_ch),
                device_id_type=MESH,
            )
            cp.start()
            passed.append(cp)
    forwarded = []
    for part in range(half):
        for hop in range(1, chans // 2):
            origin = lax.rem(ch + chans - 2 * hop, chans)
            incoming(part, origin, origin).wait_recv()
            cp = pltpu.make_async_remote_copy(
                src_ref=target.at[part, origin],
                dst_ref=target.at[part, origin],
                send_sem=fwd_sem.at[part, hop],
                recv_sem=got_sem.at[part, origin],
                device_id=(me, sibling),
                device_id_type=MESH,
            )
            cp.start()
            forwarded.append(cp)
    for cp in sent + passed + forwarded:
        cp.wait_send()
    for part in range(half):
        for hop in range(1, chans // 2):
            origin = lax.rem(sibling + chans - 2 * hop, chans)
            incoming(part, origin, origin).wait_recv()
        incoming(part, sibling, sibling).wait_recv()


def return_and_gather(block, group, chans, tag):
    half = block.shape[1]
    return pl.pallas_call(
        functools.partial(return_kernel, group, chans),
        out_shape=jax.ShapeDtypeStruct(
            (half, chans, block.shape[0]) + block.shape[2:], block.dtype
        ),
        in_specs=[pl.BlockSpec(memory_space=pl.ANY)],
        out_specs=pl.BlockSpec(memory_space=pl.ANY),
        scratch_shapes=[
            pltpu.SemaphoreType.DMA((half, group)),
            pltpu.SemaphoreType.DMA((half, group)),
            pltpu.SemaphoreType.DMA((half, chans // 2)),
            pltpu.SemaphoreType.DMA((half, chans)),
            pltpu.SemaphoreType.DMA((half, chans // 2)),
            pltpu.SemaphoreType.DMA((half,)),
        ],
        compiler_params=pltpu.CompilerParams(collective_id=tag, has_side_effects=True),
    )(block)


def contract(pattern, first_op, second_op):
    return jnp.einsum(
        pattern, first_op, second_op, precision=high, preferred_element_type=jnp.float32
    )


def tables(seq_len):
    total = 2 * seq_len
    outer = total // LANES
    half = seq_len // LANES
    keep = outer // 2 + 1
    rows = -(-keep // 8) * 8
    k1 = np.arange(rows)[:, None]
    a1 = 2.0 * np.pi * ((k1 * np.arange(half)[None, :]) % outer) / outer
    at = 2.0 * np.pi * ((k1 * np.arange(LANES)[None, :]) % total) / total
    m2 = np.arange(LANES)
    a2 = 2.0 * np.pi * ((m2[:, None] * m2[None, :]) % LANES) / LANES
    c1, s1 = np.cos(a1), np.sin(a1)
    c2, s2 = np.cos(a2), np.sin(a2)
    weight = np.where((k1 == 0) | (k1 == outer // 2), 1.0, 2.0) * (k1 < keep)
    f32 = lambda v: jnp.asarray(v, jnp.float32)
    return dict(
        first=f32(np.concatenate([c1, -s1], axis=0)),
        tc=f32(np.cos(at)[:, None, :]),
        ts=f32(np.sin(at)[:, None, :]),
        fwd2=f32(np.block([[c2, -s2], [s2, c2]])),
        inv2=f32(np.block([[c2, s2], [-s2, c2]])),
        last=f32(np.concatenate([(c1 * weight).T, -(s1 * weight).T], axis=1) / total),
    )


def forward(signal, tb):
    outer = tb["tc"].shape[0]
    both = contract("kn,ncm->kcm", tb["first"], signal)
    br, bi = both[:outer], both[outer:]
    tr, ti = tb["tc"], -tb["ts"]
    twisted = jnp.concatenate([br * tr - bi * ti, br * ti + bi * tr], axis=2)
    return contract("kcm,mj->kcj", twisted, tb["fwd2"])


def inverse(spectrum, tb):
    z = contract("kcj,jm->kcm", spectrum, tb["inv2"])
    zr, zi = z[:, :, :LANES], z[:, :, LANES:]
    tc, ts = tb["tc"], tb["ts"]
    stacked = jnp.concatenate([zr * tc - zi * ts, zr * ts + zi * tc], axis=0)
    return contract("nk,kcm->ncm", tb["last"], stacked)


def long_conv(mixed_in, long_filter):
    half = mixed_in.shape[0]
    tb = tables(half * LANES)
    width = mixed_in.shape[1]
    both = forward(jnp.concatenate([mixed_in, long_filter], axis=1), tb)
    xs, hs = both[:, :width], both[:, width:]
    xr, xi = xs[:, :, :LANES], xs[:, :, LANES:]
    hr, hi = hs[:, :, :LANES], hs[:, :, LANES:]
    product = jnp.concatenate([xr * hr - xi * hi, xr * hi + xi * hr], axis=2)
    return inverse(product, tb)


def shift_seq(signal, distance):
    rows, width, lanes = signal.shape
    prev = jnp.concatenate([jnp.zeros((1, width, lanes), signal.dtype), signal[:-1]], axis=0)
    return jnp.concatenate(
        [prev[:, :, lanes - distance :], signal[:, :, : lanes - distance]], axis=2
    )


def short_conv(signal, taps):
    summed = taps[0][None, :, None] * signal
    for offset in range(1, taps.shape[0]):
        summed = summed + taps[offset][None, :, None] * shift_seq(signal, offset)
    return summed


def to_ncm(block):
    rows, width = block.shape
    return block.reshape(rows // LANES, LANES, width).transpose(0, 2, 1)


def on_device(out_gate, in_gate, values, short_filter, long_filter, skip_gain, out_weight):
    seq_count = lax.axis_size("seq")
    seq_index = lax.axis_index("seq")
    rows = out_gate.shape[0]
    width = out_gate.shape[1] // seq_count
    half = rows // LANES

    planes = [out_gate, in_gate, values, long_filter.astype(jnp.bfloat16)]
    stacked = jnp.stack([to_ncm(plane) for plane in planes])
    spread = exchange(stacked, seq_count, 0)
    start = seq_index * width
    taps = lax.dynamic_slice_in_dim(short_filter, start, width, axis=2)
    gain = lax.dynamic_slice_in_dim(skip_gain, start, width, axis=0)
    spread = spread.astype(jnp.float32)
    gate_late = short_conv(spread[0], taps[0])
    mixed_in = short_conv(spread[1], taps[1]) * short_conv(spread[2], taps[2])
    long_out = long_conv(mixed_in, spread[3])
    filtered = long_out + gain[None, :, None] * mixed_in
    mixed = (gate_late * filtered).astype(jnp.bfloat16)
    chans = lax.axis_size("ch")
    gathered = return_and_gather(mixed.reshape(seq_count, half, width, LANES), seq_count, chans, 1)
    gathered = gathered.reshape(half, chans * seq_count * width, LANES)
    summed = jnp.einsum(
        "co,ncm->nom", out_weight, gathered, preferred_element_type=jnp.float32
    )
    return summed.astype(jnp.bfloat16).transpose(0, 2, 1).reshape(rows, -1)


def solution(mesh):
    return jax.shard_map(
        on_device,
        mesh=mesh,
        in_specs=(
            P("seq", "ch"),
            P("seq", "ch"),
            P("seq", "ch"),
            P(None, None, "ch"),
            P("seq", "ch"),
            P("ch"),
            P(None, "ch"),
        ),
        out_specs=P("seq", "ch"),
        check_vma=False,
    )
```

```python
import functools

import jax
import jax.numpy as jnp
import numpy as np
from jax import lax
from jax.experimental import pallas as pl
from jax.experimental.pallas import tpu as pltpu
from jax.sharding import PartitionSpec as P

high = lax.Precision.HIGH
LANES = 128
MESH = pl.DeviceIdType.MESH


def peer_offsets(group, inner=8):
    if group % inner:
        inner = group
    outer = group // inner
    dist = lambda d, n: min(d, n - d)
    seen, order = set(), []
    cands = [(dx, dz) for dx in range(outer) for dz in range(inner) if dx or dz]
    cands.sort(key=lambda o: (-(dist(o[0], outer) + dist(o[1], inner)), o))
    for dx, dz in cands:
        for off in ((dx, dz), ((outer - dx) % outer, (inner - dz) % inner)):
            if off not in seen:
                seen.add(off)
                order.append(off)
    return inner, order


def shifted_peer(me, off, inner, group, sign):
    outer = group // inner
    x, z = me // inner, lax.rem(me, inner)
    dx, dz = off
    return lax.rem(x + sign * dx + outer, outer) * inner + lax.rem(z + sign * dz + inner, inner)


def exchange_kernel(group, source, target, send_sem, recv_sem, local_sem):
    me = lax.axis_index("seq")
    ch = lax.axis_index("ch")
    half = source.shape[1]
    width = target.shape[2]
    barrier = pltpu.get_barrier_semaphore()
    for step in range(1, group):
        peer = lax.rem(me + step, group)
        pl.semaphore_signal(barrier, inc=1, device_id=(peer, ch), device_id_type=MESH)
    pl.semaphore_wait(barrier, group - 1)

    def piece(ref_src, peer, origin):
        return (
            ref_src.at[:, :, pl.ds(peer * width, width)],
            target.at[:, pl.ds(origin * half, half)],
        )

    src, dst = piece(source, me, me)
    local = pltpu.make_async_copy(src, dst, local_sem.at[0])
    local.start()
    inner, offsets = peer_offsets(group)
    sent = []
    for step, off in enumerate(offsets, start=1):
        peer = shifted_peer(me, off, inner, group, 1)
        src, dst = piece(source, peer, me)
        cp = pltpu.make_async_remote_copy(
            src_ref=src,
            dst_ref=dst,
            send_sem=send_sem.at[step],
            recv_sem=recv_sem.at[step],
            device_id=(peer, ch),
            device_id_type=MESH,
        )
        cp.start()
        sent.append(cp)
    local.wait()
    for cp in sent:
        cp.wait_send()
    for step, off in enumerate(offsets, start=1):
        origin = shifted_peer(me, off, inner, group, -1)
        src, dst = piece(source, me, origin)
        pltpu.make_async_remote_copy(
            src_ref=src,
            dst_ref=dst,
            send_sem=send_sem.at[step],
            recv_sem=recv_sem.at[step],
            device_id=(origin, ch),
            device_id_type=MESH,
        ).wait_recv()


def exchange(stacked, group, tag):
    planes, half, full, lanes = stacked.shape
    return pl.pallas_call(
        functools.partial(exchange_kernel, group),
        out_shape=jax.ShapeDtypeStruct((planes, group * half, full // group, lanes), stacked.dtype),
        in_specs=[pl.BlockSpec(memory_space=pl.ANY)],
        out_specs=pl.BlockSpec(memory_space=pl.ANY),
        scratch_shapes=[
            pltpu.SemaphoreType.DMA((group,)),
            pltpu.SemaphoreType.DMA((group,)),
            pltpu.SemaphoreType.DMA((1,)),
        ],
        compiler_params=pltpu.CompilerParams(collective_id=tag, has_side_effects=True),
    )(stacked)


def return_kernel(group, chans, source, target, send_sem, recv_sem, pass_sem, got_sem, fwd_sem, local_sem):
    me = lax.axis_index("seq")
    ch = lax.axis_index("ch")
    half = source.shape[1]
    sibling = ch + 1 - 2 * lax.rem(ch, 2)
    across = [lax.rem(ch + 2 * hop, chans) for hop in range(1, chans // 2)]
    barrier = pltpu.get_barrier_semaphore()
    for step in range(1, group):
        peer = lax.rem(me + step, group)
        pl.semaphore_signal(barrier, inc=1, device_id=(peer, ch), device_id_type=MESH)
    for peer_ch in across + [sibling]:
        pl.semaphore_signal(barrier, inc=1, device_id=(me, peer_ch), device_id_type=MESH)
    pl.semaphore_wait(barrier, group - 1 + len(across) + 1)

    def incoming(part, slot, peer_ch):
        return pltpu.make_async_remote_copy(
            src_ref=target.at[part, slot],
            dst_ref=target.at[part, slot],
            send_sem=pass_sem.at[part, 0],
            recv_sem=got_sem.at[part, slot],
            device_id=(me, peer_ch),
            device_id_type=MESH,
        )

    inner, offsets = peer_offsets(group)
    sent = []
    locals_ = []
    for part in range(half):
        cp = pltpu.make_async_copy(
            source.at[me, part], target.at[part, ch, me], local_sem.at[part]
        )
        cp.start()
        locals_.append(cp)
        for step, off in enumerate(offsets, start=1):
            peer = shifted_peer(me, off, inner, group, 1)
            cp = pltpu.make_async_remote_copy(
                src_ref=source.at[peer, part],
                dst_ref=target.at[part, ch, me],
                send_sem=send_sem.at[part, step],
                recv_sem=recv_sem.at[part, step],
                device_id=(peer, ch),
                device_id_type=MESH,
            )
            cp.start()
            sent.append(cp)
    passed = []
    for part in range(half):
        locals_[part].wait()
        for step, off in enumerate(offsets, start=1):
            origin = shifted_peer(me, off, inner, group, -1)
            pltpu.make_async_remote_copy(
                src_ref=source.at[origin, part],
                dst_ref=target.at[part, ch, origin],
                send_sem=send_sem.at[part, step],
                recv_sem=recv_sem.at[part, step],
                device_id=(origin, ch),
                device_id_type=MESH,
            ).wait_recv()
        for slot, peer_ch in enumerate(across + [sibling]):
            cp = pltpu.make_async_remote_copy(
                src_ref=target.at[part, ch],
                dst_ref=target.at[part, ch],
                send_sem=pass_sem.at[part, slot],
                recv_sem=got_sem.at[part, ch],
                device_id=(me, peer_ch),
                device_id_type=MESH,
            )
            cp.start()
            passed.append(cp)
    forwarded = []
    for part in range(half):
        for hop in range(1, chans // 2):
            origin = lax.rem(ch + chans - 2 * hop, chans)
            incoming(part, origin, origin).wait_recv()
            cp = pltpu.make_async_remote_copy(
                src_ref=target.at[part, origin],
                dst_ref=target.at[part, origin],
                send_sem=fwd_sem.at[part, hop],
                recv_sem=got_sem.at[part, origin],
                device_id=(me, sibling),
                device_id_type=MESH,
            )
            cp.start()
            forwarded.append(cp)
    for cp in sent + passed + forwarded:
        cp.wait_send()
    for part in range(half):
        for hop in range(1, chans // 2):
            origin = lax.rem(sibling + chans - 2 * hop, chans)
            incoming(part, origin, origin).wait_recv()
        incoming(part, sibling, sibling).wait_recv()


def return_and_gather(block, group, chans, tag):
    half = block.shape[1]
    return pl.pallas_call(
        functools.partial(return_kernel, group, chans),
        out_shape=jax.ShapeDtypeStruct(
            (half, chans, block.shape[0]) + block.shape[2:], block.dtype
        ),
        in_specs=[pl.BlockSpec(memory_space=pl.ANY)],
        out_specs=pl.BlockSpec(memory_space=pl.ANY),
        scratch_shapes=[
            pltpu.SemaphoreType.DMA((half, group)),
            pltpu.SemaphoreType.DMA((half, group)),
            pltpu.SemaphoreType.DMA((half, chans // 2)),
            pltpu.SemaphoreType.DMA((half, chans)),
            pltpu.SemaphoreType.DMA((half, chans // 2)),
            pltpu.SemaphoreType.DMA((half,)),
        ],
        compiler_params=pltpu.CompilerParams(collective_id=tag, has_side_effects=True),
    )(block)


def contract(pattern, first_op, second_op):
    return jnp.einsum(
        pattern, first_op, second_op, precision=high, preferred_element_type=jnp.float32
    )


def tables(seq_len):
    total = 2 * seq_len
    outer = total // LANES
    half = seq_len // LANES
    keep = outer // 2 + 1
    rows = -(-keep // 8) * 8
    k1 = np.arange(rows)[:, None]
    a1 = 2.0 * np.pi * ((k1 * np.arange(half)[None, :]) % outer) / outer
    at = 2.0 * np.pi * ((k1 * np.arange(LANES)[None, :]) % total) / total
    m2 = np.arange(LANES)
    a2 = 2.0 * np.pi * ((m2[:, None] * m2[None, :]) % LANES) / LANES
    c1, s1 = np.cos(a1), np.sin(a1)
    c2, s2 = np.cos(a2), np.sin(a2)
    weight = np.where((k1 == 0) | (k1 == outer // 2), 1.0, 2.0) * (k1 < keep)
    f32 = lambda v: jnp.asarray(v, jnp.float32)
    return dict(
        first=f32(np.concatenate([c1, -s1], axis=0)),
        tc=f32(np.cos(at)[:, None, :]),
        ts=f32(np.sin(at)[:, None, :]),
        fwd2=f32(np.block([[c2, -s2], [s2, c2]])),
        inv2=f32(np.block([[c2, s2], [-s2, c2]])),
        last=f32(np.concatenate([(c1 * weight).T, -(s1 * weight).T], axis=1) / total),
    )


def forward(signal, tb):
    outer = tb["tc"].shape[0]
    both = contract("kn,ncm->kcm", tb["first"], signal)
    br, bi = both[:outer], both[outer:]
    tr, ti = tb["tc"], -tb["ts"]
    twisted = jnp.concatenate([br * tr - bi * ti, br * ti + bi * tr], axis=2)
    return contract("kcm,mj->kcj", twisted, tb["fwd2"])


def inverse(spectrum, tb):
    z = contract("kcj,jm->kcm", spectrum, tb["inv2"])
    zr, zi = z[:, :, :LANES], z[:, :, LANES:]
    tc, ts = tb["tc"], tb["ts"]
    stacked = jnp.concatenate([zr * tc - zi * ts, zr * ts + zi * tc], axis=0)
    return contract("nk,kcm->ncm", tb["last"], stacked)


def long_conv(mixed_in, long_filter):
    half = mixed_in.shape[0]
    tb = tables(half * LANES)
    width = mixed_in.shape[1]
    both = forward(jnp.concatenate([mixed_in, long_filter], axis=1), tb)
    xs, hs = both[:, :width], both[:, width:]
    xr, xi = xs[:, :, :LANES], xs[:, :, LANES:]
    hr, hi = hs[:, :, :LANES], hs[:, :, LANES:]
    product = jnp.concatenate([xr * hr - xi * hi, xr * hi + xi * hr], axis=2)
    return inverse(product, tb)


def shift_seq(signal, distance):
    rows, width, lanes = signal.shape
    prev = jnp.concatenate([jnp.zeros((1, width, lanes), signal.dtype), signal[:-1]], axis=0)
    return jnp.concatenate(
        [prev[:, :, lanes - distance :], signal[:, :, : lanes - distance]], axis=2
    )


def short_conv(signal, taps):
    summed = taps[0][None, :, None] * signal
    for offset in range(1, taps.shape[0]):
        summed = summed + taps[offset][None, :, None] * shift_seq(signal, offset)
    return summed


def to_ncm(block):
    rows, width = block.shape
    return block.reshape(rows // LANES, LANES, width).transpose(0, 2, 1)


def on_device(out_gate, in_gate, values, short_filter, long_filter, skip_gain, out_weight):
    seq_count = lax.axis_size("seq")
    seq_index = lax.axis_index("seq")
    rows = out_gate.shape[0]
    width = out_gate.shape[1] // seq_count
    half = rows // LANES

    planes = [out_gate, in_gate, values, long_filter.astype(jnp.bfloat16)]
    stacked = jnp.stack([to_ncm(plane) for plane in planes])
    spread = exchange(stacked, seq_count, 0)
    start = seq_index * width
    sets, tap_count = short_filter.shape[:2]
    params = jnp.concatenate([short_filter.reshape(sets * tap_count, -1), skip_gain[None]])
    params = lax.dynamic_slice_in_dim(params, start, width, axis=1)
    taps = params[: sets * tap_count].reshape(sets, tap_count, width)
    gain = params[sets * tap_count]
    spread = spread.astype(jnp.float32)
    gate_late = short_conv(spread[0], taps[0])
    mixed_in = short_conv(spread[1], taps[1]) * short_conv(spread[2], taps[2])
    long_out = long_conv(mixed_in, spread[3])
    filtered = long_out + gain[None, :, None] * mixed_in
    mixed = (gate_late * filtered).astype(jnp.bfloat16)
    chans = lax.axis_size("ch")
    gathered = return_and_gather(mixed.reshape(seq_count, half, width, LANES), seq_count, chans, 1)
    gathered = gathered.reshape(half, chans * seq_count * width, LANES)
    summed = jnp.einsum(
        "co,ncm->nom", out_weight, gathered, preferred_element_type=jnp.float32
    )
    return summed.astype(jnp.bfloat16).transpose(0, 2, 1).reshape(rows, -1)


def solution(mesh):
    return jax.shard_map(
        on_device,
        mesh=mesh,
        in_specs=(
            P("seq", "ch"),
            P("seq", "ch"),
            P("seq", "ch"),
            P(None, None, "ch"),
            P("seq", "ch"),
            P("ch"),
            P(None, "ch"),
        ),
        out_specs=P("seq", "ch"),
        check_vma=False,
    )
```

```python
import functools

import jax
import jax.numpy as jnp
import numpy as np
from jax import lax
from jax.experimental import pallas as pl
from jax.experimental.pallas import tpu as pltpu
from jax.sharding import PartitionSpec as P

high = lax.Precision.HIGH
LANES = 128
MESH = pl.DeviceIdType.MESH


def peer_offsets(group, inner=8):
    if group % inner:
        inner = group
    outer = group // inner
    dist = lambda d, n: min(d, n - d)
    seen, order = set(), []
    cands = [(dx, dz) for dx in range(outer) for dz in range(inner) if dx or dz]
    cands.sort(key=lambda o: (-(dist(o[0], outer) + dist(o[1], inner)), o))
    for dx, dz in cands:
        for off in ((dx, dz), ((outer - dx) % outer, (inner - dz) % inner)):
            if off not in seen:
                seen.add(off)
                order.append(off)
    return inner, order


def shifted_peer(me, off, inner, group, sign):
    outer = group // inner
    x, z = me // inner, lax.rem(me, inner)
    dx, dz = off
    return lax.rem(x + sign * dx + outer, outer) * inner + lax.rem(z + sign * dz + inner, inner)


def exchange_kernel(group, source, target, send_sem, recv_sem, local_sem):
    me = lax.axis_index("seq")
    ch = lax.axis_index("ch")
    half = source.shape[1]
    width = target.shape[2]
    barrier = pltpu.get_barrier_semaphore()
    for step in range(1, group):
        peer = lax.rem(me + step, group)
        pl.semaphore_signal(barrier, inc=1, device_id=(peer, ch), device_id_type=MESH)
    pl.semaphore_wait(barrier, group - 1)

    def piece(ref_src, peer, origin):
        return (
            ref_src.at[:, :, pl.ds(peer * width, width)],
            target.at[:, pl.ds(origin * half, half)],
        )

    src, dst = piece(source, me, me)
    local = pltpu.make_async_copy(src, dst, local_sem.at[0])
    local.start()
    inner, offsets = peer_offsets(group)
    sent = []
    for step, off in enumerate(offsets, start=1):
        peer = shifted_peer(me, off, inner, group, 1)
        src, dst = piece(source, peer, me)
        cp = pltpu.make_async_remote_copy(
            src_ref=src,
            dst_ref=dst,
            send_sem=send_sem.at[step],
            recv_sem=recv_sem.at[step],
            device_id=(peer, ch),
            device_id_type=MESH,
        )
        cp.start()
        sent.append(cp)
    local.wait()
    for cp in sent:
        cp.wait_send()
    for step, off in enumerate(offsets, start=1):
        origin = shifted_peer(me, off, inner, group, -1)
        src, dst = piece(source, me, origin)
        pltpu.make_async_remote_copy(
            src_ref=src,
            dst_ref=dst,
            send_sem=send_sem.at[step],
            recv_sem=recv_sem.at[step],
            device_id=(origin, ch),
            device_id_type=MESH,
        ).wait_recv()


def exchange(stacked, group, tag):
    planes, half, full, lanes = stacked.shape
    return pl.pallas_call(
        functools.partial(exchange_kernel, group),
        out_shape=jax.ShapeDtypeStruct((planes, group * half, full // group, lanes), stacked.dtype),
        in_specs=[pl.BlockSpec(memory_space=pl.ANY)],
        out_specs=pl.BlockSpec(memory_space=pl.ANY),
        scratch_shapes=[
            pltpu.SemaphoreType.DMA((group,)),
            pltpu.SemaphoreType.DMA((group,)),
            pltpu.SemaphoreType.DMA((1,)),
        ],
        compiler_params=pltpu.CompilerParams(collective_id=tag, has_side_effects=True),
    )(stacked)


def return_kernel(group, chans, source, target, send_sem, recv_sem, pass_sem, got_sem, fwd_sem, local_sem):
    me = lax.axis_index("seq")
    ch = lax.axis_index("ch")
    half = source.shape[1]
    sibling = ch + 1 - 2 * lax.rem(ch, 2)
    across = [lax.rem(ch + 2 * hop, chans) for hop in range(1, chans // 2)]
    barrier = pltpu.get_barrier_semaphore()
    for step in range(1, group):
        peer = lax.rem(me + step, group)
        pl.semaphore_signal(barrier, inc=1, device_id=(peer, ch), device_id_type=MESH)
    for peer_ch in across + [sibling]:
        pl.semaphore_signal(barrier, inc=1, device_id=(me, peer_ch), device_id_type=MESH)
    pl.semaphore_wait(barrier, group - 1 + len(across) + 1)

    def incoming(part, slot, peer_ch):
        return pltpu.make_async_remote_copy(
            src_ref=target.at[part, slot],
            dst_ref=target.at[part, slot],
            send_sem=pass_sem.at[part, 0],
            recv_sem=got_sem.at[part, slot],
            device_id=(me, peer_ch),
            device_id_type=MESH,
        )

    inner, offsets = peer_offsets(group)
    sent = []
    locals_ = []
    for part in range(half):
        cp = pltpu.make_async_copy(
            source.at[me, part], target.at[part, ch, me], local_sem.at[part]
        )
        cp.start()
        locals_.append(cp)
        for step, off in enumerate(offsets, start=1):
            peer = shifted_peer(me, off, inner, group, 1)
            cp = pltpu.make_async_remote_copy(
                src_ref=source.at[peer, part],
                dst_ref=target.at[part, ch, me],
                send_sem=send_sem.at[part, step],
                recv_sem=recv_sem.at[part, step],
                device_id=(peer, ch),
                device_id_type=MESH,
            )
            cp.start()
            sent.append(cp)
    passed = []
    for part in range(half):
        locals_[part].wait()
        for step, off in enumerate(offsets, start=1):
            origin = shifted_peer(me, off, inner, group, -1)
            pltpu.make_async_remote_copy(
                src_ref=source.at[origin, part],
                dst_ref=target.at[part, ch, origin],
                send_sem=send_sem.at[part, step],
                recv_sem=recv_sem.at[part, step],
                device_id=(origin, ch),
                device_id_type=MESH,
            ).wait_recv()
        for slot, peer_ch in enumerate(across + [sibling]):
            cp = pltpu.make_async_remote_copy(
                src_ref=target.at[part, ch],
                dst_ref=target.at[part, ch],
                send_sem=pass_sem.at[part, slot],
                recv_sem=got_sem.at[part, ch],
                device_id=(me, peer_ch),
                device_id_type=MESH,
            )
            cp.start()
            passed.append(cp)
    forwarded = []
    for part in range(half):
        for hop in range(1, chans // 2):
            origin = lax.rem(ch + chans - 2 * hop, chans)
            incoming(part, origin, origin).wait_recv()
            cp = pltpu.make_async_remote_copy(
                src_ref=target.at[part, origin],
                dst_ref=target.at[part, origin],
                send_sem=fwd_sem.at[part, hop],
                recv_sem=got_sem.at[part, origin],
                device_id=(me, sibling),
                device_id_type=MESH,
            )
            cp.start()
            forwarded.append(cp)
    for cp in sent + passed + forwarded:
        cp.wait_send()
    for part in range(half):
        for hop in range(1, chans // 2):
            origin = lax.rem(sibling + chans - 2 * hop, chans)
            incoming(part, origin, origin).wait_recv()
        incoming(part, sibling, sibling).wait_recv()


def return_and_gather(block, group, chans, tag):
    half = block.shape[1]
    return pl.pallas_call(
        functools.partial(return_kernel, group, chans),
        out_shape=jax.ShapeDtypeStruct(
            (half, chans, block.shape[0]) + block.shape[2:], block.dtype
        ),
        in_specs=[pl.BlockSpec(memory_space=pl.ANY)],
        out_specs=pl.BlockSpec(memory_space=pl.ANY),
        scratch_shapes=[
            pltpu.SemaphoreType.DMA((half, group)),
            pltpu.SemaphoreType.DMA((half, group)),
            pltpu.SemaphoreType.DMA((half, chans // 2)),
            pltpu.SemaphoreType.DMA((half, chans)),
            pltpu.SemaphoreType.DMA((half, chans // 2)),
            pltpu.SemaphoreType.DMA((half,)),
        ],
        compiler_params=pltpu.CompilerParams(collective_id=tag, has_side_effects=True),
    )(block)


def contract(pattern, first_op, second_op):
    return jnp.einsum(
        pattern, first_op, second_op, precision=high, preferred_element_type=jnp.float32
    )


def tables(seq_len):
    total = 2 * seq_len
    outer = total // LANES
    half = seq_len // LANES
    keep = outer // 2 + 1
    rows = -(-keep // 8) * 8
    k1 = np.arange(rows)[:, None]
    a1 = 2.0 * np.pi * ((k1 * np.arange(half)[None, :]) % outer) / outer
    at = 2.0 * np.pi * ((k1 * np.arange(LANES)[None, :]) % total) / total
    m2 = np.arange(LANES)
    a2 = 2.0 * np.pi * ((m2[:, None] * m2[None, :]) % LANES) / LANES
    c1, s1 = np.cos(a1), np.sin(a1)
    c2, s2 = np.cos(a2), np.sin(a2)
    weight = np.where((k1 == 0) | (k1 == outer // 2), 1.0, 2.0) * (k1 < keep)
    f32 = lambda v: jnp.asarray(v, jnp.float32)
    return dict(
        first=f32(np.concatenate([c1, -s1], axis=0)),
        tc=f32(np.cos(at)[:, None, :]),
        ts=f32(np.sin(at)[:, None, :]),
        fwd2=f32(np.block([[c2, -s2], [s2, c2]])),
        inv2=f32(np.block([[c2, s2], [-s2, c2]])),
        last=f32(np.concatenate([(c1 * weight).T, -(s1 * weight).T], axis=1) / total),
    )


def forward(signal, tb):
    outer = tb["tc"].shape[0]
    both = contract("kn,ncm->kcm", tb["first"], signal)
    br, bi = both[:outer], both[outer:]
    tr, ti = tb["tc"], -tb["ts"]
    twisted = jnp.concatenate([br * tr - bi * ti, br * ti + bi * tr], axis=2)
    return contract("kcm,mj->kcj", twisted, tb["fwd2"])


def inverse(spectrum, tb):
    z = contract("kcj,jm->kcm", spectrum, tb["inv2"])
    zr, zi = z[:, :, :LANES], z[:, :, LANES:]
    tc, ts = tb["tc"], tb["ts"]
    stacked = jnp.concatenate([zr * tc - zi * ts, zr * ts + zi * tc], axis=0)
    return contract("nk,kcm->ncm", tb["last"], stacked)


def long_conv(mixed_in, long_filter):
    half = mixed_in.shape[0]
    tb = tables(half * LANES)
    width = mixed_in.shape[1]
    both = forward(jnp.concatenate([mixed_in, long_filter], axis=1), tb)
    xs, hs = both[:, :width], both[:, width:]
    xr, xi = xs[:, :, :LANES], xs[:, :, LANES:]
    hr, hi = hs[:, :, :LANES], hs[:, :, LANES:]
    product = jnp.concatenate([xr * hr - xi * hi, xr * hi + xi * hr], axis=2)
    return inverse(product, tb)


def shift_seq(signal, distance):
    rows, width, lanes = signal.shape
    prev = jnp.concatenate([jnp.zeros((1, width, lanes), signal.dtype), signal[:-1]], axis=0)
    return jnp.concatenate(
        [prev[:, :, lanes - distance :], signal[:, :, : lanes - distance]], axis=2
    )


def short_conv(signal, taps):
    summed = taps[0][None, :, None] * signal
    for offset in range(1, taps.shape[0]):
        summed = summed + taps[offset][None, :, None] * shift_seq(signal, offset)
    return summed


def to_ncm(block):
    rows, width = block.shape
    return block.reshape(rows // LANES, LANES, width).transpose(0, 2, 1)


def on_device(out_gate, in_gate, values, short_filter, long_filter, skip_gain, out_weight):
    seq_count = lax.axis_size("seq")
    seq_index = lax.axis_index("seq")
    rows = out_gate.shape[0]
    width = out_gate.shape[1] // seq_count
    half = rows // LANES

    planes = [out_gate, in_gate, values, long_filter.astype(jnp.bfloat16)]
    stacked = jnp.stack([to_ncm(plane) for plane in planes])
    spread = exchange(stacked, seq_count, 0)
    start = seq_index * width
    sets, tap_count = short_filter.shape[:2]
    params = jnp.concatenate([short_filter.reshape(sets * tap_count, -1), skip_gain[None]])
    params = lax.dynamic_slice_in_dim(params, start, width, axis=1)
    taps = params[: sets * tap_count].reshape(sets, tap_count, width)
    gain = params[sets * tap_count]
    wide = spread[1:].astype(jnp.float32)
    mixed_in = short_conv(wide[0], taps[1]) * short_conv(wide[1], taps[2])
    long_out = long_conv(mixed_in, wide[2])
    gate_late = short_conv(spread[0].astype(jnp.float32), taps[0])
    filtered = long_out + gain[None, :, None] * mixed_in
    mixed = (gate_late * filtered).astype(jnp.bfloat16)
    chans = lax.axis_size("ch")
    gathered = return_and_gather(mixed.reshape(seq_count, half, width, LANES), seq_count, chans, 1)
    gathered = gathered.reshape(half, chans * seq_count * width, LANES)
    summed = jnp.einsum(
        "co,ncm->nom", out_weight, gathered, preferred_element_type=jnp.float32
    )
    return summed.astype(jnp.bfloat16).transpose(0, 2, 1).reshape(rows, -1)


def solution(mesh):
    return jax.shard_map(
        on_device,
        mesh=mesh,
        in_specs=(
            P("seq", "ch"),
            P("seq", "ch"),
            P("seq", "ch"),
            P(None, None, "ch"),
            P("seq", "ch"),
            P("ch"),
            P(None, "ch"),
        ),
        out_specs=P("seq", "ch"),
        check_vma=False,
    )
```

```python
import functools

import jax
import jax.numpy as jnp
import numpy as np
from jax import lax
from jax.experimental import pallas as pl
from jax.experimental.pallas import tpu as pltpu
from jax.sharding import PartitionSpec as P

high = lax.Precision.HIGH
LANES = 128
MESH = pl.DeviceIdType.MESH


def peer_offsets(group, inner=8):
    if group % inner:
        inner = group
    outer = group // inner
    dist = lambda d, n: min(d, n - d)
    seen, order = set(), []
    cands = [(dx, dz) for dx in range(outer) for dz in range(inner) if dx or dz]
    cands.sort(key=lambda o: (-(dist(o[0], outer) + dist(o[1], inner)), o))
    for dx, dz in cands:
        for off in ((dx, dz), ((outer - dx) % outer, (inner - dz) % inner)):
            if off not in seen:
                seen.add(off)
                order.append(off)
    return inner, order


def shifted_peer(me, off, inner, group, sign):
    outer = group // inner
    x, z = me // inner, lax.rem(me, inner)
    dx, dz = off
    return lax.rem(x + sign * dx + outer, outer) * inner + lax.rem(z + sign * dz + inner, inner)


def exchange_kernel(group, source, target, send_sem, recv_sem, local_sem):
    me = lax.axis_index("seq")
    ch = lax.axis_index("ch")
    half = source.shape[1]
    width = target.shape[2]

    def piece(ref_src, peer, origin):
        return (
            ref_src.at[:, :, pl.ds(peer * width, width)],
            target.at[:, pl.ds(origin * half, half)],
        )

    src, dst = piece(source, me, me)
    local = pltpu.make_async_copy(src, dst, local_sem.at[0])
    local.start()
    barrier = pltpu.get_barrier_semaphore()
    for step in range(1, group):
        peer = lax.rem(me + step, group)
        pl.semaphore_signal(barrier, inc=1, device_id=(peer, ch), device_id_type=MESH)
    pl.semaphore_wait(barrier, group - 1)
    inner, offsets = peer_offsets(group)
    sent = []
    for step, off in enumerate(offsets, start=1):
        peer = shifted_peer(me, off, inner, group, 1)
        src, dst = piece(source, peer, me)
        cp = pltpu.make_async_remote_copy(
            src_ref=src,
            dst_ref=dst,
            send_sem=send_sem.at[step],
            recv_sem=recv_sem.at[step],
            device_id=(peer, ch),
            device_id_type=MESH,
        )
        cp.start()
        sent.append(cp)
    local.wait()
    for cp in sent:
        cp.wait_send()
    for step, off in enumerate(offsets, start=1):
        origin = shifted_peer(me, off, inner, group, -1)
        src, dst = piece(source, me, origin)
        pltpu.make_async_remote_copy(
            src_ref=src,
            dst_ref=dst,
            send_sem=send_sem.at[step],
            recv_sem=recv_sem.at[step],
            device_id=(origin, ch),
            device_id_type=MESH,
        ).wait_recv()


def exchange(stacked, group, tag):
    planes, half, full, lanes = stacked.shape
    return pl.pallas_call(
        functools.partial(exchange_kernel, group),
        out_shape=jax.ShapeDtypeStruct((planes, group * half, full // group, lanes), stacked.dtype),
        in_specs=[pl.BlockSpec(memory_space=pl.ANY)],
        out_specs=pl.BlockSpec(memory_space=pl.ANY),
        scratch_shapes=[
            pltpu.SemaphoreType.DMA((group,)),
            pltpu.SemaphoreType.DMA((group,)),
            pltpu.SemaphoreType.DMA((1,)),
        ],
        compiler_params=pltpu.CompilerParams(collective_id=tag, has_side_effects=True),
    )(stacked)


def return_kernel(group, chans, source, target, send_sem, recv_sem, pass_sem, got_sem, fwd_sem, local_sem):
    me = lax.axis_index("seq")
    ch = lax.axis_index("ch")
    half = source.shape[1]
    sibling = ch + 1 - 2 * lax.rem(ch, 2)
    across = [lax.rem(ch + 2 * hop, chans) for hop in range(1, chans // 2)]
    locals_ = []
    for part in range(half):
        cp = pltpu.make_async_copy(
            source.at[me, part], target.at[part, ch, me], local_sem.at[part]
        )
        cp.start()
        locals_.append(cp)
    barrier = pltpu.get_barrier_semaphore()
    for step in range(1, group):
        peer = lax.rem(me + step, group)
        pl.semaphore_signal(barrier, inc=1, device_id=(peer, ch), device_id_type=MESH)
    for peer_ch in across + [sibling]:
        pl.semaphore_signal(barrier, inc=1, device_id=(me, peer_ch), device_id_type=MESH)
    pl.semaphore_wait(barrier, group - 1 + len(across) + 1)

    def incoming(part, slot, peer_ch):
        return pltpu.make_async_remote_copy(
            src_ref=target.at[part, slot],
            dst_ref=target.at[part, slot],
            send_sem=pass_sem.at[part, 0],
            recv_sem=got_sem.at[part, slot],
            device_id=(me, peer_ch),
            device_id_type=MESH,
        )

    inner, offsets = peer_offsets(group)
    sent = []
    for part in range(half):
        for step, off in enumerate(offsets, start=1):
            peer = shifted_peer(me, off, inner, group, 1)
            cp = pltpu.make_async_remote_copy(
                src_ref=source.at[peer, part],
                dst_ref=target.at[part, ch, me],
                send_sem=send_sem.at[part, step],
                recv_sem=recv_sem.at[part, step],
                device_id=(peer, ch),
                device_id_type=MESH,
            )
            cp.start()
            sent.append(cp)
    passed = []
    for part in range(half):
        locals_[part].wait()
        for step, off in enumerate(offsets, start=1):
            origin = shifted_peer(me, off, inner, group, -1)
            pltpu.make_async_remote_copy(
                src_ref=source.at[origin, part],
                dst_ref=target.at[part, ch, origin],
                send_sem=send_sem.at[part, step],
                recv_sem=recv_sem.at[part, step],
                device_id=(origin, ch),
                device_id_type=MESH,
            ).wait_recv()
        for slot, peer_ch in enumerate(across + [sibling]):
            cp = pltpu.make_async_remote_copy(
                src_ref=target.at[part, ch],
                dst_ref=target.at[part, ch],
                send_sem=pass_sem.at[part, slot],
                recv_sem=got_sem.at[part, ch],
                device_id=(me, peer_ch),
                device_id_type=MESH,
            )
            cp.start()
            passed.append(cp)
    forwarded = []
    for part in range(half):
        for hop in range(1, chans // 2):
            origin = lax.rem(ch + chans - 2 * hop, chans)
            incoming(part, origin, origin).wait_recv()
            cp = pltpu.make_async_remote_copy(
                src_ref=target.at[part, origin],
                dst_ref=target.at[part, origin],
                send_sem=fwd_sem.at[part, hop],
                recv_sem=got_sem.at[part, origin],
                device_id=(me, sibling),
                device_id_type=MESH,
            )
            cp.start()
            forwarded.append(cp)
    for cp in sent + passed + forwarded:
        cp.wait_send()
    for part in range(half):
        for hop in range(1, chans // 2):
            origin = lax.rem(sibling + chans - 2 * hop, chans)
            incoming(part, origin, origin).wait_recv()
        incoming(part, sibling, sibling).wait_recv()


def return_and_gather(block, group, chans, tag):
    half = block.shape[1]
    return pl.pallas_call(
        functools.partial(return_kernel, group, chans),
        out_shape=jax.ShapeDtypeStruct(
            (half, chans, block.shape[0]) + block.shape[2:], block.dtype
        ),
        in_specs=[pl.BlockSpec(memory_space=pl.ANY)],
        out_specs=pl.BlockSpec(memory_space=pl.ANY),
        scratch_shapes=[
            pltpu.SemaphoreType.DMA((half, group)),
            pltpu.SemaphoreType.DMA((half, group)),
            pltpu.SemaphoreType.DMA((half, chans // 2)),
            pltpu.SemaphoreType.DMA((half, chans)),
            pltpu.SemaphoreType.DMA((half, chans // 2)),
            pltpu.SemaphoreType.DMA((half,)),
        ],
        compiler_params=pltpu.CompilerParams(collective_id=tag, has_side_effects=True),
    )(block)


def contract(pattern, first_op, second_op):
    return jnp.einsum(
        pattern, first_op, second_op, precision=high, preferred_element_type=jnp.float32
    )


def tables(seq_len):
    total = 2 * seq_len
    outer = total // LANES
    half = seq_len // LANES
    keep = outer // 2 + 1
    rows = -(-keep // 8) * 8
    k1 = np.arange(rows)[:, None]
    a1 = 2.0 * np.pi * ((k1 * np.arange(half)[None, :]) % outer) / outer
    at = 2.0 * np.pi * ((k1 * np.arange(LANES)[None, :]) % total) / total
    m2 = np.arange(LANES)
    a2 = 2.0 * np.pi * ((m2[:, None] * m2[None, :]) % LANES) / LANES
    c1, s1 = np.cos(a1), np.sin(a1)
    c2, s2 = np.cos(a2), np.sin(a2)
    weight = np.where((k1 == 0) | (k1 == outer // 2), 1.0, 2.0) * (k1 < keep)
    f32 = lambda v: jnp.asarray(v, jnp.float32)
    return dict(
        first=f32(np.concatenate([c1, -s1], axis=0)),
        tc=f32(np.cos(at)[:, None, :]),
        ts=f32(np.sin(at)[:, None, :]),
        fwd2=f32(np.block([[c2, -s2], [s2, c2]])),
        inv2=f32(np.block([[c2, s2], [-s2, c2]])),
        last=f32(np.concatenate([(c1 * weight).T, -(s1 * weight).T], axis=1) / total),
    )


def forward(signal, tb):
    outer = tb["tc"].shape[0]
    both = contract("kn,ncm->kcm", tb["first"], signal)
    br, bi = both[:outer], both[outer:]
    tr, ti = tb["tc"], -tb["ts"]
    twisted = jnp.concatenate([br * tr - bi * ti, br * ti + bi * tr], axis=2)
    return contract("kcm,mj->kcj", twisted, tb["fwd2"])


def inverse(spectrum, tb):
    z = contract("kcj,jm->kcm", spectrum, tb["inv2"])
    zr, zi = z[:, :, :LANES], z[:, :, LANES:]
    tc, ts = tb["tc"], tb["ts"]
    stacked = jnp.concatenate([zr * tc - zi * ts, zr * ts + zi * tc], axis=0)
    return contract("nk,kcm->ncm", tb["last"], stacked)


def long_conv(mixed_in, long_filter):
    half = mixed_in.shape[0]
    tb = tables(half * LANES)
    width = mixed_in.shape[1]
    both = forward(jnp.concatenate([mixed_in, long_filter], axis=1), tb)
    xs, hs = both[:, :width], both[:, width:]
    xr, xi = xs[:, :, :LANES], xs[:, :, LANES:]
    hr, hi = hs[:, :, :LANES], hs[:, :, LANES:]
    product = jnp.concatenate([xr * hr - xi * hi, xr * hi + xi * hr], axis=2)
    return inverse(product, tb)


def shift_seq(signal, distance):
    rows, width, lanes = signal.shape
    prev = jnp.concatenate([jnp.zeros((1, width, lanes), signal.dtype), signal[:-1]], axis=0)
    return jnp.concatenate(
        [prev[:, :, lanes - distance :], signal[:, :, : lanes - distance]], axis=2
    )


def short_conv(signal, taps):
    summed = taps[0][None, :, None] * signal
    for offset in range(1, taps.shape[0]):
        summed = summed + taps[offset][None, :, None] * shift_seq(signal, offset)
    return summed


def to_ncm(block):
    rows, width = block.shape
    return block.reshape(rows // LANES, LANES, width).transpose(0, 2, 1)


def on_device(out_gate, in_gate, values, short_filter, long_filter, skip_gain, out_weight):
    seq_count = lax.axis_size("seq")
    seq_index = lax.axis_index("seq")
    rows = out_gate.shape[0]
    width = out_gate.shape[1] // seq_count
    half = rows // LANES

    planes = [out_gate, in_gate, values, long_filter.astype(jnp.bfloat16)]
    stacked = jnp.stack([to_ncm(plane) for plane in planes])
    spread = exchange(stacked, seq_count, 0)
    start = seq_index * width
    sets, tap_count = short_filter.shape[:2]
    params = jnp.concatenate([short_filter.reshape(sets * tap_count, -1), skip_gain[None]])
    params = lax.dynamic_slice_in_dim(params, start, width, axis=1)
    taps = params[: sets * tap_count].reshape(sets, tap_count, width)
    gain = params[sets * tap_count]
    spread = spread.astype(jnp.float32)
    gate_late = short_conv(spread[0], taps[0])
    mixed_in = short_conv(spread[1], taps[1]) * short_conv(spread[2], taps[2])
    long_out = long_conv(mixed_in, spread[3])
    filtered = long_out + gain[None, :, None] * mixed_in
    mixed = (gate_late * filtered).astype(jnp.bfloat16)
    chans = lax.axis_size("ch")
    gathered = return_and_gather(mixed.reshape(seq_count, half, width, LANES), seq_count, chans, 1)
    gathered = gathered.reshape(half, chans * seq_count * width, LANES)
    summed = jnp.einsum(
        "co,ncm->nom", out_weight, gathered, preferred_element_type=jnp.float32
    )
    return summed.astype(jnp.bfloat16).transpose(0, 2, 1).reshape(rows, -1)


def solution(mesh):
    return jax.shard_map(
        on_device,
        mesh=mesh,
        in_specs=(
            P("seq", "ch"),
            P("seq", "ch"),
            P("seq", "ch"),
            P(None, None, "ch"),
            P("seq", "ch"),
            P("ch"),
            P(None, "ch"),
        ),
        out_specs=P("seq", "ch"),
        check_vma=False,
    )
```

```python
import functools

import jax
import jax.numpy as jnp
import numpy as np
from jax import lax
from jax.experimental import pallas as pl
from jax.experimental.pallas import tpu as pltpu
from jax.sharding import PartitionSpec as P

high = lax.Precision.HIGH
LANES = 128
MESH = pl.DeviceIdType.MESH


def peer_offsets(group, inner=8):
    if group % inner:
        inner = group
    outer = group // inner
    dist = lambda d, n: min(d, n - d)
    seen, order = set(), []
    cands = [(dx, dz) for dx in range(outer) for dz in range(inner) if dx or dz]
    cands.sort(key=lambda o: (-(dist(o[0], outer) + dist(o[1], inner)), o))
    for dx, dz in cands:
        for off in ((dx, dz), ((outer - dx) % outer, (inner - dz) % inner)):
            if off not in seen:
                seen.add(off)
                order.append(off)
    return inner, order


def shifted_peer(me, off, inner, group, sign):
    outer = group // inner
    x, z = me // inner, lax.rem(me, inner)
    dx, dz = off
    return lax.rem(x + sign * dx + outer, outer) * inner + lax.rem(z + sign * dz + inner, inner)


def exchange_kernel(group, source, target, send_sem, recv_sem, local_sem):
    me = lax.axis_index("seq")
    ch = lax.axis_index("ch")
    half = source.shape[1]
    width = target.shape[2]
    barrier = pltpu.get_barrier_semaphore()
    for step in range(1, group):
        peer = lax.rem(me + step, group)
        pl.semaphore_signal(barrier, inc=1, device_id=(peer, ch), device_id_type=MESH)
    pl.semaphore_wait(barrier, group - 1)

    def piece(ref_src, peer, origin):
        return (
            ref_src.at[:, :, pl.ds(peer * width, width)],
            target.at[:, pl.ds(origin * half, half)],
        )

    src, dst = piece(source, me, me)
    local = pltpu.make_async_copy(src, dst, local_sem.at[0])
    local.start()
    inner, offsets = peer_offsets(group)
    sent = []
    for step, off in enumerate(offsets, start=1):
        peer = shifted_peer(me, off, inner, group, 1)
        src, dst = piece(source, peer, me)
        cp = pltpu.make_async_remote_copy(
            src_ref=src,
            dst_ref=dst,
            send_sem=send_sem.at[step],
            recv_sem=recv_sem.at[step],
            device_id=(peer, ch),
            device_id_type=MESH,
        )
        cp.start()
        sent.append(cp)
    local.wait()
    for cp in sent:
        cp.wait_send()
    for step, off in enumerate(offsets, start=1):
        origin = shifted_peer(me, off, inner, group, -1)
        src, dst = piece(source, me, origin)
        pltpu.make_async_remote_copy(
            src_ref=src,
            dst_ref=dst,
            send_sem=send_sem.at[step],
            recv_sem=recv_sem.at[step],
            device_id=(origin, ch),
            device_id_type=MESH,
        ).wait_recv()


def exchange(stacked, group, tag):
    planes, half, full, lanes = stacked.shape
    return pl.pallas_call(
        functools.partial(exchange_kernel, group),
        out_shape=jax.ShapeDtypeStruct((planes, group * half, full // group, lanes), stacked.dtype),
        in_specs=[pl.BlockSpec(memory_space=pl.ANY)],
        out_specs=pl.BlockSpec(memory_space=pl.ANY),
        scratch_shapes=[
            pltpu.SemaphoreType.DMA((group,)),
            pltpu.SemaphoreType.DMA((group,)),
            pltpu.SemaphoreType.DMA((1,)),
        ],
        compiler_params=pltpu.CompilerParams(collective_id=tag, has_side_effects=True),
    )(stacked)


def return_kernel(group, chans, source, target, send_sem, recv_sem, pass_sem, got_sem, fwd_sem, local_sem):
    me = lax.axis_index("seq")
    ch = lax.axis_index("ch")
    half = source.shape[1]
    sibling = ch + 1 - 2 * lax.rem(ch, 2)
    across = [lax.rem(ch + 2 * hop, chans) for hop in range(1, chans // 2)]
    barrier = pltpu.get_barrier_semaphore()
    for step in range(1, group):
        peer = lax.rem(me + step, group)
        pl.semaphore_signal(barrier, inc=1, device_id=(peer, ch), device_id_type=MESH)
    for peer_ch in across + [sibling]:
        pl.semaphore_signal(barrier, inc=1, device_id=(me, peer_ch), device_id_type=MESH)
    pl.semaphore_wait(barrier, group - 1 + len(across) + 1)

    def incoming(part, slot, peer_ch):
        return pltpu.make_async_remote_copy(
            src_ref=target.at[part, slot],
            dst_ref=target.at[part, slot],
            send_sem=pass_sem.at[part, 0],
            recv_sem=got_sem.at[part, slot],
            device_id=(me, peer_ch),
            device_id_type=MESH,
        )

    inner, offsets = peer_offsets(group)
    sent = []
    locals_ = []
    for part in range(half):
        cp = pltpu.make_async_copy(
            source.at[me, part], target.at[part, ch, me], local_sem.at[part]
        )
        cp.start()
        locals_.append(cp)
        for step, off in enumerate(offsets, start=1):
            peer = shifted_peer(me, off, inner, group, 1)
            cp = pltpu.make_async_remote_copy(
                src_ref=source.at[peer, part],
                dst_ref=target.at[part, ch, me],
                send_sem=send_sem.at[part, step],
                recv_sem=recv_sem.at[part, step],
                device_id=(peer, ch),
                device_id_type=MESH,
            )
            cp.start()
            sent.append(cp)
    passed = []
    for part in range(half):
        locals_[part].wait()
        for step, off in enumerate(offsets, start=1):
            origin = shifted_peer(me, off, inner, group, -1)
            pltpu.make_async_remote_copy(
                src_ref=source.at[origin, part],
                dst_ref=target.at[part, ch, origin],
                send_sem=send_sem.at[part, step],
                recv_sem=recv_sem.at[part, step],
                device_id=(origin, ch),
                device_id_type=MESH,
            ).wait_recv()
        for slot, peer_ch in enumerate(across + [sibling]):
            cp = pltpu.make_async_remote_copy(
                src_ref=target.at[part, ch],
                dst_ref=target.at[part, ch],
                send_sem=pass_sem.at[part, slot],
                recv_sem=got_sem.at[part, ch],
                device_id=(me, peer_ch),
                device_id_type=MESH,
            )
            cp.start()
            passed.append(cp)
    forwarded = []
    for part in range(half):
        for hop in range(1, chans // 2):
            origin = lax.rem(ch + chans - 2 * hop, chans)
            incoming(part, origin, origin).wait_recv()
            cp = pltpu.make_async_remote_copy(
                src_ref=target.at[part, origin],
                dst_ref=target.at[part, origin],
                send_sem=fwd_sem.at[part, hop],
                recv_sem=got_sem.at[part, origin],
                device_id=(me, sibling),
                device_id_type=MESH,
            )
            cp.start()
            forwarded.append(cp)
    for cp in sent + passed + forwarded:
        cp.wait_send()
    for part in range(half):
        for hop in range(1, chans // 2):
            origin = lax.rem(sibling + chans - 2 * hop, chans)
            incoming(part, origin, origin).wait_recv()
        incoming(part, sibling, sibling).wait_recv()


def return_and_gather(block, group, chans, tag):
    half = block.shape[1]
    return pl.pallas_call(
        functools.partial(return_kernel, group, chans),
        out_shape=jax.ShapeDtypeStruct(
            (half, chans, block.shape[0]) + block.shape[2:], block.dtype
        ),
        in_specs=[pl.BlockSpec(memory_space=pl.ANY)],
        out_specs=pl.BlockSpec(memory_space=pl.ANY),
        scratch_shapes=[
            pltpu.SemaphoreType.DMA((half, group)),
            pltpu.SemaphoreType.DMA((half, group)),
            pltpu.SemaphoreType.DMA((half, chans // 2)),
            pltpu.SemaphoreType.DMA((half, chans)),
            pltpu.SemaphoreType.DMA((half, chans // 2)),
            pltpu.SemaphoreType.DMA((half,)),
        ],
        compiler_params=pltpu.CompilerParams(collective_id=tag, has_side_effects=True),
    )(block)


def contract(pattern, first_op, second_op):
    return jnp.einsum(
        pattern, first_op, second_op, precision=high, preferred_element_type=jnp.float32
    )


def tables(seq_len):
    total = 2 * seq_len
    outer = total // LANES
    half = seq_len // LANES
    keep = outer // 2 + 1
    rows = -(-keep // 8) * 8
    k1 = np.arange(rows)[:, None]
    a1 = 2.0 * np.pi * ((k1 * np.arange(half)[None, :]) % outer) / outer
    at = 2.0 * np.pi * ((k1 * np.arange(LANES)[None, :]) % total) / total
    m2 = np.arange(LANES)
    a2 = 2.0 * np.pi * ((m2[:, None] * m2[None, :]) % LANES) / LANES
    c1, s1 = np.cos(a1), np.sin(a1)
    c2, s2 = np.cos(a2), np.sin(a2)
    weight = np.where((k1 == 0) | (k1 == outer // 2), 1.0, 2.0) * (k1 < keep)
    f32 = lambda v: jnp.asarray(v, jnp.float32)
    return dict(
        first=f32(np.concatenate([c1, -s1], axis=0)),
        tc=f32(np.cos(at)[:, None, :]),
        ts=f32(np.sin(at)[:, None, :]),
        fwd2=f32(np.block([[c2, -s2], [s2, c2]])),
        last=f32(np.concatenate([(c1 * weight).T, -(s1 * weight).T], axis=1) / total),
    )


def forward(signal, tb):
    outer = tb["tc"].shape[0]
    both = contract("kn,ncm->kcm", tb["first"], signal)
    br, bi = both[:outer], both[outer:]
    tr, ti = tb["tc"], -tb["ts"]
    twisted = jnp.concatenate([br * tr - bi * ti, br * ti + bi * tr], axis=2)
    return contract("kcm,mj->kcj", twisted, tb["fwd2"])


def inverse(spectrum, tb):
    z = contract("kcj,mj->kcm", spectrum, tb["fwd2"])
    zr, zi = z[:, :, :LANES], z[:, :, LANES:]
    tc, ts = tb["tc"], tb["ts"]
    stacked = jnp.concatenate([zr * tc - zi * ts, zr * ts + zi * tc], axis=0)
    return contract("nk,kcm->ncm", tb["last"], stacked)


def long_conv(mixed_in, long_filter):
    half = mixed_in.shape[0]
    tb = tables(half * LANES)
    width = mixed_in.shape[1]
    both = forward(jnp.concatenate([mixed_in, long_filter], axis=1), tb)
    xs, hs = both[:, :width], both[:, width:]
    xr, xi = xs[:, :, :LANES], xs[:, :, LANES:]
    hr, hi = hs[:, :, :LANES], hs[:, :, LANES:]
    product = jnp.concatenate([xr * hr - xi * hi, xr * hi + xi * hr], axis=2)
    return inverse(product, tb)


def shift_seq(signal, distance):
    rows, width, lanes = signal.shape
    prev = jnp.concatenate([jnp.zeros((1, width, lanes), signal.dtype), signal[:-1]], axis=0)
    return jnp.concatenate(
        [prev[:, :, lanes - distance :], signal[:, :, : lanes - distance]], axis=2
    )


def short_conv(signal, taps):
    summed = taps[0][None, :, None] * signal
    for offset in range(1, taps.shape[0]):
        summed = summed + taps[offset][None, :, None] * shift_seq(signal, offset)
    return summed


def to_ncm(block):
    rows, width = block.shape
    return block.reshape(rows // LANES, LANES, width).transpose(0, 2, 1)


def on_device(out_gate, in_gate, values, short_filter, long_filter, skip_gain, out_weight):
    seq_count = lax.axis_size("seq")
    seq_index = lax.axis_index("seq")
    rows = out_gate.shape[0]
    width = out_gate.shape[1] // seq_count
    half = rows // LANES

    planes = [out_gate, in_gate, values, long_filter.astype(jnp.bfloat16)]
    stacked = jnp.stack([to_ncm(plane) for plane in planes])
    spread = exchange(stacked, seq_count, 0)
    start = seq_index * width
    sets, tap_count = short_filter.shape[:2]
    params = jnp.concatenate([short_filter.reshape(sets * tap_count, -1), skip_gain[None]])
    params = lax.dynamic_slice_in_dim(params, start, width, axis=1)
    taps = params[: sets * tap_count].reshape(sets, tap_count, width)
    gain = params[sets * tap_count]
    spread = spread.astype(jnp.float32)
    gate_late = short_conv(spread[0], taps[0])
    mixed_in = short_conv(spread[1], taps[1]) * short_conv(spread[2], taps[2])
    long_out = long_conv(mixed_in, spread[3])
    filtered = long_out + gain[None, :, None] * mixed_in
    mixed = (gate_late * filtered).astype(jnp.bfloat16)
    chans = lax.axis_size("ch")
    gathered = return_and_gather(mixed.reshape(seq_count, half, width, LANES), seq_count, chans, 1)
    gathered = gathered.reshape(half, chans * seq_count * width, LANES)
    summed = jnp.einsum(
        "co,ncm->nom", out_weight, gathered, preferred_element_type=jnp.float32
    )
    return summed.astype(jnp.bfloat16).transpose(0, 2, 1).reshape(rows, -1)


def solution(mesh):
    return jax.shard_map(
        on_device,
        mesh=mesh,
        in_specs=(
            P("seq", "ch"),
            P("seq", "ch"),
            P("seq", "ch"),
            P(None, None, "ch"),
            P("seq", "ch"),
            P("ch"),
            P(None, "ch"),
        ),
        out_specs=P("seq", "ch"),
        check_vma=False,
    )
```
